128 devices in a mesh: pb: 4 (over z), pa: 32 (over y, x, core).
Axes of the slice: x: 4, y: 4, z: 4, core: 2. Of those that a mesh axis runs over, the one named last changes fastest.
Arguments:
- queries: bfloat16 [8192, 1024], P('pb'), may hold values from -16 to 16
- passages: bfloat16 [65536, 1024], P('pa'), may hold values from -5 to 5
- teacher: float32 [8192, 16384], P('pb', 'pa'), may hold values from -20 to 300
- block_ids: int32 [64, 128], P('pb', 'pa'), may hold values from 0 to 511, as said below
Outputs:
- loss: float32 [8192], P(('pb', 'pa'))
- grad_queries: float32 [8192, 1024], P(('pb', 'pa'))
- grad_passages: float32 [65536, 1024], P(('pa', 'pb'))
The draws below stay inside these ranges and needn't reach their ends.
Inputs may be any that keep to these rules, and one draw needn't show every extreme that they name: Block g belongs to passage shard g // 16. Among the 64 entries of one device's tile of block_ids (rows of one index of pb, columns of one index of pa), at most 4 name blocks of one shard, and in every tile some shard is named exactly 4 times. The 4 entries of one row of a tile name blocks of different shards.
All inputs are finite; a program needn't handle non-finite values.
Results may differ from the reference program's by a relative error of at most 0.0024.
Values sent between devices are 32-bit elements; how exact they have to be, the bound alone decides.
No kernel may reach another device: no remote copies, remote signals or barrier semaphores. Data moves between devices by JAX's collectives and lax.ppermute only.
A program may use at most 192 MiB of HBM per device.

```python
import math
import jax
import jax.numpy as jnp
from jax import lax

D = 1024
BLOCK = 128
QBLOCKS_DEV = 16
PBLOCKS_DEV = 16
SLOTS_DEV = 4
QBLOCKS = 64
PBLOCKS = 512
QUERIES = 8192
PASSAGES = 65536
SLOTS = 128


def draw_queries(key, part):
    values = jnp.clip(jax.random.normal(jax.random.fold_in(key, 1), (QUERIES, D), jnp.float32), -5.0, 5.0)
    return values.astype(jnp.bfloat16)


def draw_passages(key, part):
    values = jnp.clip(jax.random.normal(jax.random.fold_in(key, 11), (PASSAGES, D), jnp.float32), -5.0, 5.0)
    return values.astype(jnp.bfloat16)


def draw_teacher(key, part):
    heavy = (jax.random.uniform(jax.random.fold_in(key, 24), (QUERIES, SLOTS * BLOCK), jnp.float32) < 0.3).astype(jnp.float32)
    rough = jnp.clip(0.5 * jax.random.normal(jax.random.fold_in(key, 21), (QUERIES, SLOTS * BLOCK), jnp.float32), -2.0, 2.0)
    values = 3.0 * heavy + rough
    return values


def draw_block_ids(key, part):
    pa_count = SLOTS // SLOTS_DEV
    pb_count = QBLOCKS // QBLOCKS_DEV
    entries = QBLOCKS_DEV * SLOTS_DEV
    capacity = 2 * ((entries + pa_count - 1) // pa_count)
    active = entries // capacity

    def one_tile(tile_key):
        owners = jax.random.permutation(jax.random.fold_in(tile_key, 1), pa_count)
        picked = owners[jnp.arange(entries) % active]
        local_block = jax.random.randint(jax.random.fold_in(tile_key, 2), (entries,), 0, PBLOCKS_DEV)
        return (picked * PBLOCKS_DEV + local_block).reshape(QBLOCKS_DEV, SLOTS_DEV)
    tile_keys = jax.random.split(jax.random.fold_in(key, 7), pb_count * pa_count)
    all_tiles = jax.vmap(one_tile)(tile_keys).reshape(pb_count, pa_count, QBLOCKS_DEV, SLOTS_DEV)
    return all_tiles.transpose(0, 2, 1, 3).reshape(QBLOCKS, SLOTS).astype(jnp.int32)


def setup_inputs(seed: int = 0) -> dict:
    key_list = jax.random.split(jax.random.key(seed), 5)
    queries = draw_queries(jax.random.fold_in(key_list[4], 71), 0)
    passages = draw_passages(jax.random.fold_in(key_list[4], 71), 0)
    teacher = draw_teacher(jax.random.fold_in(key_list[4], 71), 0)
    block_ids = draw_block_ids(jax.random.fold_in(key_list[4], 71), 0)
    return dict(queries=queries, passages=passages, teacher=teacher, block_ids=block_ids)


loss_scale = 1024.0

def reference(queries, passages, teacher, block_ids):
    score_scale = 2.0 / math.sqrt(D)
    teacher_max = lax.optimization_barrier(jnp.max(teacher, axis=1))
    lse_teacher = teacher_max + jnp.log(lax.optimization_barrier(jnp.sum(jnp.exp(teacher - teacher_max[:, None]), axis=1)))
    teacher_probs = jnp.exp(teacher - lse_teacher[:, None])

    def one_block(grad_pass, inputs):
        block_queries, block_teacher, block_probs, block_lse, block_row = inputs
        scores = lax.dot_general(block_queries, passages, (((1,), (1,)), ((), ())), preferred_element_type=jnp.float32) * score_scale
        row_max = lax.optimization_barrier(jnp.max(scores, axis=1))
        lse_student = row_max + jnp.log(lax.optimization_barrier(jnp.sum(jnp.exp(scores - row_max[:, None]), axis=1)))
        hard_weights = jnp.zeros((BLOCK, PBLOCKS, BLOCK), jnp.float32)
        hard_weights = hard_weights.at[:, block_row.astype(jnp.int32), :].add(block_probs.reshape(BLOCK, SLOTS, BLOCK))
        hard_weights = hard_weights.reshape(BLOCK, PASSAGES)
        block_loss = lse_student + lax.optimization_barrier(jnp.sum(block_probs * (block_teacher - block_lse[:, None]), axis=1)) - lax.optimization_barrier(jnp.sum(hard_weights * scores, axis=1))
        dscore = ((jnp.exp(scores - lse_student[:, None]) - hard_weights) * (loss_scale * score_scale)).astype(jnp.bfloat16)
        grad_query = jnp.dot(dscore, passages, preferred_element_type=jnp.float32)
        grad_pass = grad_pass + lax.dot_general(dscore, block_queries, (((0,), (0,)), ((), ())), preferred_element_type=jnp.float32)
        return (grad_pass, (block_loss, grad_query))
    scan_inputs = (queries.reshape(QBLOCKS, BLOCK, D), teacher.reshape(QBLOCKS, BLOCK, SLOTS * BLOCK), teacher_probs.reshape(QBLOCKS, BLOCK, SLOTS * BLOCK), lse_teacher.reshape(QBLOCKS, BLOCK), block_ids)
    grad_pass, (all_loss, grad_query) = lax.scan(one_block, jnp.zeros((PASSAGES, D), jnp.float32), scan_inputs)
    return (all_loss.reshape(QUERIES), grad_query.reshape(QUERIES, D), grad_pass)
```

```python
import functools

import jax
import jax.numpy as jnp
from jax import lax
from jax.experimental import pallas as pl
from jax.experimental.pallas import tpu as pltpu
from jax.sharding import Mesh
from jax.sharding import PartitionSpec as P

BLOCK = 128
D = 1024
ROWS = 2048
PBLOCKS_DEV = 16
SLOTS_DEV = 4
CAP = 4
SHARDS = 32
PLANE = ("y", "x", "c")
SCORE_SCALE = 0.0625
GRAD_SCALE = 64.0


def as_row(column):
    n = column.shape[0]
    return jnp.broadcast_to(column, (n, BLOCK)).T[0:1, :]


def as_lanes(row):
    n = row.shape[1]
    return jnp.broadcast_to(row, (BLOCK, n)).T


def pack_kernel(ids_ref, teacher_ref, first_ref, second_ref, slot_ref, count_ref):
    shard = pl.program_id(0)

    @pl.when(shard == 0)
    def _():
        def clear_count(i, carry):
            count_ref[i] = 0
            return carry

        def clear_slot(i, carry):
            slot_ref[i] = 0
            return carry

        def place(i, carry):
            owner = ids_ref[i] // PBLOCKS_DEV
            rank = count_ref[owner]
            count_ref[owner] = rank + 1
            slot_ref[owner * CAP + jnp.minimum(rank, CAP - 1)] = i
            return carry

        lax.fori_loop(0, SHARDS, clear_count, 0)
        lax.fori_loop(0, SHARDS * CAP, clear_slot, 0)
        lax.fori_loop(0, (ROWS // BLOCK) * SLOTS_DEV, place, 0)

    low = lax.broadcasted_iota(jnp.int32, (BLOCK, BLOCK), 1) < BLOCK // 2
    for pair in range(CAP // 2):
        tiles = []
        for k in range(2):
            entry = slot_ref[shard * CAP + 2 * pair + k]
            row = pl.multiple_of((entry // SLOTS_DEV) * BLOCK, BLOCK)
            col = pl.multiple_of((entry % SLOTS_DEV) * BLOCK, BLOCK)
            tiles.append(teacher_ref[pl.ds(row, BLOCK), pl.ds(col, BLOCK)])
        rolled = [pltpu.roll(t, BLOCK // 2, 1) for t in tiles]
        rows = slice(pair * BLOCK, (pair + 1) * BLOCK)
        first_ref[0, rows, :] = jnp.where(low, tiles[0], rolled[1])
        second_ref[0, rows, :] = jnp.where(low, rolled[0], tiles[1])


def pack(ids, teacher):
    out = jax.ShapeDtypeStruct((SHARDS, 2 * BLOCK, BLOCK), jnp.float32)
    spec = pl.BlockSpec((1, 2 * BLOCK, BLOCK), lambda s, ids: (s, 0, 0))
    return pl.pallas_call(
        pack_kernel,
        out_shape=(out, out),
        grid_spec=pltpu.PrefetchScalarGridSpec(
            num_scalar_prefetch=1,
            grid=(SHARDS,),
            in_specs=[pl.BlockSpec((ROWS, SLOTS_DEV * BLOCK), lambda s, ids: (0, 0))],
            out_specs=(spec, spec),
            scratch_shapes=[
                pltpu.SMEM((SHARDS * CAP,), jnp.int32),
                pltpu.SMEM((SHARDS,), jnp.int32),
            ],
        ),
        name="pack",
    )(ids, teacher)


def score_kernel(q_ref, p0_ref, p1_ref, t_ref, s0_ref, s1_ref, lse_ref):
    q = q_ref[...]
    nt = (((1,), (1,)), ((), ()))
    s0 = lax.dot_general(q, p0_ref[...], nt, preferred_element_type=jnp.float32) * SCORE_SCALE
    s1 = lax.dot_general(q, p1_ref[...], nt, preferred_element_type=jnp.float32) * SCORE_SCALE
    s0_ref[...] = s0
    s1_ref[...] = s1
    top = jnp.maximum(jnp.max(s0, axis=1, keepdims=True), jnp.max(s1, axis=1, keepdims=True))
    total = jnp.sum(jnp.exp(s0 - top), axis=1, keepdims=True) + jnp.sum(
        jnp.exp(s1 - top), axis=1, keepdims=True
    )
    lse_ref[0, 0:1, :] = as_row(top + jnp.log(total))
    t = t_ref[...]
    ttop = jnp.max(t, axis=1, keepdims=True)
    ttotal = jnp.sum(jnp.exp(t - ttop), axis=1, keepdims=True)
    lse_ref[0, 1:2, :] = as_row(ttop + jnp.log(ttotal))


def score(queries, p0, p1, teacher):
    rb = 256
    half = jax.ShapeDtypeStruct((ROWS, D), jnp.float32)
    whole = pl.BlockSpec((D, D), lambda i: (0, 0))
    return pl.pallas_call(
        score_kernel,
        out_shape=(half, half, jax.ShapeDtypeStruct((ROWS // rb, 2, rb), jnp.float32)),
        grid=(ROWS // rb,),
        in_specs=[
            pl.BlockSpec((rb, D), lambda i: (i, 0)),
            whole,
            whole,
            pl.BlockSpec((rb, SLOTS_DEV * BLOCK), lambda i: (i, 0)),
        ],
        out_specs=(
            pl.BlockSpec((rb, D), lambda i: (i, 0)),
            pl.BlockSpec((rb, D), lambda i: (i, 0)),
            pl.BlockSpec((1, 2, rb), lambda i: (i, 0, 0)),
        ),
        name="score",
    )(queries, p0, p1, teacher)


def dscore_kernel(
    pos_ref, start_ref, row_ref, shift_ref, block_ref,
    s_ref, lse_ref, recv_ref, q_ref,
    ds_ref, loss_ref, c0_ref, c1a_ref, c1b_ref, c2a_ref, c2b_ref, c3a_ref, c3b_ref,
    w_ref, lt_ref, acc_ref,
):
    step = pl.program_id(0)
    rb = 256
    half = BLOCK // 2

    @pl.when(step < ROWS // rb)
    def _():
        ls = as_lanes(lse_ref[0, 0:1, :])
        lt_ref[...] = as_lanes(lse_ref[0, 1:2, :])
        for j in range(D // BLOCK):
            cols = slice(j * BLOCK, (j + 1) * BLOCK)
            w_ref[:, cols] = jnp.exp(s_ref[:, cols] - ls)
        acc_ref[...] = jnp.zeros_like(acc_ref)
        high = lax.broadcasted_iota(jnp.int32, (BLOCK, BLOCK), 1) // half
        for sub in range(rb // BLOCK):
            rows = slice(sub * BLOCK, (sub + 1) * BLOCK)

            def body(n, carry):
                x = recv_ref[pl.ds(pl.multiple_of(row_ref[n], BLOCK), BLOCK), :]
                x = pltpu.roll(x, shift_ref[n], 1)
                block = block_ref[n]
                cols = pl.ds(pl.multiple_of((block // 2) * BLOCK, BLOCK), BLOCK)
                keep = high == block % 2
                centred = x - lt_ref[rows, :]
                prob = jnp.where(keep, jnp.exp(centred), 0.0)
                w_ref[rows, cols] = w_ref[rows, cols] - prob
                term = jnp.where(keep, prob * (centred - s_ref[rows, cols]), 0.0)
                acc_ref[rows, :] = acc_ref[rows, :] + term
                return carry

            r = step * (rb // BLOCK) + sub
            lax.fori_loop(start_ref[r], start_ref[r + 1], body, 0)
        ds_ref[pl.ds(pl.multiple_of(step * rb, rb), rb), :] = (w_ref[...] * GRAD_SCALE).astype(
            jnp.bfloat16
        )
        loss_ref[0] = as_row(jnp.sum(acc_ref[...], axis=1, keepdims=True))

    @pl.when(step == ROWS // rb)
    def _():
        outs = {0: (c0_ref,), 1: (c1a_ref, c1b_ref), 2: (c2a_ref, c2b_ref), 3: (c3a_ref, c3b_ref)}
        for d in (2, 1, 3, 0):
            off = pl.multiple_of(((pos_ref[0] + d) % 4) * (D // 4), D // 4)
            part = lax.dot_general(
                ds_ref[:, pl.ds(off, D // 4)],
                q_ref[...],
                (((0,), (0,)), ((), ())),
                preferred_element_type=jnp.float32,
            )
            if d == 0:
                c0_ref[...] = part
            else:
                outs[d][0][...] = part[: D // 8]
                outs[d][1][...] = part[D // 8 :]


def dscore(scalars, scores, lse, recv, queries):
    rb = 256
    last = ROWS // rb - 1
    full = lambda *shape: pl.BlockSpec(shape, lambda i, *_: (0,) * len(shape))
    piece = jax.ShapeDtypeStruct((D // 8, D), jnp.float32)
    return pl.pallas_call(
        dscore_kernel,
        out_shape=(
            jax.ShapeDtypeStruct((ROWS, D), jnp.bfloat16),
            jax.ShapeDtypeStruct((ROWS // rb, 1, rb), jnp.float32),
            jax.ShapeDtypeStruct((D // 4, D), jnp.float32),
        )
        + (piece,) * 6,
        grid_spec=pltpu.PrefetchScalarGridSpec(
            num_scalar_prefetch=len(scalars),
            grid=(ROWS // rb + 1,),
            in_specs=[
                pl.BlockSpec((rb, D), lambda i, *_: (jnp.minimum(i, last), 0)),
                pl.BlockSpec((1, 2, rb), lambda i, *_: (jnp.minimum(i, last), 0, 0)),
                full(SHARDS * 2 * BLOCK, BLOCK),
                full(ROWS, D),
            ],
            out_specs=(
                full(ROWS, D),
                pl.BlockSpec((1, 1, rb), lambda i, *_: (jnp.minimum(i, last), 0, 0)),
                full(D // 4, D),
            )
            + (full(D // 8, D),) * 6,
            scratch_shapes=[
                pltpu.VMEM((rb, D), jnp.float32),
                pltpu.VMEM((rb, BLOCK), jnp.float32),
                pltpu.VMEM((rb, BLOCK), jnp.float32),
            ],
        ),
        name="dscore",
    )(*scalars, scores, lse, recv.reshape(SHARDS * 2 * BLOCK, BLOCK), queries)


def first_query_kernel(ds_ref, p_ref, out_ref):
    out_ref[...] = jnp.dot(ds_ref[...], p_ref[...], preferred_element_type=jnp.float32)


def first_query(ds, passages):
    rb = 256
    return pl.pallas_call(
        first_query_kernel,
        out_shape=jax.ShapeDtypeStruct((ROWS, D), jnp.float32),
        grid=(ROWS // rb,),
        in_specs=[pl.BlockSpec((rb, D), lambda i: (i, 0)), pl.BlockSpec((D, D), lambda i: (0, 0))],
        out_specs=pl.BlockSpec((rb, D), lambda i: (i, 0)),
        name="first_query",
    )(ds, passages)


def last_query_kernel(pos_ref, ds_ref, p_ref, add_ref, own_ref, other_ref):
    step = pl.program_id(0)
    part = add_ref[...] + jnp.dot(ds_ref[...], p_ref[...], preferred_element_type=jnp.float32)
    dy = (step // 2 + 4 - pos_ref[1]) % 4
    for j in range(4):
        dx = (2 * step + j // 2 + 4 - pos_ref[2]) % 4
        a = pl.ds(pl.multiple_of(dx * 128 + dy * 32, 32), 32)
        b = pl.ds(pl.multiple_of(512 + dy * 128 + dx * 32, 32), 32)

        @pl.when(pos_ref[3] == j % 2)
        def _():
            own_ref[a, :] = part[64 * j : 64 * j + 32]
            own_ref[b, :] = part[64 * j + 32 : 64 * j + 64]

        @pl.when(pos_ref[3] != j % 2)
        def _():
            other_ref[a, :] = part[64 * j : 64 * j + 32]
            other_ref[b, :] = part[64 * j + 32 : 64 * j + 64]


def last_query(pos, ds, passages, add):
    rb = 256
    out = jax.ShapeDtypeStruct((ROWS // 2, D), jnp.float32)
    return pl.pallas_call(
        last_query_kernel,
        out_shape=(out, out),
        grid_spec=pltpu.PrefetchScalarGridSpec(
            num_scalar_prefetch=1,
            grid=(ROWS // rb,),
            in_specs=[
                pl.BlockSpec((rb, D), lambda i, *_: (i, 0)),
                pl.BlockSpec((D, D), lambda i, *_: (0, 0)),
                pl.BlockSpec((rb, D), lambda i, *_: (i, 0)),
            ],
            out_specs=(pl.BlockSpec((ROWS // 2, D), lambda i, *_: (0, 0)),) * 2,
        ),
        name="last_query",
    )(pos, ds, passages, add)


def ring(d, n=4):
    return [(i, (i + d) % n) for i in range(n)]


def merge_lse(lse):
    for axis, n in (("c", 2), ("x", 4), ("y", 4)):
        parts = [lse] + [lax.ppermute(lse, axis, ring(d, n)) for d in range(1, n)]
        top = functools.reduce(jnp.maximum, parts)
        lse = top + jnp.log(sum(jnp.exp(p - top) for p in parts))
    return lse


def scatter_halves(c0, c1, c2, c3, axis):
    h = c0.shape[0] // 2
    near_p = lax.ppermute(c2[0], axis, ring(1))
    near_m = lax.ppermute(c2[1], axis, ring(-1))
    free_p = lax.ppermute(c1[1], axis, ring(1))
    free_m = lax.ppermute(c3[0], axis, ring(-1))
    sum_p = lax.ppermute(c1[0] + near_p, axis, ring(1))
    sum_m = lax.ppermute(c3[1] + near_m, axis, ring(-1))
    return jnp.concatenate([c0[:h] + sum_p + free_m, c0[h:] + free_p + sum_m], axis=0)


def scatter_whole(c0, c1, c2, c3, axis):
    h = c0.shape[0] // 2
    near_p = lax.ppermute(c2[:h], axis, ring(1))
    near_m = lax.ppermute(c2[h:], axis, ring(-1))
    s1 = jnp.concatenate([c1[:h] + near_p, c1[h:]], axis=0)
    s3 = jnp.concatenate([c3[:h], c3[h:] + near_m], axis=0)
    return c0 + lax.ppermute(s1, axis, ring(1)) + lax.ppermute(s3, axis, ring(-1))


def scatter_plane(own, other):
    both = own + lax.ppermute(other, "c", ring(1, 2))
    cut = lambda v, n: [v[n * i : n * (i + 1)] for i in range(4)]
    a = scatter_whole(*cut(both[:512], 128), "x")
    b = scatter_whole(*cut(both[512:], 128), "y")
    a = scatter_whole(*cut(a, 32), "y")
    b = scatter_whole(*cut(b, 32), "x")
    return jnp.concatenate([a, b], axis=0)


def receive_lists(all_ids, me):
    entries = all_ids.shape[1]
    mine = all_ids // PBLOCKS_DEV == me
    hit = mine.astype(jnp.int32)
    earlier = (
        jnp.arange(entries, dtype=jnp.int32)[:, None] < jnp.arange(entries, dtype=jnp.int32)[None]
    ).astype(jnp.float32)
    rank = jnp.dot(hit.astype(jnp.float32), earlier).astype(jnp.int32)
    src = jnp.arange(SHARDS, dtype=jnp.int32)[:, None]
    block = all_ids % PBLOCKS_DEV
    row = src * (2 * BLOCK) + (rank // 2) * BLOCK
    shift = ((rank + block) % 2) * (BLOCK // 2)
    per_row = jnp.sum(hit.reshape(SHARDS, -1, SLOTS_DEV), axis=2)
    row_total = jnp.sum(per_row, axis=0)
    order = jnp.arange(ROWS // BLOCK + 1, dtype=jnp.int32)
    start = jnp.sum(jnp.where(order[None, :-1] < order[:, None], row_total[None, :], 0), axis=1)
    before_src = (
        jnp.arange(SHARDS, dtype=jnp.int32)[:, None] > jnp.arange(SHARDS, dtype=jnp.int32)[None]
    )
    src_before = jnp.sum(jnp.where(before_src[:, :, None], per_row[None], 0), axis=1)
    hit4 = hit.reshape(SHARDS, -1, SLOTS_DEV)
    inner = jnp.cumsum(hit4, axis=2) - hit4
    place = start[None, :-1, None] + src_before[:, :, None] + inner
    place = jnp.where(mine, place.reshape(SHARDS, entries), -1).reshape(1, -1)
    onehot = place == jnp.arange(SHARDS * CAP, dtype=jnp.int32)[:, None]
    pick = lambda v: jnp.sum(jnp.where(onehot, v.reshape(1, -1), 0), axis=1)
    return start, pick(row), pick(shift), pick(block)


def per_device(queries, passages, teacher, block_ids):
    mz, my, mx, mc = (lax.axis_index(a) for a in ("pb", "y", "x", "c"))
    me = my * 8 + mx * 2 + mc
    pos = jnp.stack([mz, my, mx, mc]).astype(jnp.int32)
    flat_ids = block_ids.reshape(-1)
    sent = pack(flat_ids, teacher)
    exchange = functools.partial(
        lax.all_to_all, axis_name=PLANE, split_axis=0, concat_axis=0, tiled=True
    )
    all_ids = exchange(jnp.broadcast_to(flat_ids[None], (SHARDS, flat_ids.shape[0])))
    recv = [exchange(part) for part in sent]
    halves = passages.reshape(PBLOCKS_DEV, 2, BLOCK // 2, D)
    p0, p1 = (halves[:, i].reshape(D, D) for i in range(2))
    s0, s1, lse = score(queries, p0, p1, teacher)
    lse = merge_lse(lse)
    scalars = (pos,) + receive_lists(all_ids, me)
    ds0, loss0, *g0 = dscore(scalars, s0, lse, recv[0], queries)
    gp0 = scatter_halves(g0[0], g0[1:3], g0[3:5], g0[5:7], "pb")
    q0 = first_query(ds0, p0)
    ds1, loss1, *g1 = dscore(scalars, s1, lse, recv[1], queries)
    gp1 = scatter_halves(g1[0], g1[1:3], g1[3:5], g1[5:7], "pb")
    own, other = last_query(pos, ds1, p1, q0)
    grad_queries = scatter_plane(own, other)
    loss_part = exchange((loss0 + loss1).reshape(SHARDS, ROWS // SHARDS))
    lse_rows = lax.dynamic_slice_in_dim(
        lse[:, 0, :].reshape(ROWS), me * (ROWS // SHARDS), ROWS // SHARDS
    )
    loss = jnp.sum(loss_part, axis=0) + lse_rows
    grad_passages = jnp.stack(
        [gp0.reshape(4, BLOCK // 2, D), gp1.reshape(4, BLOCK // 2, D)], axis=1
    ).reshape(4 * BLOCK, D)
    return loss, grad_queries, grad_passages


def solution(mesh):
    fine = Mesh(mesh.devices.reshape(4, 4, 4, 2), ("pb",) + PLANE)
    in_specs = (P("pb", None), P(PLANE, None), P("pb", PLANE), P("pb", PLANE))
    out_specs = (P(("pb",) + PLANE), P(("pb",) + PLANE, None), P(PLANE + ("pb",), None))
    return jax.shard_map(
        per_device, mesh=fine, in_specs=in_specs, out_specs=out_specs, check_vma=False
    )
```

```python
import functools

import jax
import jax.numpy as jnp
from jax import lax
from jax.experimental import pallas as pl
from jax.experimental.pallas import tpu as pltpu
from jax.sharding import Mesh
from jax.sharding import PartitionSpec as P


BLOCK = 128
D = 1024
ROWS = 2048
PBLOCKS_DEV = 16
SLOTS_DEV = 4
CAP = 4
SHARDS = 32
ENTRIES = 64
PACK_STEP = 8
QUARTER = 32
LSE_ROWS = 32
PLANE = ("y", "x", "c")
SCORE_SCALE = 0.0625
GRAD_SCALE = 64.0


def as_row(column):
    n = column.shape[0]
    return jnp.broadcast_to(column, (n, BLOCK)).T[0:1, :]


def as_lanes(row):
    n = row.shape[1]
    return jnp.broadcast_to(row, (BLOCK, n)).T


def pack_kernel(piece, ids_ref, teacher_ref, out_ref, slot_ref, count_ref):
    step = pl.program_id(0)

    @pl.when(step == 0)
    def _():
        for i in range(SHARDS):
            count_ref[i] = 0
        for i in range(SHARDS * CAP):
            slot_ref[i] = -1

        def place(i, carry):
            owner = ids_ref[i] // PBLOCKS_DEV
            rank = count_ref[owner]
            count_ref[owner] = rank + 1
            slot_ref[owner * CAP + jnp.minimum(rank, CAP - 1)] = i
            return carry

        lax.fori_loop(0, ENTRIES, place, 0, unroll=8)

    quarter = lax.broadcasted_iota(jnp.int32, (BLOCK, BLOCK), 1) // QUARTER
    lane = lax.broadcasted_iota(jnp.int32, (8, BLOCK), 1)
    move = lambda t, lanes: t if lanes % BLOCK == 0 else pltpu.roll(t, lanes % BLOCK, 1)
    for j in range(PACK_STEP):
        meta = jnp.zeros((8, BLOCK), jnp.float32)
        tiles = []
        for k in range(CAP):
            slot = slot_ref[(step * PACK_STEP + j) * CAP + k]
            entry = jnp.maximum(slot, 0)
            row = pl.multiple_of((entry // SLOTS_DEV) * BLOCK, BLOCK)
            col = pl.multiple_of((entry % SLOTS_DEV) * BLOCK, BLOCK)
            tiles.append(teacher_ref[pl.ds(row, BLOCK), pl.ds(col, BLOCK)])
            if piece == 0:
                where = jnp.where(slot < 0, -1, entry // SLOTS_DEV).astype(jnp.float32)
                block = (ids_ref[entry] % PBLOCKS_DEV).astype(jnp.float32)
                meta = jnp.where(lane == k, where, meta)
                meta = jnp.where(lane == CAP + k, block, meta)
        if piece < 2:
            moved = [move(t, QUARTER * (k - piece)) for k, t in enumerate(tiles)]
            low = jnp.where(quarter == 0, moved[0], moved[1])
            high = jnp.where(quarter == 2, moved[2], moved[3])
            out_ref[j, :BLOCK, :] = jnp.where(quarter < 2, low, high)
        else:
            for pair in range(CAP // 2):
                first = pltpu.roll(tiles[2 * pair], BLOCK // 2, 1)
                rows = slice(pair * BLOCK, (pair + 1) * BLOCK)
                out_ref[j, rows, :] = jnp.where(quarter < 2, first, tiles[2 * pair + 1])
        if piece == 0:
            out_ref[j, BLOCK:, :] = meta


def pack(piece, ids, teacher):
    rows = (BLOCK + 8, BLOCK, 2 * BLOCK)[piece]
    total = rows + (LSE_ROWS if piece == 1 else 0)
    return pl.pallas_call(
        functools.partial(pack_kernel, piece),
        out_shape=jax.ShapeDtypeStruct((SHARDS, total, BLOCK), jnp.float32),
        grid_spec=pltpu.PrefetchScalarGridSpec(
            num_scalar_prefetch=1,
            grid=(SHARDS // PACK_STEP,),
            in_specs=[pl.BlockSpec((ROWS, SLOTS_DEV * BLOCK), lambda s, ids: (0, 0))],
            out_specs=pl.BlockSpec((PACK_STEP, rows, BLOCK), lambda s, ids: (s, 0, 0)),
            scratch_shapes=[
                pltpu.SMEM((SHARDS * CAP,), jnp.int32),
                pltpu.SMEM((SHARDS,), jnp.int32),
            ],
        ),
        name="pack",
    )(ids, teacher)


def fill_kernel(lse_ref, sent_ref, out_ref):
    out_ref[...] = jnp.broadcast_to(lse_ref[...][None], out_ref.shape)


def fill_lse(sent, lse):
    return pl.pallas_call(
        fill_kernel,
        out_shape=jax.ShapeDtypeStruct(sent.shape, sent.dtype),
        grid=(1,),
        in_specs=[
            pl.BlockSpec((LSE_ROWS, BLOCK), lambda i: (0, 0)),
            pl.BlockSpec(memory_space=pl.ANY),
        ],
        out_specs=pl.BlockSpec((SHARDS, LSE_ROWS, BLOCK), lambda i: (0, BLOCK // LSE_ROWS, 0)),
        input_output_aliases={1: 0},
        name="fill_lse",
    )(lse, sent)


def list_kernel(meta_ref, start_ref, row_ref, block_ref, next_ref):
    blocks = ROWS // BLOCK
    for r in range(blocks):
        next_ref[r] = 0

    def count(n, carry):
        r = meta_ref[(n // CAP) * (2 * CAP) + n % CAP]

        @pl.when(r >= 0)
        def _():
            next_ref[r] = next_ref[r] + 1

        row_ref[n] = 0
        block_ref[n] = 0
        return carry

    lax.fori_loop(0, SHARDS * CAP, count, 0, unroll=4)
    total = 0
    for r in range(blocks):
        start_ref[r] = total
        size = next_ref[r]
        next_ref[r] = total
        total = total + size
    start_ref[blocks] = total

    def place(n, carry):
        src, k = n // CAP, n % CAP
        r = meta_ref[src * (2 * CAP) + k]

        @pl.when(r >= 0)
        def _():
            at = next_ref[r]
            next_ref[r] = at + 1
            row_ref[at] = n
            block_ref[at] = meta_ref[src * (2 * CAP) + CAP + k]

        return carry

    lax.fori_loop(0, SHARDS * CAP, place, 0, unroll=4)


def make_lists(meta):
    smem = pl.BlockSpec(memory_space=pltpu.SMEM)
    ints = lambda n: jax.ShapeDtypeStruct((n,), jnp.int32)
    return pl.pallas_call(
        list_kernel,
        out_shape=(ints(ROWS // BLOCK + 1), ints(SHARDS * CAP), ints(SHARDS * CAP)),
        in_specs=[smem],
        out_specs=(smem, smem, smem),
        scratch_shapes=[pltpu.SMEM((ROWS // BLOCK,), jnp.int32)],
        name="make_lists",
    )(meta)


def score_kernel(q_ref, p_ref, t_ref, s0_ref, s1_ref, lse_ref, p0_ref, p1_ref):
    half = BLOCK // 2

    @pl.when(pl.program_id(0) == 0)
    def _():
        for block in range(PBLOCKS_DEV):
            here = slice(block * half, (block + 1) * half)
            p0_ref[here, :] = p_ref[block * BLOCK : block * BLOCK + half, :]
            p1_ref[here, :] = p_ref[block * BLOCK + half : (block + 1) * BLOCK, :]

    q = q_ref[...]
    nt = (((1,), (1,)), ((), ()))
    s0 = lax.dot_general(q, p0_ref[...], nt, preferred_element_type=jnp.float32) * SCORE_SCALE
    s1 = lax.dot_general(q, p1_ref[...], nt, preferred_element_type=jnp.float32) * SCORE_SCALE
    s0_ref[...] = s0
    s1_ref[...] = s1
    top = jnp.maximum(jnp.max(s0, axis=1, keepdims=True), jnp.max(s1, axis=1, keepdims=True))
    total = jnp.sum(jnp.exp(s0 - top), axis=1, keepdims=True) + jnp.sum(
        jnp.exp(s1 - top), axis=1, keepdims=True
    )
    lse_ref[0, 0:1, :] = as_row(top + jnp.log(total))
    t = t_ref[...]
    ttop = jnp.max(t, axis=1, keepdims=True)
    ttotal = jnp.sum(jnp.exp(t - ttop), axis=1, keepdims=True)
    lse_ref[0, 1:2, :] = as_row(ttop + jnp.log(ttotal))


def score(queries, passages, teacher):
    rb = 256
    block = pl.BlockSpec((rb, D), lambda i: (i, 0))
    whole = pl.BlockSpec((D, D), lambda i: (0, 0))
    scores = jax.ShapeDtypeStruct((ROWS, D), jnp.float32)
    part = jax.ShapeDtypeStruct((D, D), jnp.bfloat16)
    return pl.pallas_call(
        score_kernel,
        out_shape=(
            scores,
            scores,
            jax.ShapeDtypeStruct((ROWS // rb, 2, rb), jnp.float32),
            part,
            part,
        ),
        grid=(ROWS // rb,),
        in_specs=[
            block,
            pl.BlockSpec((ROWS, D), lambda i: (0, 0)),
            pl.BlockSpec((rb, SLOTS_DEV * BLOCK), lambda i: (i, 0)),
        ],
        out_specs=(block, block, pl.BlockSpec((1, 2, rb), lambda i: (i, 0, 0)), whole, whole),
        name="score",
    )(queries, passages, teacher)


def rows_kernel(
    last, pos_ref, start_ref, row_ref, block_ref, s_ref, lse_ref, *refs
):
    if last:
        recv_ref, p_ref, add_ref, ds_ref, loss_ref, own_ref, other_ref, w_ref, lt_ref, acc_ref = refs
    else:
        recv_ref, recv2_ref, p_ref, ds_ref, loss_ref, out_ref, w_ref, lt_ref, acc_ref = refs
    step = pl.program_id(0)
    rb = 256
    half = BLOCK // 2
    ls = as_lanes(lse_ref[0, 0:1, :])
    lt_ref[...] = as_lanes(lse_ref[0, 1:2, :])
    for j in range(D // BLOCK):
        cols = slice(j * BLOCK, (j + 1) * BLOCK)
        w_ref[:, cols] = jnp.exp(s_ref[:, cols] - ls)
    acc_ref[...] = jnp.zeros_like(acc_ref)
    lane = lax.broadcasted_iota(jnp.int32, (BLOCK, BLOCK), 1)
    side = lane // half
    early = lane % half < QUARTER

    def fetch(n):
        slot = row_ref[n]
        block = block_ref[n]
        src, k = slot // CAP, slot % CAP
        shift = (block % 2) * half
        if last:
            at = pl.multiple_of(src * (2 * BLOCK) + (k // 2) * BLOCK, BLOCK)
            x = recv_ref[pl.ds(at, BLOCK), :]
            x = pltpu.roll(x, (shift + (k % 2) * half) % BLOCK, 1)
        else:
            at = pl.multiple_of(src * (BLOCK + 8), 8)
            x = recv_ref[pl.ds(at, BLOCK), :]
            x = pltpu.roll(x, (shift - k * QUARTER + BLOCK) % BLOCK, 1)
            at = pl.multiple_of(src * (BLOCK + LSE_ROWS), 8)
            y = recv2_ref[pl.ds(at, BLOCK), :]
            y = pltpu.roll(y, (shift + QUARTER - k * QUARTER + BLOCK) % BLOCK, 1)
            x = jnp.where(early, x, y)
        return x, block

    for sub in range(rb // BLOCK):
        rows = slice(sub * BLOCK, (sub + 1) * BLOCK)
        r = step * (rb // BLOCK) + sub
        end = start_ref[r + 1]

        def body(n, carry):
            first = start_ref[r] + 2 * n
            parts = []
            for at in (first, first + 1):
                x, block = fetch(jnp.minimum(at, end - 1))
                keep = (side == block % 2) & (at < end)
                centred = x - lt_ref[rows, :]
                prob = jnp.where(keep, jnp.exp(centred), 0.0)
                cols = pl.ds(pl.multiple_of((block // 2) * BLOCK, BLOCK), BLOCK)
                term = jnp.where(keep, prob * (centred - s_ref[rows, cols]), 0.0)
                parts.append((prob, cols, term))
            acc_ref[rows, :] = acc_ref[rows, :] + (parts[0][2] + parts[1][2])
            for prob, cols, _ in parts:
                w_ref[rows, cols] = w_ref[rows, cols] - prob
            return carry

        lax.fori_loop(0, (end - start_ref[r] + 1) // 2, body, 0)
    ds = (w_ref[...] * GRAD_SCALE).astype(jnp.bfloat16)
    ds_ref[...] = ds
    loss_ref[0] = as_row(jnp.sum(acc_ref[...], axis=1, keepdims=True))
    part = jnp.dot(ds, p_ref[...], preferred_element_type=jnp.float32)
    if not last:
        out_ref[...] = part
        return
    part = part + add_ref[...]
    dy = (step // 2 + 4 - pos_ref[1]) % 4
    for j in range(4):
        dx = (2 * step + j // 2 + 4 - pos_ref[2]) % 4
        a = pl.ds(pl.multiple_of(dx * 128 + dy * 32, 32), 32)
        b = pl.ds(pl.multiple_of(512 + dy * 128 + dx * 32, 32), 32)

        @pl.when(pos_ref[3] == j % 2)
        def _():
            own_ref[a, :] = part[64 * j : 64 * j + 32]
            own_ref[b, :] = part[64 * j + 32 : 64 * j + 64]

        @pl.when(pos_ref[3] != j % 2)
        def _():
            other_ref[a, :] = part[64 * j : 64 * j + 32]
            other_ref[b, :] = part[64 * j + 32 : 64 * j + 64]


def rows_call(scalars, scores, lse, recvs, passages, add=None):
    rb = 256
    last = add is not None
    recvs = [r.reshape(-1, BLOCK) for r in recvs]
    block = pl.BlockSpec((rb, D), lambda i, *_: (i, 0))
    full = lambda *shape: pl.BlockSpec(shape, lambda i, *_: (0,) * len(shape))
    grad = jax.ShapeDtypeStruct((ROWS // 2 if last else ROWS, D), jnp.float32)
    return pl.pallas_call(
        functools.partial(rows_kernel, last),
        out_shape=(
            jax.ShapeDtypeStruct((ROWS, D), jnp.bfloat16),
            jax.ShapeDtypeStruct((ROWS // rb, 1, rb), jnp.float32),
        )
        + ((grad, grad) if last else (grad,)),
        grid_spec=pltpu.PrefetchScalarGridSpec(
            num_scalar_prefetch=len(scalars),
            grid=(ROWS // rb,),
            in_specs=[block, pl.BlockSpec((1, 2, rb), lambda i, *_: (i, 0, 0))]
            + [full(*r.shape) for r in recvs]
            + [full(D, D)]
            + ([block] if last else []),
            out_specs=(block, pl.BlockSpec((1, 1, rb), lambda i, *_: (i, 0, 0)))
            + ((full(ROWS // 2, D),) * 2 if last else (block,)),
            scratch_shapes=[
                pltpu.VMEM((rb, D), jnp.float32),
                pltpu.VMEM((rb, BLOCK), jnp.float32),
                pltpu.VMEM((rb, BLOCK), jnp.float32),
            ],
        ),
        name="rows",
    )(*scalars, scores, lse, *recvs, passages, *([add] if last else []))


def columns_kernel(pos_ref, ds_ref, q_ref, *outs):
    groups = {0: outs[:1], 1: outs[1:3], 2: outs[3:5], 3: outs[5:7]}
    for d in (2, 1, 3, 0):
        off = pl.multiple_of(((pos_ref[0] + d) % 4) * (D // 4), D // 4)
        part = lax.dot_general(
            ds_ref[:, pl.ds(off, D // 4)],
            q_ref[...],
            (((0,), (0,)), ((), ())),
            preferred_element_type=jnp.float32,
        )
        size = D // 4 // len(groups[d])
        for i, out in enumerate(groups[d]):
            out[...] = part[size * i : size * (i + 1)]


def columns_call(pos, ds, queries):
    full = lambda *shape: pl.BlockSpec(shape, lambda i, *_: (0,) * len(shape))
    sizes = (D // 4,) + (D // 8,) * 6
    return pl.pallas_call(
        columns_kernel,
        out_shape=tuple(jax.ShapeDtypeStruct((n, D), jnp.float32) for n in sizes),
        grid_spec=pltpu.PrefetchScalarGridSpec(
            num_scalar_prefetch=1,
            grid=(1,),
            in_specs=[full(ROWS, D), full(ROWS, D)],
            out_specs=tuple(full(n, D) for n in sizes),
        ),
        name="columns",
    )(pos, ds, queries)


def ring(d, n=4):
    return [(i, (i + d) % n) for i in range(n)]


def combine_kernel(own_ref, other_ref, *outs):
    for base, group in ((0, outs[:5]), (512, outs[5:])):
        at = lambda lo, n: own_ref[base + lo : base + lo + n] + other_ref[base + lo : base + lo + n]
        group[0][...] = at(0, 128)
        group[1][...] = at(128, 128)
        group[2][...] = at(256, 64)
        group[3][...] = at(320, 64)
        group[4][...] = at(384, 128)


def combine(own, other):
    full = lambda n: pl.BlockSpec((n, D), lambda i: (0, 0))
    sizes = (128, 128, 64, 64, 128) * 2
    return pl.pallas_call(
        combine_kernel,
        out_shape=tuple(jax.ShapeDtypeStruct((n, D), jnp.float32) for n in sizes),
        grid=(1,),
        in_specs=[full(ROWS // 2)] * 2,
        out_specs=tuple(full(n) for n in sizes),
        name="combine",
    )(own, other)


def send(value, axis, d, n=4):
    return lax.ppermute(value, axis, ring(d, n))


def together(*values):
    return lax.optimization_barrier(values)


def near(low, high, axis):
    return [send(low, axis, 1), send(high, axis, -1)]


def far(c1, c3, near_p, near_m, axis):
    h = near_p.shape[0]
    s1 = jnp.concatenate([c1[:h] + near_p, c1[h:]], axis=0)
    s3 = jnp.concatenate([c3[:h], c3[h:] + near_m], axis=0)
    return [send(s1, axis, 1), send(s3, axis, -1)]


def per_device(queries, passages, teacher, block_ids):
    mz, my, mx, mc = (lax.axis_index(a) for a in ("pb", "y", "x", "c"))
    me = my * 8 + mx * 2 + mc
    pos = jnp.stack([mz, my, mx, mc]).astype(jnp.int32)
    flat_ids = block_ids.reshape(-1)
    exchange = functools.partial(
        lax.all_to_all, axis_name=PLANE, split_axis=0, concat_axis=0, tiled=True
    )
    sent0 = pack(0, flat_ids, teacher)
    recv0 = exchange(sent0)
    ids1, _ = together(flat_ids, sent0)
    sent1 = pack(1, ids1, teacher)
    s0, s1, lse, p0, p1 = score(queries, passages, teacher)
    sent1 = fill_lse(sent1, lse.reshape(LSE_ROWS, BLOCK))
    recv1 = exchange(sent1)
    ids2, _ = together(flat_ids, lse)
    sent2 = pack(2, ids2, teacher)
    sent2, _ = together(sent2, recv1[0, 0, 0])
    recv2 = exchange(sent2)
    meta = recv0[:, BLOCK, : 2 * CAP].astype(jnp.int32).reshape(-1)
    scalars = (pos,) + tuple(make_lists(meta))
    every = recv1[:, BLOCK:, :]
    top = jnp.max(every, axis=0)
    lse = top + jnp.log(jnp.sum(jnp.exp(every - top[None]), axis=0))
    lse = lse.reshape(8, 2, 256)
    ds0, loss0, q0 = rows_call(scalars, s0, lse, [recv0, recv1], p0)
    g0 = columns_call(pos, ds0, queries)
    z0 = [g0[0], g0[1:3], g0[3:5], g0[5:7]]
    np0, nm0 = send(z0[2][0], "pb", 1), send(z0[2][1], "pb", -1)
    fp0, fm0 = send(z0[1][1], "pb", 1), send(z0[3][0], "pb", -1)
    sp0 = send(z0[1][0] + np0, "pb", 1)
    sm0 = send(z0[3][1] + nm0, "pb", -1)

    ds1, loss1, own, other = rows_call(scalars, s1, lse, [recv2], p1, q0)
    swapped = send(other, "c", 1, 2)
    g1 = columns_call(pos, ds1, queries)
    z1 = [g1[0], g1[1:3], g1[3:5], g1[5:7]]
    np1, nm1 = send(z1[2][0], "pb", 1), send(z1[2][1], "pb", -1)
    fp1, fm1 = send(z1[1][1], "pb", 1), send(z1[3][0], "pb", -1)
    a0, a1, a2, a3, a4, b0, b1, b2, b3, b4 = combine(own, swapped)
    loss_sum = (loss0 + loss1).reshape(SHARDS, ROWS // SHARDS)
    np1, nm1, apn, anm, bpn, bnm, loss_sum = together(
        np1, nm1, *near(a2, a3, "x"), *near(b2, b3, "y"), loss_sum
    )
    af, bf = far(a1, a4, apn, anm, "x"), far(b1, b4, bpn, bnm, "y")
    sp1 = send(z1[1][0] + np1, "pb", 1)
    sm1 = send(z1[3][1] + nm1, "pb", -1)
    loss_part = exchange(loss_sum)
    af0, af1, bf0, bf1 = together(*af, *bf)
    cut = lambda v: [v[32 * i : 32 * (i + 1)] for i in range(4)]
    a, b = cut(a0 + af0 + af1), cut(b0 + bf0 + bf1)
    apn, anm, bpn, bnm = together(
        *near(a[2][:16], a[2][16:], "y"), *near(b[2][:16], b[2][16:], "x")
    )
    af, bf = far(a[1], a[3], apn, anm, "y"), far(b[1], b[3], bpn, bnm, "x")
    af0, af1, bf0, bf1 = together(*af, *bf)
    grad_queries = jnp.concatenate([a[0] + af0 + af1, b[0] + bf0 + bf1], axis=0)

    h = D // 8
    parts = [
        z0[0][:h] + sp0 + fm0,
        z0[0][h:] + fp0 + sm0,
        z1[0][:h] + sp1 + fm1,
        z1[0][h:] + fp1 + sm1,
    ]
    gp0, gp1 = jnp.concatenate(parts[:2]), jnp.concatenate(parts[2:])
    lse_rows = lax.dynamic_slice_in_dim(
        lse[:, 0, :].reshape(ROWS), me * (ROWS // SHARDS), ROWS // SHARDS
    )
    loss = jnp.sum(loss_part, axis=0) + lse_rows
    grad_passages = jnp.stack(
        [gp0.reshape(4, BLOCK // 2, D), gp1.reshape(4, BLOCK // 2, D)], axis=1
    ).reshape(4 * BLOCK, D)
    return loss, grad_queries, grad_passages


def solution(mesh):
    fine = Mesh(mesh.devices.reshape(4, 4, 4, 2), ("pb",) + PLANE)
    in_specs = (P("pb", None), P(PLANE, None), P("pb", PLANE), P("pb", PLANE))
    out_specs = (P(("pb",) + PLANE), P(("pb",) + PLANE, None), P(PLANE + ("pb",), None))
    return jax.shard_map(
        per_device, mesh=fine, in_specs=in_specs, out_specs=out_specs, check_vma=False
    )
```

```python
import functools

import jax
import jax.numpy as jnp
from jax import lax
from jax.experimental import pallas as pl
from jax.experimental.pallas import tpu as pltpu
from jax.sharding import Mesh
from jax.sharding import PartitionSpec as P


BLOCK = 128
D = 1024
ROWS = 2048
PBLOCKS_DEV = 16
SLOTS_DEV = 4
CAP = 4
SHARDS = 32
ENTRIES = 64
PACK_STEP = 8
QUARTER = 32
LSE_ROWS = 32
PLANE = ("y", "x", "c")
SCORE_SCALE = 0.0625
GRAD_SCALE = 64.0


def as_row(column):
    n = column.shape[0]
    return jnp.broadcast_to(column, (n, BLOCK)).T[0:1, :]


def as_lanes(row):
    n = row.shape[1]
    return jnp.broadcast_to(row, (BLOCK, n)).T


def pack_kernel(piece, ids_ref, teacher_ref, out_ref, slot_ref, count_ref):
    step = pl.program_id(0)

    @pl.when(step == 0)
    def _():
        for i in range(SHARDS):
            count_ref[i] = 0
        for i in range(SHARDS * CAP):
            slot_ref[i] = -1

        def place(i, carry):
            owner = ids_ref[i] // PBLOCKS_DEV
            rank = count_ref[owner]
            count_ref[owner] = rank + 1
            slot_ref[owner * CAP + jnp.minimum(rank, CAP - 1)] = i
            return carry

        lax.fori_loop(0, ENTRIES, place, 0, unroll=8)

    quarter = lax.broadcasted_iota(jnp.int32, (BLOCK, BLOCK), 1) // QUARTER
    lane = lax.broadcasted_iota(jnp.int32, (8, BLOCK), 1)
    move = lambda t, lanes: t if lanes % BLOCK == 0 else pltpu.roll(t, lanes % BLOCK, 1)
    for j in range(PACK_STEP):
        meta = jnp.zeros((8, BLOCK), jnp.float32)
        tiles = []
        for k in range(CAP):
            slot = slot_ref[(step * PACK_STEP + j) * CAP + k]
            entry = jnp.maximum(slot, 0)
            row = pl.multiple_of((entry // SLOTS_DEV) * BLOCK, BLOCK)
            col = pl.multiple_of((entry % SLOTS_DEV) * BLOCK, BLOCK)
            tiles.append(teacher_ref[pl.ds(row, BLOCK), pl.ds(col, BLOCK)])
            if piece == 0:
                where = jnp.where(slot < 0, -1, entry // SLOTS_DEV).astype(jnp.float32)
                block = (ids_ref[entry] % PBLOCKS_DEV).astype(jnp.float32)
                meta = jnp.where(lane == k, where, meta)
                meta = jnp.where(lane == CAP + k, block, meta)
        if piece < 2:
            moved = [move(t, QUARTER * (k - piece)) for k, t in enumerate(tiles)]
            low = jnp.where(quarter == 0, moved[0], moved[1])
            high = jnp.where(quarter == 2, moved[2], moved[3])
            out_ref[j, :BLOCK, :] = jnp.where(quarter < 2, low, high)
        else:
            for pair in range(CAP // 2):
                first = pltpu.roll(tiles[2 * pair], BLOCK // 2, 1)
                both = jnp.where(quarter < 2, first, tiles[2 * pair + 1])
                for end in range(2):
                    at = 2 * QUARTER * end + QUARTER * (piece - 2)
                    out = QUARTER * (2 * pair + end)
                    out_ref[j, out : out + QUARTER, :] = both[at : at + QUARTER]
        if piece == 0:
            out_ref[j, BLOCK:, :] = meta


def pack(piece, ids, teacher):
    rows = BLOCK + (8 if piece == 0 else 0)
    total = rows + (LSE_ROWS if piece == 1 else 0)
    return pl.pallas_call(
        functools.partial(pack_kernel, piece),
        out_shape=jax.ShapeDtypeStruct((SHARDS, total, BLOCK), jnp.float32),
        grid_spec=pltpu.PrefetchScalarGridSpec(
            num_scalar_prefetch=1,
            grid=(SHARDS // PACK_STEP,),
            in_specs=[pl.BlockSpec((ROWS, SLOTS_DEV * BLOCK), lambda s, ids: (0, 0))],
            out_specs=pl.BlockSpec((PACK_STEP, rows, BLOCK), lambda s, ids: (s, 0, 0)),
            scratch_shapes=[
                pltpu.SMEM((SHARDS * CAP,), jnp.int32),
                pltpu.SMEM((SHARDS,), jnp.int32),
            ],
        ),
        name="pack",
    )(ids, teacher)


def fill_kernel(lse_ref, sent_ref, out_ref):
    out_ref[...] = jnp.broadcast_to(lse_ref[...][None], out_ref.shape)


def fill_lse(sent, lse):
    return pl.pallas_call(
        fill_kernel,
        out_shape=jax.ShapeDtypeStruct(sent.shape, sent.dtype),
        grid=(1,),
        in_specs=[
            pl.BlockSpec((LSE_ROWS, BLOCK), lambda i: (0, 0)),
            pl.BlockSpec(memory_space=pl.ANY),
        ],
        out_specs=pl.BlockSpec((SHARDS, LSE_ROWS, BLOCK), lambda i: (0, BLOCK // LSE_ROWS, 0)),
        input_output_aliases={1: 0},
        name="fill_lse",
    )(lse, sent)


def list_kernel(meta_ref, start_ref, row_ref, block_ref, next_ref):
    blocks = ROWS // BLOCK
    for r in range(blocks):
        next_ref[r] = 0

    def count(n, carry):
        r = meta_ref[(n // CAP) * (2 * CAP) + n % CAP]

        @pl.when(r >= 0)
        def _():
            next_ref[r] = next_ref[r] + 1

        row_ref[n] = 0
        block_ref[n] = 0
        return carry

    lax.fori_loop(0, SHARDS * CAP, count, 0, unroll=4)
    total = 0
    for r in range(blocks):
        start_ref[r] = total
        size = next_ref[r]
        next_ref[r] = total
        total = total + size
    start_ref[blocks] = total

    def place(n, carry):
        src, k = n // CAP, n % CAP
        r = meta_ref[src * (2 * CAP) + k]

        @pl.when(r >= 0)
        def _():
            at = next_ref[r]
            next_ref[r] = at + 1
            row_ref[at] = n
            block_ref[at] = meta_ref[src * (2 * CAP) + CAP + k]

        return carry

    lax.fori_loop(0, SHARDS * CAP, place, 0, unroll=4)


def make_lists(meta):
    smem = pl.BlockSpec(memory_space=pltpu.SMEM)
    ints = lambda n: jax.ShapeDtypeStruct((n,), jnp.int32)
    return pl.pallas_call(
        list_kernel,
        out_shape=(ints(ROWS // BLOCK + 1), ints(SHARDS * CAP), ints(SHARDS * CAP)),
        in_specs=[smem],
        out_specs=(smem, smem, smem),
        scratch_shapes=[pltpu.SMEM((ROWS // BLOCK,), jnp.int32)],
        name="make_lists",
    )(meta)


def score_kernel(q_ref, p_ref, t_ref, s0_ref, s1_ref, lse_ref, p0_ref, p1_ref):
    half = BLOCK // 2

    @pl.when(pl.program_id(0) == 0)
    def _():
        for block in range(PBLOCKS_DEV):
            here = slice(block * half, (block + 1) * half)
            p0_ref[here, :] = p_ref[block * BLOCK : block * BLOCK + half, :]
            p1_ref[here, :] = p_ref[block * BLOCK + half : (block + 1) * BLOCK, :]

    q = q_ref[...]
    nt = (((1,), (1,)), ((), ()))
    s0 = lax.dot_general(q, p0_ref[...], nt, preferred_element_type=jnp.float32) * SCORE_SCALE
    s1 = lax.dot_general(q, p1_ref[...], nt, preferred_element_type=jnp.float32) * SCORE_SCALE
    s0_ref[...] = s0
    s1_ref[...] = s1
    top = jnp.maximum(jnp.max(s0, axis=1, keepdims=True), jnp.max(s1, axis=1, keepdims=True))
    total = jnp.sum(jnp.exp(s0 - top), axis=1, keepdims=True) + jnp.sum(
        jnp.exp(s1 - top), axis=1, keepdims=True
    )
    lse_ref[0, 0:1, :] = as_row(top + jnp.log(total))
    t = t_ref[...]
    ttop = jnp.max(t, axis=1, keepdims=True)
    ttotal = jnp.sum(jnp.exp(t - ttop), axis=1, keepdims=True)
    lse_ref[0, 1:2, :] = as_row(ttop + jnp.log(ttotal))


def score(queries, passages, teacher):
    rb = 256
    block = pl.BlockSpec((rb, D), lambda i: (i, 0))
    whole = pl.BlockSpec((D, D), lambda i: (0, 0))
    scores = jax.ShapeDtypeStruct((ROWS, D), jnp.float32)
    part = jax.ShapeDtypeStruct((D, D), jnp.bfloat16)
    return pl.pallas_call(
        score_kernel,
        out_shape=(
            scores,
            scores,
            jax.ShapeDtypeStruct((ROWS // rb, 2, rb), jnp.float32),
            part,
            part,
        ),
        grid=(ROWS // rb,),
        in_specs=[
            block,
            pl.BlockSpec((ROWS, D), lambda i: (0, 0)),
            pl.BlockSpec((rb, SLOTS_DEV * BLOCK), lambda i: (i, 0)),
        ],
        out_specs=(block, block, pl.BlockSpec((1, 2, rb), lambda i: (i, 0, 0)), whole, whole),
        name="score",
    )(queries, passages, teacher)


def subtract_tiles(
    fetch, sub_rows, first, end, block_ref, s_cols, lt_ref, rows, w_ref, acc_ref
):
    lane = lax.broadcasted_iota(jnp.int32, (sub_rows, BLOCK), 1)
    side = lane // (BLOCK // 2)

    def body(n, carry):
        parts = []
        for at in (first + 2 * n, first + 2 * n + 1):
            here = jnp.minimum(at, end - 1)
            block = block_ref[here]
            x = fetch(here, block)
            keep = (side == block % 2) & (at < end)
            centred = x - lt_ref[rows, :]
            prob = jnp.where(keep, jnp.exp(centred), 0.0)
            cols = pl.ds(pl.multiple_of((block // 2) * BLOCK, BLOCK), BLOCK)
            term = jnp.where(keep, prob * (centred - s_cols(cols)), 0.0)
            parts.append((prob, cols, term))
        acc_ref[rows, :] = acc_ref[rows, :] + (parts[0][2] + parts[1][2])
        for prob, cols, _ in parts:
            w_ref[rows, cols] = w_ref[rows, cols] - prob
        return carry

    lax.fori_loop(0, (end - first + 1) // 2, body, 0)


def rows0_kernel(
    start_ref, row_ref, block_ref, s_ref, lse_ref, recv0_ref, recv1_ref,
    ds_ref, loss_ref, w_ref, lt_ref, acc_ref,
):
    step = pl.program_id(0)
    rb = 256
    half = BLOCK // 2
    ls = as_lanes(lse_ref[0, 0:1, :])
    lt_ref[...] = as_lanes(lse_ref[0, 1:2, :])
    for j in range(D // BLOCK):
        cols = slice(j * BLOCK, (j + 1) * BLOCK)
        w_ref[:, cols] = jnp.exp(s_ref[:, cols] - ls)
    acc_ref[...] = jnp.zeros_like(acc_ref)
    early = lax.broadcasted_iota(jnp.int32, (BLOCK, BLOCK), 1) % half < QUARTER

    def fetch(n, block):
        slot = row_ref[n]
        src, k = slot // CAP, slot % CAP
        shift = (block % 2) * half
        at = pl.multiple_of(src * (BLOCK + 8), 8)
        x = recv0_ref[pl.ds(at, BLOCK), :]
        x = pltpu.roll(x, (shift - k * QUARTER + BLOCK) % BLOCK, 1)
        at = pl.multiple_of(src * (BLOCK + LSE_ROWS), 8)
        y = recv1_ref[pl.ds(at, BLOCK), :]
        y = pltpu.roll(y, (shift + QUARTER - k * QUARTER + BLOCK) % BLOCK, 1)
        return jnp.where(early, x, y)

    for sub in range(rb // BLOCK):
        rows = slice(sub * BLOCK, (sub + 1) * BLOCK)
        r = step * (rb // BLOCK) + sub
        subtract_tiles(
            fetch, BLOCK, start_ref[r], start_ref[r + 1], block_ref,
            lambda cols: s_ref[rows, cols], lt_ref, rows, w_ref, acc_ref,
        )
    ds_ref[...] = (w_ref[...] * GRAD_SCALE).astype(jnp.bfloat16)
    loss_ref[0] = as_row(jnp.sum(acc_ref[...], axis=1, keepdims=True))


ROW_SCRATCH = [
    pltpu.VMEM((256, D), jnp.float32),
    pltpu.VMEM((256, BLOCK), jnp.float32),
    pltpu.VMEM((256, BLOCK), jnp.float32),
]


def full_spec(*shape):
    return pl.BlockSpec(shape, lambda i, *_: (0,) * len(shape))


def rows0_call(lists, scores, lse, recvs):
    rb = 256
    recvs = [r.reshape(-1, BLOCK) for r in recvs]
    block = pl.BlockSpec((rb, D), lambda i, *_: (i, 0))
    return pl.pallas_call(
        rows0_kernel,
        out_shape=(
            jax.ShapeDtypeStruct((ROWS, D), jnp.bfloat16),
            jax.ShapeDtypeStruct((ROWS // rb, 1, rb), jnp.float32),
        ),
        grid_spec=pltpu.PrefetchScalarGridSpec(
            num_scalar_prefetch=len(lists),
            grid=(ROWS // rb,),
            in_specs=[block, pl.BlockSpec((1, 2, rb), lambda i, *_: (i, 0, 0))]
            + [full_spec(*r.shape) for r in recvs],
            out_specs=(block, pl.BlockSpec((1, 1, rb), lambda i, *_: (i, 0, 0))),
            scratch_shapes=ROW_SCRATCH,
        ),
        name="rows0",
    )(*lists, scores, lse, *recvs)


def rows1_kernel(
    pos_ref, start_ref, row_ref, block_ref, s_ref, lse_ref, recv_ref, ds0_ref, p0_ref, p1_ref,
    *refs,
):
    ds_ref, loss_ref, own_ref, other_ref, w_ref, lt_ref, acc_ref = refs[-7:]
    step = pl.program_id(0)
    rb = 256
    half = BLOCK // 2
    ls = as_lanes(lse_ref[0, 0:1, :])
    lt_ref[...] = as_lanes(lse_ref[0, 1:2, :])
    for j in range(D // BLOCK):
        cols = slice(j * BLOCK, (j + 1) * BLOCK)
        w_ref[:, cols] = jnp.exp(s_ref[:, 0, :, cols].reshape(rb, BLOCK) - ls)
    acc_ref[...] = jnp.zeros_like(acc_ref)

    def fetch(n, block):
        slot = row_ref[n]
        k = slot % CAP
        at = pl.multiple_of((slot // 2) * half, half)
        x = recv_ref[pl.ds(at, half), :]
        return pltpu.roll(x, ((block + k) % 2) * half, 1)

    for sub in range(rb // half):
        rows = slice(sub * half, (sub + 1) * half)
        r = step * (rb // half) + sub
        subtract_tiles(
            fetch, half, start_ref[r], start_ref[r + 1], block_ref,
            lambda cols: s_ref[2 * sub : 2 * sub + 2, 0, :, cols].reshape(half, BLOCK),
            lt_ref, rows, w_ref, acc_ref,
        )
    ds = (w_ref[...] * GRAD_SCALE).astype(jnp.bfloat16)
    ds_ref[...] = ds.reshape(ds_ref.shape)
    loss_ref[0] = as_row(jnp.sum(acc_ref[...], axis=1, keepdims=True))
    part = jnp.dot(ds, p1_ref[...], preferred_element_type=jnp.float32)
    ds0 = ds0_ref[...].reshape(rb, D)
    part = part + jnp.dot(ds0, p0_ref[...], preferred_element_type=jnp.float32)
    part = part.reshape(rb // QUARTER, 2, QUARTER // 2, D)

    @pl.when(pos_ref[3] == 0)
    def _():
        own_ref[...] = part[:, 0]
        other_ref[...] = part[:, 1]

    @pl.when(pos_ref[3] != 0)
    def _():
        own_ref[...] = part[:, 1]
        other_ref[...] = part[:, 0]


def rows1_call(h, scalars, scores, lse, recv, ds0, p0, p1, ds=None):
    rb = 256
    view = (SHARDS, 2, QUARTER, D)
    recv = recv.reshape(-1, BLOCK)
    group = pl.BlockSpec((rb // QUARTER, 1, QUARTER, D), lambda i, *_: (i, h, 0, 0))
    out = pl.BlockSpec((rb // QUARTER, QUARTER // 2, D), lambda i, *_: (i, 0, 0))
    out_type = jax.ShapeDtypeStruct((SHARDS, QUARTER // 2, D), jnp.float32)
    again = [] if ds is None else [ds]
    return pl.pallas_call(
        rows1_kernel,
        out_shape=(
            jax.ShapeDtypeStruct(view, jnp.bfloat16),
            jax.ShapeDtypeStruct((ROWS // 2 // rb, 1, rb), jnp.float32),
            out_type,
            out_type,
        ),
        grid_spec=pltpu.PrefetchScalarGridSpec(
            num_scalar_prefetch=len(scalars),
            grid=(ROWS // 2 // rb,),
            in_specs=[
                group,
                pl.BlockSpec((1, 2, rb), lambda i, *_: (i, 0, 0)),
                full_spec(*recv.shape),
                group,
                full_spec(D, D),
                full_spec(D, D),
            ]
            + [pl.BlockSpec(memory_space=pl.ANY)] * len(again),
            out_specs=(group, pl.BlockSpec((1, 1, rb), lambda i, *_: (i, 0, 0)), out, out),
            scratch_shapes=ROW_SCRATCH,
        ),
        input_output_aliases={len(scalars) + 6: 0} if again else {},
        name="rows1",
    )(*scalars, scores.reshape(view), lse, recv, ds0.reshape(view), p0, p1, *again)


def columns_kernel(pos_ref, ds_ref, q_ref, *outs):
    groups = {0: outs[:1], 1: outs[1:3], 2: outs[3:5], 3: outs[5:7]}
    for d in (2, 1, 3, 0):
        off = pl.multiple_of(((pos_ref[0] + d) % 4) * (D // 4), D // 4)
        part = lax.dot_general(
            ds_ref[:, pl.ds(off, D // 4)],
            q_ref[...],
            (((0,), (0,)), ((), ())),
            preferred_element_type=jnp.float32,
        )
        size = D // 4 // len(groups[d])
        for i, out in enumerate(groups[d]):
            out[...] = part[size * i : size * (i + 1)]


def columns_call(pos, ds, queries):
    full = lambda *shape: pl.BlockSpec(shape, lambda i, *_: (0,) * len(shape))
    sizes = (D // 4,) + (D // 8,) * 6
    return pl.pallas_call(
        columns_kernel,
        out_shape=tuple(jax.ShapeDtypeStruct((n, D), jnp.float32) for n in sizes),
        grid_spec=pltpu.PrefetchScalarGridSpec(
            num_scalar_prefetch=1,
            grid=(1,),
            in_specs=[full(ROWS, D), full(ROWS, D)],
            out_specs=tuple(full(n, D) for n in sizes),
        ),
        name="columns",
    )(pos, ds, queries)


def ring(d, n=4):
    return [(i, (i + d) % n) for i in range(n)]


def combine_kernel(own_ref, other_ref, *refs):
    out_ref = refs[-1]
    out_ref[:, :, :D] = own_ref[...] + other_ref[...]
    if len(refs) == 2:
        loss = refs[0][...]
        out_ref[:, :, D:] = jnp.broadcast_to(loss[:, None, :], (*out_ref.shape[:2], BLOCK))


def combine(own, other, *loss):
    step = 8
    width = D + BLOCK * len(loss)
    block = lambda w: pl.BlockSpec((step, QUARTER // 2, w), lambda i: (i, 0, 0))
    return pl.pallas_call(
        combine_kernel,
        out_shape=jax.ShapeDtypeStruct((SHARDS, QUARTER // 2, width), jnp.float32),
        grid=(SHARDS // step,),
        in_specs=[block(D), block(D)] + [pl.BlockSpec((step, BLOCK), lambda i: (i, 0))] * len(loss),
        out_specs=block(width),
        name="combine",
    )(own, other, *loss)


def send(value, axis, d, n=4):
    return lax.ppermute(value, axis, ring(d, n))


def together(*values):
    return lax.optimization_barrier(values)


def per_device(queries, passages, teacher, block_ids):
    mz, my, mx, mc = (lax.axis_index(a) for a in ("pb", "y", "x", "c"))
    me = my * 8 + mx * 2 + mc
    pos = jnp.stack([mz, my, mx, mc]).astype(jnp.int32)
    flat_ids = block_ids.reshape(-1)

    def exchange(value):
        return lax.all_to_all(value, PLANE, split_axis=0, concat_axis=0, tiled=True)

    sent0 = pack(0, flat_ids, teacher)
    recv0 = exchange(sent0)
    ids1, _ = together(flat_ids, sent0)
    sent1 = pack(1, ids1, teacher)
    s0, s1, lse, p0, p1 = score(queries, passages, teacher)
    sent1 = fill_lse(sent1, lse.reshape(LSE_ROWS, BLOCK))
    recv1 = exchange(sent1)
    ids2, _ = together(flat_ids, lse)
    sent2 = pack(2, ids2, teacher)
    sent3 = pack(3, ids2, teacher)
    sent2, _ = together(sent2, recv1[0, 0, 0])
    recv2 = exchange(sent2)
    meta = recv0[:, BLOCK, : 2 * CAP].astype(jnp.int32).reshape(-1)
    lists = tuple(make_lists(meta))
    every = recv1[:, BLOCK:, :]
    top = jnp.max(every, axis=0)
    lse = (top + jnp.log(jnp.sum(jnp.exp(every - top[None]), axis=0))).reshape(8, 2, 256)
    split = lse.transpose(1, 0, 2).reshape(2, SHARDS, 2, QUARTER)
    lse_half = [split[:, :, h].reshape(2, 4, 256).transpose(1, 0, 2) for h in range(2)]
    ds0, loss0 = rows0_call(lists, s0, lse, [recv0, recv1])
    g0 = columns_call(pos, ds0, queries)
    z0 = [g0[0], g0[1:3], g0[3:5], g0[5:7]]
    np0, nm0 = send(z0[2][0], "pb", 1), send(z0[2][1], "pb", -1)
    fp0, fm0 = send(z0[1][1], "pb", 1), send(z0[3][0], "pb", -1)

    sent3, _ = together(sent3, recv2[0, 0, 0])
    recv3 = exchange(sent3)
    scalars = (pos,) + lists
    ds1, loss_a, own_a, other_a = rows1_call(0, scalars, s1, lse_half[0], recv2, ds0, p0, p1)
    swap_a = send(other_a, "c", 1, 2)
    sp0 = send(z0[1][0] + np0, "pb", 1)
    sm0 = send(z0[3][1] + nm0, "pb", -1)
    both_a = combine(own_a, swap_a)
    both_a, _ = together(both_a, recv3[0, 0, 0])
    got_a = exchange(both_a)
    ds1, loss_b, own_b, other_b = rows1_call(1, scalars, s1, lse_half[1], recv3, ds0, p0, p1, ds1)
    swap_b = send(other_b, "c", 1, 2)
    g1 = columns_call(pos, ds1.reshape(ROWS, D), queries)
    z1 = [g1[0], g1[1:3], g1[3:5], g1[5:7]]
    np1, nm1 = send(z1[2][0], "pb", 1), send(z1[2][1], "pb", -1)
    fp1, fm1 = send(z1[1][1], "pb", 1), send(z1[3][0], "pb", -1)
    loss_ab = jnp.stack([loss_a.reshape(SHARDS, QUARTER), loss_b.reshape(SHARDS, QUARTER)], axis=1)
    loss_sum = loss0.reshape(SHARDS, 2 * QUARTER) + loss_ab.reshape(SHARDS, 2 * QUARTER)
    loss_sum = jnp.pad(loss_sum, ((0, 0), (0, BLOCK - 2 * QUARTER)))
    both_b = combine(own_b, swap_b, loss_sum)
    both_b, _ = together(both_b, got_a[0, 0, 0])
    got_b = exchange(both_b)
    sp1 = send(z1[1][0] + np1, "pb", 1)
    sm1 = send(z1[3][1] + nm1, "pb", -1)

    h = D // 8
    parts = [
        z0[0][:h] + sp0 + fm0,
        z0[0][h:] + fp0 + sm0,
        z1[0][:h] + sp1 + fm1,
        z1[0][h:] + fp1 + sm1,
    ]
    gp0, gp1 = jnp.concatenate(parts[:2]), jnp.concatenate(parts[2:])
    grad_passages = jnp.stack(
        [gp0.reshape(4, BLOCK // 2, D), gp1.reshape(4, BLOCK // 2, D)], axis=1
    ).reshape(4 * BLOCK, D)
    chips = SHARDS // 2
    sum_a = jnp.sum(got_a.reshape(chips, QUARTER, D), axis=0)
    sum_b = jnp.sum(got_b[:, :, :D].reshape(chips, QUARTER, D), axis=0)
    grad_queries = jnp.concatenate([sum_a, sum_b], axis=0)
    lse_rows = lax.dynamic_slice_in_dim(
        lse[:, 0, :].reshape(ROWS), me * (ROWS // SHARDS), ROWS // SHARDS
    )
    loss = jnp.sum(got_b[:, 0, D : D + 2 * QUARTER], axis=0) + lse_rows
    return loss, grad_queries, grad_passages


def solution(mesh):
    fine = Mesh(mesh.devices.reshape(4, 4, 4, 2), ("pb",) + PLANE)
    in_specs = (P("pb", None), P(PLANE, None), P("pb", PLANE), P("pb", PLANE))
    out_specs = (P(("pb",) + PLANE), P(("pb",) + PLANE, None), P(PLANE + ("pb",), None))
    return jax.shard_map(
        per_device, mesh=fine, in_specs=in_specs, out_specs=out_specs, check_vma=False
    )
```

```python
import functools

import jax
import jax.numpy as jnp
from jax import lax
from jax.experimental import pallas as pl
from jax.experimental.pallas import tpu as pltpu
from jax.sharding import Mesh
from jax.sharding import PartitionSpec as P


BLOCK = 128
D = 1024
ROWS = 2048
PBLOCKS_DEV = 16
SLOTS_DEV = 4
CAP = 4
SHARDS = 32
ENTRIES = 64
PACK_STEP = 8
QUARTER = 32
LSE_ROWS = 32
SUM_ROWS = 256
PLANE = ("y", "x", "c")
SCORE_SCALE = 0.0625
GRAD_SCALE = 64.0


def as_row(column):
    n = column.shape[0]
    return jnp.broadcast_to(column, (n, BLOCK)).T[0:1, :]


def as_lanes(row):
    n = row.shape[1]
    return jnp.broadcast_to(row, (BLOCK, n)).T


def pack_kernel(piece, ids_ref, teacher_ref, out_ref, slot_ref, count_ref):
    step = pl.program_id(0)

    @pl.when(step == 0)
    def _():
        for i in range(SHARDS):
            count_ref[i] = 0
        for i in range(SHARDS * CAP):
            slot_ref[i] = -1

        def place(i, carry):
            owner = ids_ref[i] // PBLOCKS_DEV
            rank = count_ref[owner]
            count_ref[owner] = rank + 1
            slot_ref[owner * CAP + jnp.minimum(rank, CAP - 1)] = i
            return carry

        lax.fori_loop(0, ENTRIES, place, 0, unroll=8)

    quarter = lax.broadcasted_iota(jnp.int32, (BLOCK, BLOCK), 1) // QUARTER
    lane = lax.broadcasted_iota(jnp.int32, (8, BLOCK), 1)
    move = lambda t, lanes: t if lanes % BLOCK == 0 else pltpu.roll(t, lanes % BLOCK, 1)
    for j in range(PACK_STEP):
        meta = jnp.zeros((8, BLOCK), jnp.float32)
        tiles = []
        for k in range(CAP):
            slot = slot_ref[(step * PACK_STEP + j) * CAP + k]
            entry = jnp.maximum(slot, 0)
            row = pl.multiple_of((entry // SLOTS_DEV) * BLOCK, BLOCK)
            col = pl.multiple_of((entry % SLOTS_DEV) * BLOCK, BLOCK)
            tiles.append(teacher_ref[pl.ds(row, BLOCK), pl.ds(col, BLOCK)])
            if piece == 0:
                where = jnp.where(slot < 0, -1, entry // SLOTS_DEV).astype(jnp.float32)
                block = (ids_ref[entry] % PBLOCKS_DEV).astype(jnp.float32)
                meta = jnp.where(lane == k, where, meta)
                meta = jnp.where(lane == CAP + k, block, meta)
        if piece < 2:
            moved = [move(t, QUARTER * (k - piece)) for k, t in enumerate(tiles)]
            low = jnp.where(quarter == 0, moved[0], moved[1])
            high = jnp.where(quarter == 2, moved[2], moved[3])
            out_ref[j, :BLOCK, :] = jnp.where(quarter < 2, low, high)
        else:
            for pair in range(CAP // 2):
                first = pltpu.roll(tiles[2 * pair], BLOCK // 2, 1)
                rows = slice(pair * BLOCK, (pair + 1) * BLOCK)
                out_ref[j, rows, :] = jnp.where(quarter < 2, first, tiles[2 * pair + 1])
        if piece == 0:
            out_ref[j, BLOCK:, :] = meta


def pack(piece, ids, teacher):
    rows = (BLOCK + 8, BLOCK, 2 * BLOCK)[piece]
    total = rows + (LSE_ROWS if piece == 1 else 0)
    return pl.pallas_call(
        functools.partial(pack_kernel, piece),
        out_shape=jax.ShapeDtypeStruct((SHARDS, total, BLOCK), jnp.float32),
        grid_spec=pltpu.PrefetchScalarGridSpec(
            num_scalar_prefetch=1,
            grid=(SHARDS // PACK_STEP,),
            in_specs=[pl.BlockSpec((ROWS, SLOTS_DEV * BLOCK), lambda s, ids: (0, 0))],
            out_specs=pl.BlockSpec((PACK_STEP, rows, BLOCK), lambda s, ids: (s, 0, 0)),
            scratch_shapes=[
                pltpu.SMEM((SHARDS * CAP,), jnp.int32),
                pltpu.SMEM((SHARDS,), jnp.int32),
            ],
        ),
        name="pack",
    )(ids, teacher)


def fill_kernel(lse_ref, sent_ref, out_ref):
    out_ref[...] = jnp.broadcast_to(lse_ref[...][None], out_ref.shape)


def fill_lse(sent, lse):
    return pl.pallas_call(
        fill_kernel,
        out_shape=jax.ShapeDtypeStruct(sent.shape, sent.dtype),
        grid=(1,),
        in_specs=[
            pl.BlockSpec((LSE_ROWS, BLOCK), lambda i: (0, 0)),
            pl.BlockSpec(memory_space=pl.ANY),
        ],
        out_specs=pl.BlockSpec((SHARDS, LSE_ROWS, BLOCK), lambda i: (0, BLOCK // LSE_ROWS, 0)),
        input_output_aliases={1: 0},
        name="fill_lse",
    )(lse, sent)


def list_kernel(meta_ref, start_ref, row_ref, block_ref, next_ref):
    blocks = ROWS // BLOCK
    for r in range(blocks):
        next_ref[r] = 0

    def count(n, carry):
        r = meta_ref[(n // CAP) * (2 * CAP) + n % CAP]

        @pl.when(r >= 0)
        def _():
            next_ref[r] = next_ref[r] + 1

        row_ref[n] = 0
        block_ref[n] = 0
        return carry

    lax.fori_loop(0, SHARDS * CAP, count, 0, unroll=4)
    total = 0
    for r in range(blocks):
        start_ref[r] = total
        size = next_ref[r]
        next_ref[r] = total
        total = total + size
    start_ref[blocks] = total

    def place(n, carry):
        src, k = n // CAP, n % CAP
        r = meta_ref[src * (2 * CAP) + k]

        @pl.when(r >= 0)
        def _():
            at = next_ref[r]
            next_ref[r] = at + 1
            row_ref[at] = n
            block_ref[at] = meta_ref[src * (2 * CAP) + CAP + k]

        return carry

    lax.fori_loop(0, SHARDS * CAP, place, 0, unroll=4)


def make_lists(meta):
    smem = pl.BlockSpec(memory_space=pltpu.SMEM)
    ints = lambda n: jax.ShapeDtypeStruct((n,), jnp.int32)
    return pl.pallas_call(
        list_kernel,
        out_shape=(ints(ROWS // BLOCK + 1), ints(SHARDS * CAP), ints(SHARDS * CAP)),
        in_specs=[smem],
        out_specs=(smem, smem, smem),
        scratch_shapes=[pltpu.SMEM((ROWS // BLOCK,), jnp.int32)],
        name="make_lists",
    )(meta)


def score_kernel(q_ref, p_ref, t_ref, s0_ref, s1_ref, lse_ref, p0_ref, p1_ref):
    half = BLOCK // 2

    @pl.when(pl.program_id(0) == 0)
    def _():
        for block in range(PBLOCKS_DEV):
            here = slice(block * half, (block + 1) * half)
            p0_ref[here, :] = p_ref[block * BLOCK : block * BLOCK + half, :]
            p1_ref[here, :] = p_ref[block * BLOCK + half : (block + 1) * BLOCK, :]

    q = q_ref[...]
    nt = (((1,), (1,)), ((), ()))
    s0 = lax.dot_general(q, p0_ref[...], nt, preferred_element_type=jnp.float32) * SCORE_SCALE
    s1 = lax.dot_general(q, p1_ref[...], nt, preferred_element_type=jnp.float32) * SCORE_SCALE
    s0_ref[...] = s0
    s1_ref[...] = s1
    top = jnp.maximum(jnp.max(s0, axis=1, keepdims=True), jnp.max(s1, axis=1, keepdims=True))
    total = jnp.sum(jnp.exp(s0 - top), axis=1, keepdims=True) + jnp.sum(
        jnp.exp(s1 - top), axis=1, keepdims=True
    )
    lse_ref[0, 0:1, :] = as_row(top + jnp.log(total))
    t = t_ref[...]
    ttop = jnp.max(t, axis=1, keepdims=True)
    ttotal = jnp.sum(jnp.exp(t - ttop), axis=1, keepdims=True)
    lse_ref[0, 1:2, :] = as_row(ttop + jnp.log(ttotal))


def score(queries, passages, teacher):
    rb = 256
    block = pl.BlockSpec((rb, D), lambda i: (i, 0))
    whole = pl.BlockSpec((D, D), lambda i: (0, 0))
    scores = jax.ShapeDtypeStruct((ROWS, D), jnp.float32)
    part = jax.ShapeDtypeStruct((D, D), jnp.bfloat16)
    return pl.pallas_call(
        score_kernel,
        out_shape=(
            scores,
            scores,
            jax.ShapeDtypeStruct((ROWS // rb, 2, rb), jnp.float32),
            part,
            part,
        ),
        grid=(ROWS // rb,),
        in_specs=[
            block,
            pl.BlockSpec((ROWS, D), lambda i: (0, 0)),
            pl.BlockSpec((rb, SLOTS_DEV * BLOCK), lambda i: (i, 0)),
        ],
        out_specs=(block, block, pl.BlockSpec((1, 2, rb), lambda i: (i, 0, 0)), whole, whole),
        name="score",
    )(queries, passages, teacher)


def subtract_tiles(
    fetch, sub_rows, first, end, block_ref, s_cols, lt_ref, rows, w_ref, acc_ref
):
    lane = lax.broadcasted_iota(jnp.int32, (sub_rows, BLOCK), 1)
    side = lane // (BLOCK // 2)

    def body(n, carry):
        parts = []
        for at in (first + 2 * n, first + 2 * n + 1):
            here = jnp.minimum(at, end - 1)
            block = block_ref[here]
            x = fetch(here, block)
            keep = (side == block % 2) & (at < end)
            centred = x - lt_ref[rows, :]
            prob = jnp.where(keep, jnp.exp(centred), 0.0)
            cols = pl.ds(pl.multiple_of((block // 2) * BLOCK, BLOCK), BLOCK)
            term = jnp.where(keep, prob * (centred - s_cols(cols)), 0.0)
            parts.append((prob, cols, term))
        acc_ref[rows, :] = acc_ref[rows, :] + (parts[0][2] + parts[1][2])
        for prob, cols, _ in parts:
            w_ref[rows, cols] = w_ref[rows, cols] - prob
        return carry

    lax.fori_loop(0, (end - first + 1) // 2, body, 0)


def rows0_kernel(
    start_ref, row_ref, block_ref, s_ref, lse_ref, recv0_ref, recv1_ref,
    ds_ref, loss_ref, w_ref, lt_ref, acc_ref,
):
    step = pl.program_id(0)
    rb = 256
    half = BLOCK // 2
    ls = as_lanes(lse_ref[0, 0:1, :])
    lt_ref[...] = as_lanes(lse_ref[0, 1:2, :])
    for j in range(D // BLOCK):
        cols = slice(j * BLOCK, (j + 1) * BLOCK)
        w_ref[:, cols] = jnp.exp(s_ref[:, cols] - ls)
    acc_ref[...] = jnp.zeros_like(acc_ref)
    early = lax.broadcasted_iota(jnp.int32, (BLOCK, BLOCK), 1) % half < QUARTER

    def fetch(n, block):
        slot = row_ref[n]
        src, k = slot // CAP, slot % CAP
        shift = (block % 2) * half
        at = pl.multiple_of(src * (BLOCK + 8), 8)
        x = recv0_ref[pl.ds(at, BLOCK), :]
        x = pltpu.roll(x, (shift - k * QUARTER + BLOCK) % BLOCK, 1)
        at = pl.multiple_of(src * (BLOCK + LSE_ROWS), 8)
        y = recv1_ref[pl.ds(at, BLOCK), :]
        y = pltpu.roll(y, (shift + QUARTER - k * QUARTER + BLOCK) % BLOCK, 1)
        return jnp.where(early, x, y)

    for sub in range(rb // BLOCK):
        rows = slice(sub * BLOCK, (sub + 1) * BLOCK)
        r = step * (rb // BLOCK) + sub
        subtract_tiles(
            fetch, BLOCK, start_ref[r], start_ref[r + 1], block_ref,
            lambda cols: s_ref[rows, cols], lt_ref, rows, w_ref, acc_ref,
        )
    ds_ref[...] = (w_ref[...] * GRAD_SCALE).astype(jnp.bfloat16)
    loss_ref[0] = as_row(jnp.sum(acc_ref[...], axis=1, keepdims=True))


ROW_SCRATCH = [
    pltpu.VMEM((256, D), jnp.float32),
    pltpu.VMEM((256, BLOCK), jnp.float32),
    pltpu.VMEM((256, BLOCK), jnp.float32),
]


def full_spec(*shape):
    return pl.BlockSpec(shape, lambda i, *_: (0,) * len(shape))


def rows0_call(lists, scores, lse, recvs):
    rb = 256
    recvs = [r.reshape(-1, BLOCK) for r in recvs]
    block = pl.BlockSpec((rb, D), lambda i, *_: (i, 0))
    return pl.pallas_call(
        rows0_kernel,
        out_shape=(
            jax.ShapeDtypeStruct((ROWS, D), jnp.bfloat16),
            jax.ShapeDtypeStruct((ROWS // rb, 1, rb), jnp.float32),
        ),
        grid_spec=pltpu.PrefetchScalarGridSpec(
            num_scalar_prefetch=len(lists),
            grid=(ROWS // rb,),
            in_specs=[block, pl.BlockSpec((1, 2, rb), lambda i, *_: (i, 0, 0))]
            + [full_spec(*r.shape) for r in recvs],
            out_specs=(block, pl.BlockSpec((1, 1, rb), lambda i, *_: (i, 0, 0))),
            scratch_shapes=ROW_SCRATCH,
        ),
        name="rows0",
    )(*lists, scores, lse, *recvs)


def rows1_kernel(
    pos_ref, start_ref, row_ref, block_ref, s_ref, lse_ref, recv_ref, add_ref, p_ref,
    ds_ref, loss_ref, own_ref, other_ref, w_ref, lt_ref, acc_ref, past_ref,
):
    step = pl.program_id(0)
    steps = pl.num_programs(0) - 1
    rb = 256
    half = BLOCK // 2
    part = add_ref[...] + jnp.dot(past_ref[...], p_ref[...], preferred_element_type=jnp.float32)
    ls = as_lanes(lse_ref[0, 0:1, :])
    lt_ref[...] = as_lanes(lse_ref[0, 1:2, :])
    for j in range(D // BLOCK):
        cols = slice(j * BLOCK, (j + 1) * BLOCK)
        w_ref[:, cols] = jnp.exp(s_ref[:, cols] - ls)
    acc_ref[...] = jnp.zeros_like(acc_ref)
    part = part.reshape(rb // (2 * QUARTER), 2, QUARTER, D)
    first = pos_ref[3] == 0
    own_ref[...] = jnp.where(first, part[:, 0], part[:, 1])
    other_ref[...] = jnp.where(first, part[:, 1], part[:, 0])

    def fetch(n, block):
        slot = row_ref[n]
        at = pl.multiple_of((slot // 2) * BLOCK, BLOCK)
        return pltpu.roll(recv_ref[pl.ds(at, BLOCK), :], ((block + slot) % 2) * half, 1)

    @pl.when(step < steps)
    def _():
        for sub in range(rb // BLOCK):
            rows = slice(sub * BLOCK, (sub + 1) * BLOCK)
            r = step * (rb // BLOCK) + sub
            subtract_tiles(
                fetch, BLOCK, start_ref[r], start_ref[r + 1], block_ref,
                lambda cols: s_ref[rows, cols], lt_ref, rows, w_ref, acc_ref,
            )
        ds = (w_ref[...] * GRAD_SCALE).astype(jnp.bfloat16)
        ds_ref[...] = ds
        past_ref[...] = ds
        loss_ref[0] = as_row(jnp.sum(acc_ref[...], axis=1, keepdims=True))


def rows1_call(scalars, scores, lse, recv, add, passages):
    rb = 256
    steps = ROWS // rb
    recv = recv.reshape(-1, BLOCK)
    now = lambda i, *_: (jnp.minimum(i, steps - 1), 0)
    now3 = lambda i, *_: (jnp.minimum(i, steps - 1), 0, 0)
    past = lambda i, *_: (jnp.maximum(i - 1, 0), 0)
    past3 = lambda i, *_: (jnp.maximum(i - 1, 0), 0, 0)
    out = pl.BlockSpec((rb // (2 * QUARTER), QUARTER, D), past3)
    out_type = jax.ShapeDtypeStruct((SHARDS, QUARTER, D), jnp.float32)
    return pl.pallas_call(
        rows1_kernel,
        out_shape=(
            jax.ShapeDtypeStruct((ROWS, D), jnp.bfloat16),
            jax.ShapeDtypeStruct((steps, 1, rb), jnp.float32),
            out_type,
            out_type,
        ),
        grid_spec=pltpu.PrefetchScalarGridSpec(
            num_scalar_prefetch=len(scalars),
            grid=(steps + 1,),
            in_specs=[
                pl.BlockSpec((rb, D), now),
                pl.BlockSpec((1, 2, rb), now3),
                full_spec(*recv.shape),
                pl.BlockSpec((rb, D), past),
                full_spec(D, D),
            ],
            out_specs=(pl.BlockSpec((rb, D), now), pl.BlockSpec((1, 1, rb), now3), out, out),
            scratch_shapes=ROW_SCRATCH + [pltpu.VMEM((rb, D), jnp.bfloat16)],
        ),
        name="rows1",
    )(*scalars, scores, lse, recv, add, passages)


def query_kernel(ds_ref, p_ref, out_ref):
    out_ref[...] = jnp.dot(ds_ref[...], p_ref[...], preferred_element_type=jnp.float32)


def query_call(ds, passages):
    rb = 512
    return pl.pallas_call(
        query_kernel,
        out_shape=jax.ShapeDtypeStruct((ROWS, D), jnp.float32),
        grid=(ROWS // rb,),
        in_specs=[pl.BlockSpec((rb, D), lambda i: (i, 0)), full_spec(D, D)],
        out_specs=pl.BlockSpec((rb, D), lambda i: (i, 0)),
        name="query",
    )(ds, passages)


def columns_kernel(pos_ref, ds_ref, q_ref, *outs):
    groups = {0: outs[:1], 1: outs[1:3], 2: outs[3:5], 3: outs[5:7]}
    for d in (2, 1, 3, 0):
        off = pl.multiple_of(((pos_ref[0] + d) % 4) * (D // 4), D // 4)
        part = lax.dot_general(
            ds_ref[:, pl.ds(off, D // 4)],
            q_ref[...],
            (((0,), (0,)), ((), ())),
            preferred_element_type=jnp.float32,
        )
        size = D // 4 // len(groups[d])
        for i, out in enumerate(groups[d]):
            out[...] = part[size * i : size * (i + 1)]


def columns_call(pos, ds, queries):
    full = lambda *shape: pl.BlockSpec(shape, lambda i, *_: (0,) * len(shape))
    sizes = (D // 4,) + (D // 8,) * 6
    return pl.pallas_call(
        columns_kernel,
        out_shape=tuple(jax.ShapeDtypeStruct((n, D), jnp.float32) for n in sizes),
        grid_spec=pltpu.PrefetchScalarGridSpec(
            num_scalar_prefetch=1,
            grid=(1,),
            in_specs=[full(ROWS, D), full(ROWS, D)],
            out_specs=tuple(full(n, D) for n in sizes),
        ),
        name="columns",
    )(pos, ds, queries)


def ring(d, n=4):
    return [(i, (i + d) % n) for i in range(n)]


def combine_kernel(own_ref, other_ref, loss_ref, out_ref):
    for j in range(D // BLOCK):
        cols = slice(j * BLOCK, (j + 1) * BLOCK)
        rows = slice(j * QUARTER, (j + 1) * QUARTER)
        out_ref[:, rows, :] = own_ref[:, :, cols] + other_ref[:, :, cols]
    shape = (out_ref.shape[0], 8, BLOCK)
    out_ref[:, SUM_ROWS:, :] = jnp.broadcast_to(loss_ref[...][:, None, :], shape)


def combine(own, other, loss):
    step = 8
    block = pl.BlockSpec((step, QUARTER, D), lambda i: (i, 0, 0))
    return pl.pallas_call(
        combine_kernel,
        out_shape=jax.ShapeDtypeStruct((SHARDS, SUM_ROWS + 8, BLOCK), jnp.float32),
        grid=(SHARDS // step,),
        in_specs=[block, block, pl.BlockSpec((step, BLOCK), lambda i: (i, 0))],
        out_specs=pl.BlockSpec((step, SUM_ROWS + 8, BLOCK), lambda i: (i, 0, 0)),
        name="combine",
    )(own, other, loss)


def total_kernel(got_ref, lse_ref, grad_ref, loss_ref):
    step = pl.program_id(0)
    loss = jnp.sum(got_ref[:, SUM_ROWS:, :], axis=0)

    @pl.when(step == 0)
    def _():
        loss_ref[...] = lse_ref[...] + loss

    @pl.when(step > 0)
    def _():
        loss_ref[...] = loss_ref[...] + loss

    for core in range(2):
        for j in range(D // BLOCK):
            rows = slice(j * QUARTER, (j + 1) * QUARTER)
            to = (slice(core * QUARTER, (core + 1) * QUARTER), slice(j * BLOCK, (j + 1) * BLOCK))
            part = got_ref[core, rows, :]
            for chip in range(1, got_ref.shape[0] // 2):
                part = part + got_ref[2 * chip + core, rows, :]

            @pl.when(step == 0)
            def _(part=part, to=to):
                grad_ref[to] = part

            @pl.when(step > 0)
            def _(part=part, to=to):
                grad_ref[to] = grad_ref[to] + part


def total(got, lse_rows):
    step = 8
    return pl.pallas_call(
        total_kernel,
        out_shape=(
            jax.ShapeDtypeStruct((2 * QUARTER, D), jnp.float32),
            jax.ShapeDtypeStruct((8, BLOCK), jnp.float32),
        ),
        grid=(SHARDS // step,),
        in_specs=[
            pl.BlockSpec((step, SUM_ROWS + 8, BLOCK), lambda i: (i, 0, 0)),
            full_spec(8, BLOCK),
        ],
        out_specs=(full_spec(2 * QUARTER, D), full_spec(8, BLOCK)),
        name="total",
    )(got, lse_rows)


def send(value, axis, d, n=4):
    return lax.ppermute(value, axis, ring(d, n))


def together(*values):
    return lax.optimization_barrier(values)


def per_device(queries, passages, teacher, block_ids):
    mz, my, mx, mc = (lax.axis_index(a) for a in ("pb", "y", "x", "c"))
    me = my * 8 + mx * 2 + mc
    pos = jnp.stack([mz, my, mx, mc]).astype(jnp.int32)
    flat_ids = block_ids.reshape(-1)

    def exchange(value):
        return lax.all_to_all(value, PLANE, split_axis=0, concat_axis=0, tiled=True)

    sent0 = pack(0, flat_ids, teacher)
    recv0 = exchange(sent0)
    ids1, _ = together(flat_ids, sent0)
    sent1 = pack(1, ids1, teacher)
    s0, s1, lse, p0, p1 = score(queries, passages, teacher)
    sent1 = fill_lse(sent1, lse.reshape(LSE_ROWS, BLOCK))
    recv1 = exchange(sent1)
    ids2, _ = together(flat_ids, lse)
    sent2 = pack(2, ids2, teacher)
    sent2, _ = together(sent2, recv1[0, 0, 0])
    recv2 = exchange(sent2)
    meta = recv0[:, BLOCK, : 2 * CAP].astype(jnp.int32).reshape(-1)
    lists = tuple(make_lists(meta))
    every = recv1[:, BLOCK:, :]
    top = jnp.max(every, axis=0)
    lse = (top + jnp.log(jnp.sum(jnp.exp(every - top[None]), axis=0))).reshape(8, 2, 256)
    ds0, loss0 = rows0_call(lists, s0, lse, [recv0, recv1])
    g0 = columns_call(pos, ds0, queries)
    z0 = [g0[0], g0[1:3], g0[3:5], g0[5:7]]
    np0, nm0 = send(z0[2][0], "pb", 1), send(z0[2][1], "pb", -1)
    fp0, fm0 = send(z0[1][1], "pb", 1), send(z0[3][0], "pb", -1)
    q0 = query_call(ds0, p0)
    sp0 = send(z0[1][0] + np0, "pb", 1)
    sm0 = send(z0[3][1] + nm0, "pb", -1)

    ds1, loss1, own, other = rows1_call((pos,) + lists, s1, lse, recv2, q0, p1)
    swapped = send(other, "c", 1, 2)
    loss_sum = (loss0 + loss1).reshape(SHARDS, 2 * QUARTER)
    loss_sum = jnp.pad(loss_sum, ((0, 0), (0, BLOCK - 2 * QUARTER)))
    both = combine(own, swapped, loss_sum)
    got = exchange(both)
    g1 = columns_call(pos, ds1, queries)
    z1 = [g1[0], g1[1:3], g1[3:5], g1[5:7]]
    np1, nm1 = send(z1[2][0], "pb", 1), send(z1[2][1], "pb", -1)
    fp1, fm1 = send(z1[1][1], "pb", 1), send(z1[3][0], "pb", -1)
    sp1 = send(z1[1][0] + np1, "pb", 1)
    sm1 = send(z1[3][1] + nm1, "pb", -1)

    h = D // 8
    parts = [
        z0[0][:h] + sp0 + fm0,
        z0[0][h:] + fp0 + sm0,
        z1[0][:h] + sp1 + fm1,
        z1[0][h:] + fp1 + sm1,
    ]
    gp0, gp1 = jnp.concatenate(parts[:2]), jnp.concatenate(parts[2:])
    grad_passages = jnp.stack(
        [gp0.reshape(4, BLOCK // 2, D), gp1.reshape(4, BLOCK // 2, D)], axis=1
    ).reshape(4 * BLOCK, D)
    lse_rows = lax.dynamic_slice_in_dim(
        lse[:, 0, :].reshape(ROWS), me * (ROWS // SHARDS), ROWS // SHARDS
    )
    lse_rows = jnp.broadcast_to(jnp.pad(lse_rows, (0, BLOCK - 2 * QUARTER)), (8, BLOCK))
    grad_queries, loss = total(got, lse_rows)
    return loss[0, : 2 * QUARTER], grad_queries, grad_passages


def solution(mesh):
    fine = Mesh(mesh.devices.reshape(4, 4, 4, 2), ("pb",) + PLANE)
    in_specs = (P("pb", None), P(PLANE, None), P("pb", PLANE), P("pb", PLANE))
    out_specs = (P(("pb",) + PLANE), P(("pb",) + PLANE, None), P(PLANE + ("pb",), None))
    return jax.shard_map(
        per_device, mesh=fine, in_specs=in_specs, out_specs=out_specs, check_vma=False
    )
```

```python
import functools

import jax
import jax.numpy as jnp
from jax import lax
from jax.experimental import pallas as pl
from jax.experimental.pallas import tpu as pltpu
from jax.sharding import Mesh
from jax.sharding import PartitionSpec as P


BLOCK = 128
D = 1024
ROWS = 2048
PBLOCKS_DEV = 16
SLOTS_DEV = 4
CAP = 4
SHARDS = 32
ENTRIES = 64
PACK_STEP = 8
QUARTER = 32
LSE_ROWS = 32
SUM_ROWS = 256
PLANE = ("y", "x", "c")
SCORE_SCALE = 0.0625
GRAD_SCALE = 64.0


def as_row(column):
    n = column.shape[0]
    return jnp.broadcast_to(column, (n, BLOCK)).T[0:1, :]


def as_lanes(row):
    n = row.shape[1]
    return jnp.broadcast_to(row, (BLOCK, n)).T


def pack_kernel(piece, ids_ref, teacher_ref, out_ref, slot_ref, count_ref):
    step = pl.program_id(0)

    @pl.when(step == 0)
    def _():
        for i in range(SHARDS):
            count_ref[i] = 0
        for i in range(SHARDS * CAP):
            slot_ref[i] = -1

        def place(i, carry):
            owner = ids_ref[i // SLOTS_DEV, i % SLOTS_DEV] // PBLOCKS_DEV
            rank = count_ref[owner]
            count_ref[owner] = rank + 1
            slot_ref[owner * CAP + jnp.minimum(rank, CAP - 1)] = i
            return carry

        lax.fori_loop(0, ENTRIES, place, 0, unroll=8)

    quarter = lax.broadcasted_iota(jnp.int32, (BLOCK, BLOCK), 1) // QUARTER
    lane = lax.broadcasted_iota(jnp.int32, (8, BLOCK), 1)
    move = lambda t, lanes: t if lanes % BLOCK == 0 else pltpu.roll(t, lanes % BLOCK, 1)
    for j in range(PACK_STEP):
        meta = jnp.zeros((8, BLOCK), jnp.float32)
        tiles = []
        for k in range(CAP):
            slot = slot_ref[(step * PACK_STEP + j) * CAP + k]
            entry = jnp.maximum(slot, 0)
            row = pl.multiple_of((entry // SLOTS_DEV) * BLOCK, BLOCK)
            col = pl.multiple_of((entry % SLOTS_DEV) * BLOCK, BLOCK)
            tiles.append(teacher_ref[pl.ds(row, BLOCK), pl.ds(col, BLOCK)])
            if piece == 0:
                where = jnp.where(slot < 0, -1, entry // SLOTS_DEV).astype(jnp.float32)
                block = ids_ref[entry // SLOTS_DEV, entry % SLOTS_DEV] % PBLOCKS_DEV
                block = block.astype(jnp.float32)
                meta = jnp.where(lane == k, where, meta)
                meta = jnp.where(lane == CAP + k, block, meta)
        if piece < 2:
            moved = [move(t, QUARTER * (k - piece)) for k, t in enumerate(tiles)]
            low = jnp.where(quarter == 0, moved[0], moved[1])
            high = jnp.where(quarter == 2, moved[2], moved[3])
            out_ref[j, :BLOCK, :] = jnp.where(quarter < 2, low, high)
        else:
            for pair in range(CAP // 2):
                first = pltpu.roll(tiles[2 * pair], BLOCK // 2, 1)
                rows = slice(pair * BLOCK, (pair + 1) * BLOCK)
                out_ref[j, rows, :] = jnp.where(quarter < 2, first, tiles[2 * pair + 1])
        if piece == 0:
            out_ref[j, BLOCK:, :] = meta


def pack(piece, ids, teacher):
    rows = (BLOCK + 8, BLOCK, 2 * BLOCK)[piece]
    total = rows + (LSE_ROWS if piece == 1 else 0)
    return pl.pallas_call(
        functools.partial(pack_kernel, piece),
        out_shape=jax.ShapeDtypeStruct((SHARDS, total, BLOCK), jnp.float32),
        grid_spec=pltpu.PrefetchScalarGridSpec(
            num_scalar_prefetch=1,
            grid=(SHARDS // PACK_STEP,),
            in_specs=[pl.BlockSpec((ROWS, SLOTS_DEV * BLOCK), lambda s, ids: (0, 0))],
            out_specs=pl.BlockSpec((PACK_STEP, rows, BLOCK), lambda s, ids: (s, 0, 0)),
            scratch_shapes=[
                pltpu.SMEM((SHARDS * CAP,), jnp.int32),
                pltpu.SMEM((SHARDS,), jnp.int32),
            ],
        ),
        name="pack",
    )(ids, teacher)


def fill_kernel(lse_ref, sent_ref, out_ref):
    out_ref[...] = jnp.broadcast_to(lse_ref[...][None], out_ref.shape)


def fill_lse(sent, lse):
    return pl.pallas_call(
        fill_kernel,
        out_shape=jax.ShapeDtypeStruct(sent.shape, sent.dtype),
        grid=(1,),
        in_specs=[
            pl.BlockSpec((LSE_ROWS, BLOCK), lambda i: (0, 0)),
            pl.BlockSpec(memory_space=pl.ANY),
        ],
        out_specs=pl.BlockSpec((SHARDS, LSE_ROWS, BLOCK), lambda i: (0, BLOCK // LSE_ROWS, 0)),
        input_output_aliases={1: 0},
        name="fill_lse",
    )(lse, sent)


def list_kernel(meta_ref, start_ref, row_ref, block_ref, next_ref):
    blocks = ROWS // BLOCK
    for r in range(blocks):
        next_ref[r] = 0

    def count(n, carry):
        r = meta_ref[(n // CAP) * (2 * CAP) + n % CAP]

        @pl.when(r >= 0)
        def _():
            next_ref[r] = next_ref[r] + 1

        row_ref[n] = 0
        block_ref[n] = 0
        return carry

    lax.fori_loop(0, SHARDS * CAP, count, 0, unroll=4)
    total = 0
    for r in range(blocks):
        start_ref[r] = total
        size = next_ref[r]
        next_ref[r] = total
        total = total + size
    start_ref[blocks] = total

    def place(n, carry):
        src, k = n // CAP, n % CAP
        r = meta_ref[src * (2 * CAP) + k]

        @pl.when(r >= 0)
        def _():
            at = next_ref[r]
            next_ref[r] = at + 1
            row_ref[at] = n
            block_ref[at] = meta_ref[src * (2 * CAP) + CAP + k]

        return carry

    lax.fori_loop(0, SHARDS * CAP, place, 0, unroll=4)


def make_lists(meta):
    smem = pl.BlockSpec(memory_space=pltpu.SMEM)
    ints = lambda n: jax.ShapeDtypeStruct((n,), jnp.int32)
    return pl.pallas_call(
        list_kernel,
        out_shape=(ints(ROWS // BLOCK + 1), ints(SHARDS * CAP), ints(SHARDS * CAP)),
        in_specs=[smem],
        out_specs=(smem, smem, smem),
        scratch_shapes=[pltpu.SMEM((ROWS // BLOCK,), jnp.int32)],
        name="make_lists",
    )(meta)


def score_kernel(q_ref, p_ref, t_ref, s0_ref, s1_ref, lse_ref, p0_ref, p1_ref):
    half = BLOCK // 2

    @pl.when(pl.program_id(0) == 0)
    def _():
        for block in range(PBLOCKS_DEV):
            here = slice(block * half, (block + 1) * half)
            p0_ref[here, :] = p_ref[block * BLOCK : block * BLOCK + half, :]
            p1_ref[here, :] = p_ref[block * BLOCK + half : (block + 1) * BLOCK, :]

    q = q_ref[...]
    nt = (((1,), (1,)), ((), ()))
    s0 = lax.dot_general(q, p0_ref[...], nt, preferred_element_type=jnp.float32) * SCORE_SCALE
    s1 = lax.dot_general(q, p1_ref[...], nt, preferred_element_type=jnp.float32) * SCORE_SCALE
    s0_ref[...] = s0
    s1_ref[...] = s1
    top = jnp.maximum(jnp.max(s0, axis=1, keepdims=True), jnp.max(s1, axis=1, keepdims=True))
    total = jnp.sum(jnp.exp(s0 - top), axis=1, keepdims=True) + jnp.sum(
        jnp.exp(s1 - top), axis=1, keepdims=True
    )
    lse_ref[0, 0:1, :] = as_row(top + jnp.log(total))
    t = t_ref[...]
    ttop = jnp.max(t, axis=1, keepdims=True)
    ttotal = jnp.sum(jnp.exp(t - ttop), axis=1, keepdims=True)
    lse_ref[0, 1:2, :] = as_row(ttop + jnp.log(ttotal))


def score(queries, passages, teacher):
    rb = 256
    block = pl.BlockSpec((rb, D), lambda i: (i, 0))
    whole = pl.BlockSpec((D, D), lambda i: (0, 0))
    scores = jax.ShapeDtypeStruct((ROWS, D), jnp.float32)
    part = jax.ShapeDtypeStruct((D, D), jnp.bfloat16)
    return pl.pallas_call(
        score_kernel,
        out_shape=(
            scores,
            scores,
            jax.ShapeDtypeStruct((ROWS // rb, 2, rb), jnp.float32),
            part,
            part,
        ),
        grid=(ROWS // rb,),
        in_specs=[
            block,
            pl.BlockSpec((ROWS, D), lambda i: (0, 0)),
            pl.BlockSpec((rb, SLOTS_DEV * BLOCK), lambda i: (i, 0)),
        ],
        out_specs=(block, block, pl.BlockSpec((1, 2, rb), lambda i: (i, 0, 0)), whole, whole),
        name="score",
    )(queries, passages, teacher)


def subtract_tiles(
    fetch, sub_rows, first, end, block_ref, s_cols, lt_ref, rows, w_ref, acc_ref
):
    lane = lax.broadcasted_iota(jnp.int32, (sub_rows, BLOCK), 1)
    side = lane // (BLOCK // 2)

    def body(n, carry):
        parts = []
        for at in (first + 2 * n, first + 2 * n + 1):
            here = jnp.minimum(at, end - 1)
            block = block_ref[here]
            x = fetch(here, block)
            keep = (side == block % 2) & (at < end)
            centred = x - lt_ref[rows, :]
            prob = jnp.where(keep, jnp.exp(centred), 0.0)
            cols = pl.ds(pl.multiple_of((block // 2) * BLOCK, BLOCK), BLOCK)
            term = jnp.where(keep, prob * (centred - s_cols(cols)), 0.0)
            parts.append((prob, cols, term))
        acc_ref[rows, :] = acc_ref[rows, :] + (parts[0][2] + parts[1][2])
        for prob, cols, _ in parts:
            w_ref[rows, cols] = w_ref[rows, cols] - prob
        return carry

    lax.fori_loop(0, (end - first + 1) // 2, body, 0)


def rows0_kernel(
    start_ref, row_ref, block_ref, s_ref, lse_ref, recv0_ref, recv1_ref,
    ds_ref, loss_ref, w_ref, lt_ref, acc_ref,
):
    step = pl.program_id(0)
    rb = 256
    half = BLOCK // 2
    ls = as_lanes(lse_ref[0, 0:1, :])
    lt_ref[...] = as_lanes(lse_ref[0, 1:2, :])
    for j in range(D // BLOCK):
        cols = slice(j * BLOCK, (j + 1) * BLOCK)
        w_ref[:, cols] = jnp.exp(s_ref[:, cols] - ls)
    acc_ref[...] = jnp.zeros_like(acc_ref)
    early = lax.broadcasted_iota(jnp.int32, (BLOCK, BLOCK), 1) % half < QUARTER

    def fetch(n, block):
        slot = row_ref[n]
        src, k = slot // CAP, slot % CAP
        shift = (block % 2) * half
        at = pl.multiple_of(src * (BLOCK + 8), 8)
        x = recv0_ref[pl.ds(at, BLOCK), :]
        x = pltpu.roll(x, (shift - k * QUARTER + BLOCK) % BLOCK, 1)
        at = pl.multiple_of(src * (BLOCK + LSE_ROWS), 8)
        y = recv1_ref[pl.ds(at, BLOCK), :]
        y = pltpu.roll(y, (shift + QUARTER - k * QUARTER + BLOCK) % BLOCK, 1)
        return jnp.where(early, x, y)

    for sub in range(rb // BLOCK):
        rows = slice(sub * BLOCK, (sub + 1) * BLOCK)
        r = step * (rb // BLOCK) + sub
        subtract_tiles(
            fetch, BLOCK, start_ref[r], start_ref[r + 1], block_ref,
            lambda cols: s_ref[rows, cols], lt_ref, rows, w_ref, acc_ref,
        )
    ds_ref[...] = (w_ref[...] * GRAD_SCALE).astype(jnp.bfloat16)
    loss_ref[0] = as_row(jnp.sum(acc_ref[...], axis=1, keepdims=True))


ROW_SCRATCH = [
    pltpu.VMEM((256, D), jnp.float32),
    pltpu.VMEM((256, BLOCK), jnp.float32),
    pltpu.VMEM((256, BLOCK), jnp.float32),
]


def full_spec(*shape):
    return pl.BlockSpec(shape, lambda i, *_: (0,) * len(shape))


def rows0_call(lists, scores, lse, recvs):
    rb = 256
    recvs = [r.reshape(-1, BLOCK) for r in recvs]
    block = pl.BlockSpec((rb, D), lambda i, *_: (i, 0))
    return pl.pallas_call(
        rows0_kernel,
        out_shape=(
            jax.ShapeDtypeStruct((ROWS, D), jnp.bfloat16),
            jax.ShapeDtypeStruct((ROWS // rb, 1, rb), jnp.float32),
        ),
        grid_spec=pltpu.PrefetchScalarGridSpec(
            num_scalar_prefetch=len(lists),
            grid=(ROWS // rb,),
            in_specs=[block, pl.BlockSpec((1, 2, rb), lambda i, *_: (i, 0, 0))]
            + [full_spec(*r.shape) for r in recvs],
            out_specs=(block, pl.BlockSpec((1, 1, rb), lambda i, *_: (i, 0, 0))),
            scratch_shapes=ROW_SCRATCH,
        ),
        name="rows0",
    )(*lists, scores, lse, *recvs)


def rows1_kernel(
    side_ref, start_ref, row_ref, block_ref, s_ref, lse_ref, recv_ref, add_ref, p_ref, *refs
):
    ds_ref, loss_ref, grad_ref, w_ref, lt_ref, acc_ref, past_ref = refs[-7:]
    step = pl.program_id(0)
    steps = pl.num_programs(0) - 1
    rb = 256
    half = BLOCK // 2
    part = add_ref[...].reshape(rb, D) + jnp.dot(
        past_ref[...], p_ref[...], preferred_element_type=jnp.float32
    )
    ls = as_lanes(lse_ref[0, 0, 0:1, :])
    lt_ref[...] = as_lanes(lse_ref[0, 0, 1:2, :])
    for j in range(D // BLOCK):
        cols = slice(j * BLOCK, (j + 1) * BLOCK)
        w_ref[:, cols] = jnp.exp(s_ref[:, 0, :, cols].reshape(rb, BLOCK) - ls)
    acc_ref[...] = jnp.zeros_like(acc_ref)
    grad_ref[...] = part.reshape(grad_ref.shape)

    def fetch(n, block):
        slot = row_ref[n]
        x = recv_ref[pl.ds((slot // 2) * 2, 2), 0, :, :].reshape(half, BLOCK)
        return pltpu.roll(x, ((block + slot) % 2) * half, 1)

    @pl.when(step < steps)
    def _():
        for sub in range(rb // half):
            rows = slice(sub * half, (sub + 1) * half)
            r = step * (rb // half) + sub
            subtract_tiles(
                fetch, half, start_ref[r], start_ref[r + 1], block_ref,
                lambda cols: s_ref[2 * sub : 2 * sub + 2, 0, :, cols].reshape(half, BLOCK),
                lt_ref, rows, w_ref, acc_ref,
            )
        ds = (w_ref[...] * GRAD_SCALE).astype(jnp.bfloat16)
        ds_ref[...] = ds.reshape(ds_ref.shape)
        past_ref[...] = ds
        loss_ref[0] = as_row(jnp.sum(acc_ref[...], axis=1, keepdims=True))


def rows1_call(side, lists, scores, lse, recv, add, passages, ds=None):
    rb = 256
    steps = ROWS // 2 // rb
    view = (SHARDS, 2, QUARTER, D)
    scalars = (side,) + lists
    now = lambda i: jnp.minimum(i, steps - 1)
    past = lambda i: jnp.maximum(i - 1, 0)
    group = (rb // QUARTER, 1, QUARTER, D)
    again = [] if ds is None else [ds]
    return pl.pallas_call(
        rows1_kernel,
        out_shape=(
            jax.ShapeDtypeStruct(view, jnp.bfloat16),
            jax.ShapeDtypeStruct((steps, 1, rb), jnp.float32),
            jax.ShapeDtypeStruct((SHARDS, QUARTER, D), jnp.float32),
        ),
        grid_spec=pltpu.PrefetchScalarGridSpec(
            num_scalar_prefetch=len(scalars),
            grid=(steps + 1,),
            in_specs=[
                pl.BlockSpec(group, lambda i, h, *_: (now(i), h[0], 0, 0)),
                pl.BlockSpec((1, 1, 2, rb), lambda i, h, *_: (h[0], now(i), 0, 0)),
                pl.BlockSpec((4 * SHARDS, 1, QUARTER, BLOCK), lambda i, h, *_: (0, h[0], 0, 0)),
                pl.BlockSpec(group, lambda i, h, *_: (past(i), h[0], 0, 0)),
                full_spec(D, D),
            ]
            + [pl.BlockSpec(memory_space=pl.ANY)] * len(again),
            out_specs=(
                pl.BlockSpec(group, lambda i, h, *_: (now(i), h[0], 0, 0)),
                pl.BlockSpec((1, 1, rb), lambda i, *_: (now(i), 0, 0)),
                pl.BlockSpec((rb // QUARTER, QUARTER, D), lambda i, *_: (past(i), 0, 0)),
            ),
            scratch_shapes=ROW_SCRATCH + [pltpu.VMEM((rb, D), jnp.bfloat16)],
        ),
        input_output_aliases={len(scalars) + 5: 0} if again else {},
        name="rows1",
    )(
        *scalars, scores.reshape(view), lse, recv.reshape(4 * SHARDS, 2, QUARTER, BLOCK),
        add.reshape(view), passages, *again,
    )


def query_kernel(ds_ref, p_ref, out_ref):
    out_ref[...] = jnp.dot(ds_ref[...], p_ref[...], preferred_element_type=jnp.float32)


def query_call(ds, passages):
    rb = 512
    return pl.pallas_call(
        query_kernel,
        out_shape=jax.ShapeDtypeStruct((ROWS, D), jnp.float32),
        grid=(ROWS // rb,),
        in_specs=[pl.BlockSpec((rb, D), lambda i: (i, 0)), full_spec(D, D)],
        out_specs=pl.BlockSpec((rb, D), lambda i: (i, 0)),
        name="query",
    )(ds, passages)


def columns_kernel(pos_ref, ds_ref, q_ref, *outs):
    groups = {0: outs[:1], 1: outs[1:3], 2: outs[3:5], 3: outs[5:7]}
    for d in (2, 1, 3, 0):
        off = pl.multiple_of(((pos_ref[0] + d) % 4) * (D // 4), D // 4)
        part = lax.dot_general(
            ds_ref[:, pl.ds(off, D // 4)],
            q_ref[...],
            (((0,), (0,)), ((), ())),
            preferred_element_type=jnp.float32,
        )
        size = D // 4 // len(groups[d])
        for i, out in enumerate(groups[d]):
            out[...] = part[size * i : size * (i + 1)]


def columns_call(pos, ds, queries):
    full = lambda *shape: pl.BlockSpec(shape, lambda i, *_: (0,) * len(shape))
    sizes = (D // 4,) + (D // 8,) * 6
    return pl.pallas_call(
        columns_kernel,
        out_shape=tuple(jax.ShapeDtypeStruct((n, D), jnp.float32) for n in sizes),
        grid_spec=pltpu.PrefetchScalarGridSpec(
            num_scalar_prefetch=1,
            grid=(1,),
            in_specs=[full(ROWS, D), full(ROWS, D)],
            out_specs=tuple(full(n, D) for n in sizes),
        ),
        name="columns",
    )(pos, ds, queries)


def ring(d, n=4):
    return [(i, (i + d) % n) for i in range(n)]


def combine_kernel(pos_ref, own_ref, other_ref, loss0_ref, mine_ref, partner_ref, out_ref):
    for j in range(D // BLOCK):
        cols = slice(j * BLOCK, (j + 1) * BLOCK)
        rows = slice(j * QUARTER, (j + 1) * QUARTER)
        out_ref[:, rows, :] = own_ref[:, :, cols] + other_ref[:, :, cols]
    first = pos_ref[3] == 0
    for i in range(2):
        cols = slice(i * BLOCK, (i + 1) * BLOCK)
        mine, partner = mine_ref[0, :, cols], partner_ref[0, :, cols]
        lines = {
            i: jnp.where(first, mine, partner),
            2 + i: jnp.where(first, partner, mine),
            4 + i: loss0_ref[0, :, cols],
            6 + i: loss0_ref[1, :, cols],
        }
        for at, line in lines.items():
            shape = (out_ref.shape[0], 1, BLOCK)
            out_ref[:, SUM_ROWS + at : SUM_ROWS + at + 1, :] = jnp.broadcast_to(line[None], shape)


def combine(pos, own, other, loss0, mine, partner):
    step = 4
    block = pl.BlockSpec((step, QUARTER, D), lambda i, *_: (i, 0, 0))
    group = lambda n: pl.BlockSpec((n, 1, 256), lambda i, *_: (i // (8 // step), 0, 0))
    return pl.pallas_call(
        combine_kernel,
        out_shape=jax.ShapeDtypeStruct((SHARDS, SUM_ROWS + 8, BLOCK), jnp.float32),
        grid_spec=pltpu.PrefetchScalarGridSpec(
            num_scalar_prefetch=1,
            grid=(SHARDS // step,),
            in_specs=[block, block, group(2), group(1), group(1)],
            out_specs=pl.BlockSpec((step, SUM_ROWS + 8, BLOCK), lambda i, *_: (i, 0, 0)),
        ),
        name="combine",
    )(pos, own, other, loss0, mine, partner)


def total_kernel(me_ref, got_ref, lines_ref, lse_ref, grad_ref, loss_ref, sum_ref):
    chips = SHARDS // 2
    for core in range(2):
        for j in range(got_ref.shape[1] // QUARTER):
            rows = slice(j * QUARTER, (j + 1) * QUARTER)
            part = got_ref[core, rows, :]
            for chip in range(1, chips):
                part = part + got_ref[2 * chip + core, rows, :]
            to = slice(core * QUARTER, (core + 1) * QUARTER)
            grad_ref[to, j * BLOCK : (j + 1) * BLOCK] = part

    @pl.when(pl.program_id(0) == 0)
    def _():
        sum_ref[...] = jnp.sum(lines_ref[...], axis=0)
        mine = me_ref[0] % 8
        lane = lax.broadcasted_iota(jnp.int32, (8, BLOCK), 1)
        row = lambda at: jnp.broadcast_to(sum_ref[pl.ds(at, 1), :], (8, BLOCK))
        shift = BLOCK - QUARTER * (mine % 4)
        low = pltpu.roll(row(mine // 4), shift % BLOCK, 1)
        high = pltpu.roll(row(2 + mine // 4), (shift + QUARTER) % BLOCK, 1)
        early = pltpu.roll(row(4 + mine // 2), (mine % 2) * (BLOCK // 2), 1)
        loss = jnp.where(lane < QUARTER, low, high) + early + lse_ref[...]
        loss_ref[...] = loss[0:1, :]


def total(me, got, lse_rows):
    step = 2 * QUARTER
    return pl.pallas_call(
        total_kernel,
        out_shape=(
            jax.ShapeDtypeStruct((2 * QUARTER, D), jnp.float32),
            jax.ShapeDtypeStruct((1, BLOCK), jnp.float32),
        ),
        grid_spec=pltpu.PrefetchScalarGridSpec(
            num_scalar_prefetch=1,
            grid=(SUM_ROWS // step,),
            in_specs=[
                pl.BlockSpec((SHARDS, step, BLOCK), lambda i, *_: (0, i, 0)),
                pl.BlockSpec((SHARDS, 8, BLOCK), lambda i, *_: (0, SUM_ROWS // 8, 0)),
                full_spec(8, BLOCK),
            ],
            out_specs=(
                pl.BlockSpec((2 * QUARTER, 2 * BLOCK), lambda i, *_: (0, i)),
                full_spec(1, BLOCK),
            ),
            scratch_shapes=[pltpu.VMEM((8, BLOCK), jnp.float32)],
        ),
        name="total",
    )(me, got, got, lse_rows)


def send(value, axis, d, n=4):
    return lax.ppermute(value, axis, ring(d, n))


def together(*values):
    return lax.optimization_barrier(values)


def per_device(queries, passages, teacher, block_ids):
    mz, my, mx, mc = (lax.axis_index(a) for a in ("pb", "y", "x", "c"))
    me = my * 8 + mx * 2 + mc
    pos = jnp.stack([mz, my, mx, mc]).astype(jnp.int32)

    def exchange(value):
        return lax.all_to_all(value, PLANE, split_axis=0, concat_axis=0, tiled=True)

    sent0 = pack(0, block_ids, teacher)
    recv0 = exchange(sent0)
    ids1, _ = together(block_ids, sent0)
    sent1 = pack(1, ids1, teacher)
    s0, s1, lse, p0, p1 = score(queries, passages, teacher)
    sent1 = fill_lse(sent1, lse.reshape(LSE_ROWS, BLOCK))
    recv1 = exchange(sent1)
    ids2, _ = together(block_ids, lse)
    sent2 = pack(2, ids2, teacher)
    sent2, _ = together(sent2, recv1[0, 0, 0])
    recv2 = exchange(sent2)
    meta = recv0[:, BLOCK, : 2 * CAP].astype(jnp.int32).reshape(-1)
    lists = tuple(make_lists(meta))
    every = recv1[:, BLOCK:, :]
    top = jnp.max(every, axis=0)
    lse = (top + jnp.log(jnp.sum(jnp.exp(every - top[None]), axis=0))).reshape(8, 2, 256)
    split = lse.transpose(1, 0, 2).reshape(2, SHARDS, 2, QUARTER).transpose(2, 0, 1, 3)
    lse_half = split.reshape(2, 2, 4, 256).transpose(0, 2, 1, 3)
    ds0, loss0 = rows0_call(lists, s0, lse, [recv0, recv1])
    g0 = columns_call(pos, ds0, queries)
    z0 = [g0[0], g0[1:3], g0[3:5], g0[5:7]]
    np0, nm0 = send(z0[2][0], "pb", 1), send(z0[2][1], "pb", -1)
    fp0, fm0 = send(z0[1][1], "pb", 1), send(z0[3][0], "pb", -1)
    q0 = query_call(ds0, p0)
    sp0 = send(z0[1][0] + np0, "pb", 1)
    sm0 = send(z0[3][1] + nm0, "pb", -1)

    ds1, loss_other, other = rows1_call(1 - pos[3:], lists, s1, lse_half, recv2, q0, p1)
    swapped = send(other, "c", 1, 2)
    ds1, loss_own, own = rows1_call(pos[3:], lists, s1, lse_half, recv2, q0, p1, ds1)
    both = combine(pos, own, swapped, loss0, loss_own, loss_other)
    got = exchange(both)
    g1 = columns_call(pos, ds1.reshape(ROWS, D), queries)
    z1 = [g1[0], g1[1:3], g1[3:5], g1[5:7]]
    np1, nm1 = send(z1[2][0], "pb", 1), send(z1[2][1], "pb", -1)
    fp1, fm1 = send(z1[1][1], "pb", 1), send(z1[3][0], "pb", -1)
    sp1 = send(z1[1][0] + np1, "pb", 1)
    sm1 = send(z1[3][1] + nm1, "pb", -1)

    h = D // 8
    parts = [
        z0[0][:h] + sp0 + fm0,
        z0[0][h:] + fp0 + sm0,
        z1[0][:h] + sp1 + fm1,
        z1[0][h:] + fp1 + sm1,
    ]
    gp0, gp1 = jnp.concatenate(parts[:2]), jnp.concatenate(parts[2:])
    grad_passages = jnp.stack(
        [gp0.reshape(4, BLOCK // 2, D), gp1.reshape(4, BLOCK // 2, D)], axis=1
    ).reshape(4 * BLOCK, D)
    lse_rows = lax.dynamic_slice_in_dim(
        lse[:, 0, :].reshape(ROWS), me * (ROWS // SHARDS), ROWS // SHARDS
    )
    lse_rows = jnp.broadcast_to(jnp.pad(lse_rows, (0, BLOCK - 2 * QUARTER)), (8, BLOCK))
    grad_queries, loss = total(me.astype(jnp.int32).reshape(1), got, lse_rows)
    return loss[0, : 2 * QUARTER], grad_queries, grad_passages


def solution(mesh):
    fine = Mesh(mesh.devices.reshape(4, 4, 4, 2), ("pb",) + PLANE)
    in_specs = (P("pb", None), P(PLANE, None), P("pb", PLANE), P("pb", PLANE))
    out_specs = (P(("pb",) + PLANE), P(("pb",) + PLANE, None), P(PLANE + ("pb",), None))
    return jax.shard_map(
        per_device, mesh=fine, in_specs=in_specs, out_specs=out_specs, check_vma=False
    )
```

```python
import functools

import jax
import jax.numpy as jnp
from jax import lax
from jax.experimental import pallas as pl
from jax.experimental.pallas import tpu as pltpu
from jax.sharding import Mesh
from jax.sharding import PartitionSpec as P


BLOCK = 128
D = 1024
ROWS = 2048
PBLOCKS_DEV = 16
SLOTS_DEV = 4
CAP = 4
SHARDS = 32
ENTRIES = 64
PACK_STEP = 8
QUARTER = 32
LSE_ROWS = 32
SUM_ROWS = 256
PLANE = ("y", "x", "c")
SCORE_SCALE = 0.0625
GRAD_SCALE = 64.0


def as_row(column):
    n = column.shape[0]
    return jnp.broadcast_to(column, (n, BLOCK)).T[0:1, :]


def as_lanes(row):
    n = row.shape[1]
    return jnp.broadcast_to(row, (BLOCK, n)).T


def pack_kernel(piece, ids_ref, whole_ref, out_ref, slot_ref, count_ref, teacher_ref, sem):
    step = pl.program_id(0)

    @pl.when(step == 0)
    def _():
        copy = pltpu.make_async_copy(whole_ref, teacher_ref, sem)
        copy.start()
        for i in range(SHARDS):
            count_ref[i] = 0
        for i in range(SHARDS * CAP):
            slot_ref[i] = -1

        def place(i, carry):
            owner = ids_ref[i] // PBLOCKS_DEV
            rank = count_ref[owner]
            count_ref[owner] = rank + 1
            slot_ref[owner * CAP + jnp.minimum(rank, CAP - 1)] = i
            return carry

        lax.fori_loop(0, ENTRIES, place, 0, unroll=8)
        copy.wait()

    quarter = lax.broadcasted_iota(jnp.int32, (BLOCK, BLOCK), 1) // QUARTER
    lane = lax.broadcasted_iota(jnp.int32, (8, BLOCK), 1)
    move = lambda t, lanes: t if lanes % BLOCK == 0 else pltpu.roll(t, lanes % BLOCK, 1)
    for j in range(PACK_STEP):
        meta = jnp.zeros((8, BLOCK), jnp.float32)
        tiles = []
        for k in range(CAP):
            slot = slot_ref[(step * PACK_STEP + j) * CAP + k]
            entry = jnp.maximum(slot, 0)
            row = pl.multiple_of((entry // SLOTS_DEV) * BLOCK, BLOCK)
            col = pl.multiple_of((entry % SLOTS_DEV) * BLOCK, BLOCK)
            tiles.append(teacher_ref[pl.ds(row, BLOCK), pl.ds(col, BLOCK)])
            if piece == 0:
                where = jnp.where(slot < 0, -1, entry // SLOTS_DEV).astype(jnp.float32)
                block = (ids_ref[entry] % PBLOCKS_DEV).astype(jnp.float32)
                meta = jnp.where(lane == k, where, meta)
                meta = jnp.where(lane == CAP + k, block, meta)
        if piece < 2:
            moved = [move(t, QUARTER * (k - piece)) for k, t in enumerate(tiles)]
            low = jnp.where(quarter == 0, moved[0], moved[1])
            high = jnp.where(quarter == 2, moved[2], moved[3])
            out_ref[j, :BLOCK, :] = jnp.where(quarter < 2, low, high)
        else:
            for pair in range(CAP // 2):
                first = pltpu.roll(tiles[2 * pair], BLOCK // 2, 1)
                rows = slice(pair * BLOCK, (pair + 1) * BLOCK)
                out_ref[j, rows, :] = jnp.where(quarter < 2, first, tiles[2 * pair + 1])
        if piece == 0:
            out_ref[j, BLOCK:, :] = meta


def pack(piece, ids, teacher):
    rows = (BLOCK + 8, BLOCK, 2 * BLOCK)[piece]
    total = rows + (LSE_ROWS if piece == 1 else 0)
    return pl.pallas_call(
        functools.partial(pack_kernel, piece),
        out_shape=jax.ShapeDtypeStruct((SHARDS, total, BLOCK), jnp.float32),
        grid_spec=pltpu.PrefetchScalarGridSpec(
            num_scalar_prefetch=1,
            grid=(SHARDS // PACK_STEP,),
            in_specs=[pl.BlockSpec(memory_space=pl.ANY)],
            out_specs=pl.BlockSpec((PACK_STEP, rows, BLOCK), lambda s, ids: (s, 0, 0)),
            scratch_shapes=[
                pltpu.SMEM((SHARDS * CAP,), jnp.int32),
                pltpu.SMEM((SHARDS,), jnp.int32),
                pltpu.VMEM((ROWS, SLOTS_DEV * BLOCK), jnp.float32),
                pltpu.SemaphoreType.DMA,
            ],
        ),
        name="pack",
    )(ids, teacher)


def fill_kernel(lse_ref, sent_ref, out_ref):
    out_ref[...] = jnp.broadcast_to(lse_ref[...][None], out_ref.shape)


def fill_lse(sent, lse):
    return pl.pallas_call(
        fill_kernel,
        out_shape=jax.ShapeDtypeStruct(sent.shape, sent.dtype),
        grid=(1,),
        in_specs=[
            pl.BlockSpec((LSE_ROWS, BLOCK), lambda i: (0, 0)),
            pl.BlockSpec(memory_space=pl.ANY),
        ],
        out_specs=pl.BlockSpec((SHARDS, LSE_ROWS, BLOCK), lambda i: (0, BLOCK // LSE_ROWS, 0)),
        input_output_aliases={1: 0},
        name="fill_lse",
    )(lse, sent)


def list_kernel(meta_ref, start_ref, row_ref, block_ref, next_ref):
    blocks = ROWS // BLOCK
    for r in range(blocks):
        next_ref[r] = 0

    def count(n, carry):
        r = meta_ref[(n // CAP) * (2 * CAP) + n % CAP]

        @pl.when(r >= 0)
        def _():
            next_ref[r] = next_ref[r] + 1

        row_ref[n] = 0
        block_ref[n] = 0
        return carry

    lax.fori_loop(0, SHARDS * CAP, count, 0, unroll=4)
    total = 0
    for r in range(blocks):
        start_ref[r] = total
        size = next_ref[r]
        next_ref[r] = total
        total = total + size
    start_ref[blocks] = total

    def place(n, carry):
        src, k = n // CAP, n % CAP
        r = meta_ref[src * (2 * CAP) + k]

        @pl.when(r >= 0)
        def _():
            at = next_ref[r]
            next_ref[r] = at + 1
            row_ref[at] = n
            block_ref[at] = meta_ref[src * (2 * CAP) + CAP + k]

        return carry

    lax.fori_loop(0, SHARDS * CAP, place, 0, unroll=4)


def make_lists(meta):
    smem = pl.BlockSpec(memory_space=pltpu.SMEM)
    ints = lambda n: jax.ShapeDtypeStruct((n,), jnp.int32)
    return pl.pallas_call(
        list_kernel,
        out_shape=(ints(ROWS // BLOCK + 1), ints(SHARDS * CAP), ints(SHARDS * CAP)),
        in_specs=[smem],
        out_specs=(smem, smem, smem),
        scratch_shapes=[pltpu.SMEM((ROWS // BLOCK,), jnp.int32)],
        name="make_lists",
    )(meta)


def score_kernel(q_ref, p_ref, t_ref, s0_ref, s1_ref, lse_ref, p0_ref, p1_ref):
    half = BLOCK // 2

    @pl.when(pl.program_id(0) == 0)
    def _():
        for block in range(PBLOCKS_DEV):
            here = slice(block * half, (block + 1) * half)
            p0_ref[here, :] = p_ref[block * BLOCK : block * BLOCK + half, :]
            p1_ref[here, :] = p_ref[block * BLOCK + half : (block + 1) * BLOCK, :]

    q = q_ref[...]
    nt = (((1,), (1,)), ((), ()))
    s0 = lax.dot_general(q, p0_ref[...], nt, preferred_element_type=jnp.float32) * SCORE_SCALE
    s1 = lax.dot_general(q, p1_ref[...], nt, preferred_element_type=jnp.float32) * SCORE_SCALE
    s0_ref[...] = s0
    s1_ref[...] = s1
    top = jnp.maximum(jnp.max(s0, axis=1, keepdims=True), jnp.max(s1, axis=1, keepdims=True))
    total = jnp.sum(jnp.exp(s0 - top), axis=1, keepdims=True) + jnp.sum(
        jnp.exp(s1 - top), axis=1, keepdims=True
    )
    lse_ref[0, 0:1, :] = as_row(top + jnp.log(total))
    t = t_ref[...]
    ttop = jnp.max(t, axis=1, keepdims=True)
    ttotal = jnp.sum(jnp.exp(t - ttop), axis=1, keepdims=True)
    lse_ref[0, 1:2, :] = as_row(ttop + jnp.log(ttotal))


def score(queries, passages, teacher):
    rb = 256
    block = pl.BlockSpec((rb, D), lambda i: (i, 0))
    whole = pl.BlockSpec((D, D), lambda i: (0, 0))
    scores = jax.ShapeDtypeStruct((ROWS, D), jnp.float32)
    part = jax.ShapeDtypeStruct((D, D), jnp.bfloat16)
    return pl.pallas_call(
        score_kernel,
        out_shape=(
            scores,
            scores,
            jax.ShapeDtypeStruct((ROWS // rb, 2, rb), jnp.float32),
            part,
            part,
        ),
        grid=(ROWS // rb,),
        in_specs=[
            block,
            pl.BlockSpec((ROWS, D), lambda i: (0, 0)),
            pl.BlockSpec((rb, SLOTS_DEV * BLOCK), lambda i: (i, 0)),
        ],
        out_specs=(block, block, pl.BlockSpec((1, 2, rb), lambda i: (i, 0, 0)), whole, whole),
        name="score",
    )(queries, passages, teacher)


def subtract_tiles(
    fetch, sub_rows, first, end, block_ref, s_cols, lt_ref, rows, w_ref, acc_ref
):
    lane = lax.broadcasted_iota(jnp.int32, (sub_rows, BLOCK), 1)
    side = lane // (BLOCK // 2)

    def body(n, carry):
        parts = []
        for at in (first + 2 * n, first + 2 * n + 1):
            here = jnp.minimum(at, end - 1)
            block = block_ref[here]
            x = fetch(here, block)
            keep = (side == block % 2) & (at < end)
            centred = x - lt_ref[rows, :]
            prob = jnp.where(keep, jnp.exp(centred), 0.0)
            cols = pl.ds(pl.multiple_of((block // 2) * BLOCK, BLOCK), BLOCK)
            term = jnp.where(keep, prob * (centred - s_cols(cols)), 0.0)
            parts.append((prob, cols, term))
        acc_ref[rows, :] = acc_ref[rows, :] + (parts[0][2] + parts[1][2])
        for prob, cols, _ in parts:
            w_ref[rows, cols] = w_ref[rows, cols] - prob
        return carry

    lax.fori_loop(0, (end - first + 1) // 2, body, 0)


def rows0_kernel(
    start_ref, row_ref, block_ref, s_ref, lse_ref, recv0_ref, recv1_ref,
    ds_ref, loss_ref, w_ref, lt_ref, acc_ref,
):
    step = pl.program_id(0)
    rb = 256
    half = BLOCK // 2
    ls = as_lanes(lse_ref[0, 0:1, :])
    lt_ref[...] = as_lanes(lse_ref[0, 1:2, :])
    for j in range(D // BLOCK):
        cols = slice(j * BLOCK, (j + 1) * BLOCK)
        w_ref[:, cols] = jnp.exp(s_ref[:, cols] - ls)
    acc_ref[...] = jnp.zeros_like(acc_ref)
    early = lax.broadcasted_iota(jnp.int32, (BLOCK, BLOCK), 1) % half < QUARTER

    def fetch(n, block):
        slot = row_ref[n]
        src, k = slot // CAP, slot % CAP
        shift = (block % 2) * half
        at = pl.multiple_of(src * (BLOCK + 8), 8)
        x = recv0_ref[pl.ds(at, BLOCK), :]
        x = pltpu.roll(x, (shift - k * QUARTER + BLOCK) % BLOCK, 1)
        at = pl.multiple_of(src * (BLOCK + LSE_ROWS), 8)
        y = recv1_ref[pl.ds(at, BLOCK), :]
        y = pltpu.roll(y, (shift + QUARTER - k * QUARTER + BLOCK) % BLOCK, 1)
        return jnp.where(early, x, y)

    for sub in range(rb // BLOCK):
        rows = slice(sub * BLOCK, (sub + 1) * BLOCK)
        r = step * (rb // BLOCK) + sub
        subtract_tiles(
            fetch, BLOCK, start_ref[r], start_ref[r + 1], block_ref,
            lambda cols: s_ref[rows, cols], lt_ref, rows, w_ref, acc_ref,
        )
    ds_ref[...] = (w_ref[...] * GRAD_SCALE).astype(jnp.bfloat16)
    loss_ref[0] = as_row(jnp.sum(acc_ref[...], axis=1, keepdims=True))


ROW_SCRATCH = [
    pltpu.VMEM((256, D), jnp.float32),
    pltpu.VMEM((256, BLOCK), jnp.float32),
    pltpu.VMEM((256, BLOCK), jnp.float32),
]


def full_spec(*shape):
    return pl.BlockSpec(shape, lambda i, *_: (0,) * len(shape))


def rows0_call(lists, scores, lse, recvs):
    rb = 256
    recvs = [r.reshape(-1, BLOCK) for r in recvs]
    block = pl.BlockSpec((rb, D), lambda i, *_: (i, 0))
    return pl.pallas_call(
        rows0_kernel,
        out_shape=(
            jax.ShapeDtypeStruct((ROWS, D), jnp.bfloat16),
            jax.ShapeDtypeStruct((ROWS // rb, 1, rb), jnp.float32),
        ),
        grid_spec=pltpu.PrefetchScalarGridSpec(
            num_scalar_prefetch=len(lists),
            grid=(ROWS // rb,),
            in_specs=[block, pl.BlockSpec((1, 2, rb), lambda i, *_: (i, 0, 0))]
            + [full_spec(*r.shape) for r in recvs],
            out_specs=(block, pl.BlockSpec((1, 1, rb), lambda i, *_: (i, 0, 0))),
            scratch_shapes=ROW_SCRATCH,
        ),
        name="rows0",
    )(*lists, scores, lse, *recvs)


def rows1_kernel(
    pos_ref, start_ref, row_ref, block_ref, s_ref, lse_ref, recv_ref, add_ref, p_ref, loss0_ref,
    ds_ref, own_ref, other_ref, w_ref, lt_ref, acc_ref, past_ref, line_ref,
):
    step = pl.program_id(0)
    steps = pl.num_programs(0) - 1
    rb = 256
    half = BLOCK // 2
    part = add_ref[...] + jnp.dot(past_ref[...], p_ref[...], preferred_element_type=jnp.float32)
    ls = as_lanes(lse_ref[0, 0:1, :])
    lt_ref[...] = as_lanes(lse_ref[0, 1:2, :])
    for j in range(D // BLOCK):
        cols = slice(j * BLOCK, (j + 1) * BLOCK)
        w_ref[:, cols] = jnp.exp(s_ref[:, cols] - ls)
    acc_ref[...] = jnp.zeros_like(acc_ref)
    part = part.reshape(rb // (2 * QUARTER), 2, QUARTER, D)
    first = pos_ref[3] == 0
    for j in range(D // BLOCK):
        cols = slice(j * BLOCK, (j + 1) * BLOCK)
        rows = slice(j * QUARTER, (j + 1) * QUARTER)
        even, odd = part[:, 0, :, cols], part[:, 1, :, cols]
        own_ref[:, rows, :] = jnp.where(first, even, odd)
        other_ref[:, rows, :] = jnp.where(first, odd, even)
    lines = (own_ref.shape[0], 8, BLOCK)
    own_ref[:, SUM_ROWS:, :] = jnp.broadcast_to(line_ref[...][None], lines)
    other_ref[:, SUM_ROWS:, :] = jnp.zeros(lines, jnp.float32)

    def fetch(n, block):
        slot = row_ref[n]
        at = pl.multiple_of((slot // 2) * BLOCK, BLOCK)
        return pltpu.roll(recv_ref[pl.ds(at, BLOCK), :], ((block + slot) % 2) * half, 1)

    @pl.when(step < steps)
    def _():
        for sub in range(rb // BLOCK):
            rows = slice(sub * BLOCK, (sub + 1) * BLOCK)
            r = step * (rb // BLOCK) + sub
            subtract_tiles(
                fetch, BLOCK, start_ref[r], start_ref[r + 1], block_ref,
                lambda cols: s_ref[rows, cols], lt_ref, rows, w_ref, acc_ref,
            )
        ds = (w_ref[...] * GRAD_SCALE).astype(jnp.bfloat16)
        ds_ref[...] = ds
        past_ref[...] = ds
        loss = as_row(jnp.sum(acc_ref[...], axis=1, keepdims=True)) + loss0_ref[0]
        low = jnp.broadcast_to(loss[:, :BLOCK], (8, BLOCK))
        high = jnp.broadcast_to(loss[:, BLOCK:], (8, BLOCK))
        line_ref[...] = jnp.where(lax.broadcasted_iota(jnp.int32, (8, BLOCK), 0) == 0, low, high)


def rows1_call(scalars, scores, lse, recv, add, passages, loss0):
    rb = 256
    steps = ROWS // rb
    recv = recv.reshape(-1, BLOCK)
    now = lambda i, *_: (jnp.minimum(i, steps - 1), 0)
    now3 = lambda i, *_: (jnp.minimum(i, steps - 1), 0, 0)
    past = lambda i, *_: (jnp.maximum(i - 1, 0), 0)
    past3 = lambda i, *_: (jnp.maximum(i - 1, 0), 0, 0)
    out = pl.BlockSpec((rb // (2 * QUARTER), SUM_ROWS + 8, BLOCK), past3)
    out_type = jax.ShapeDtypeStruct((SHARDS, SUM_ROWS + 8, BLOCK), jnp.float32)
    return pl.pallas_call(
        rows1_kernel,
        out_shape=(
            jax.ShapeDtypeStruct((ROWS, D), jnp.bfloat16),
            out_type,
            out_type,
        ),
        grid_spec=pltpu.PrefetchScalarGridSpec(
            num_scalar_prefetch=len(scalars),
            grid=(steps + 1,),
            in_specs=[
                pl.BlockSpec((rb, D), now),
                pl.BlockSpec((1, 2, rb), now3),
                full_spec(*recv.shape),
                pl.BlockSpec((rb, D), past),
                full_spec(D, D),
                pl.BlockSpec((1, 1, rb), now3),
            ],
            out_specs=(pl.BlockSpec((rb, D), now), out, out),
            scratch_shapes=ROW_SCRATCH
            + [pltpu.VMEM((rb, D), jnp.bfloat16), pltpu.VMEM((8, BLOCK), jnp.float32)],
        ),
        name="rows1",
    )(*scalars, scores, lse, recv, add, passages, loss0)


def query_kernel(ds_ref, p_ref, out_ref):
    out_ref[...] = jnp.dot(ds_ref[...], p_ref[...], preferred_element_type=jnp.float32)


def query_call(ds, passages):
    rb = 512
    return pl.pallas_call(
        query_kernel,
        out_shape=jax.ShapeDtypeStruct((ROWS, D), jnp.float32),
        grid=(ROWS // rb,),
        in_specs=[pl.BlockSpec((rb, D), lambda i: (i, 0)), full_spec(D, D)],
        out_specs=pl.BlockSpec((rb, D), lambda i: (i, 0)),
        name="query",
    )(ds, passages)


def columns_kernel(groups, pos_ref, ds_ref, q_ref, *outs):
    step = pl.program_id(0)
    part = lax.dot_general(
        ds_ref[...], q_ref[...], (((0,), (0,)), ((), ())), preferred_element_type=jnp.float32
    )
    at = 0
    for i, d in enumerate(groups):
        count = 1 if d == 0 else 2
        mine = outs[at : at + count]
        at += count

        @pl.when(step == i)
        def _(mine=mine):
            size = D // 4 // len(mine)
            for n, out in enumerate(mine):
                out[...] = part[size * n : size * (n + 1)]


def columns_call(pos, ds, queries, groups):
    def column(i, pos_ref):
        d = functools.reduce(lambda v, n: jnp.where(i == n, groups[n], v), range(len(groups)), 0)
        return 0, (pos_ref[0] + d) % 4

    sizes = sum(([D // 4] if d == 0 else [D // 8] * 2 for d in groups), [])
    outs = pl.pallas_call(
        functools.partial(columns_kernel, groups),
        out_shape=tuple(jax.ShapeDtypeStruct((n, D), jnp.float32) for n in sizes),
        grid_spec=pltpu.PrefetchScalarGridSpec(
            num_scalar_prefetch=1,
            grid=(len(groups),),
            in_specs=[pl.BlockSpec((ROWS, D // 4), column), full_spec(ROWS, D)],
            out_specs=tuple(full_spec(n, D) for n in sizes),
        ),
        name="columns",
    )(pos, ds, queries)
    outs = list(outs)
    return {d: [outs.pop(0) for _ in range(1 if d == 0 else 2)] for d in groups}


def total_kernel(me_ref, got_ref, lines_ref, lse_ref, grad_ref, loss_ref, sum_ref):
    chips = SHARDS // 2
    for core in range(2):
        for j in range(got_ref.shape[1] // QUARTER):
            rows = slice(j * QUARTER, (j + 1) * QUARTER)
            part = got_ref[core, rows, :]
            for chip in range(1, chips):
                part = part + got_ref[2 * chip + core, rows, :]
            to = slice(core * QUARTER, (core + 1) * QUARTER)
            grad_ref[to, j * BLOCK : (j + 1) * BLOCK] = part

    @pl.when(pl.program_id(0) == 0)
    def _():
        sum_ref[...] = jnp.sum(lines_ref[...], axis=0)
        mine = me_ref[0] % 4
        line = jnp.broadcast_to(sum_ref[pl.ds(mine // 2, 1), :], (8, BLOCK))
        line = pltpu.roll(line, (mine % 2) * (BLOCK // 2), 1) + lse_ref[...]
        loss_ref[...] = line[0:1, : 2 * QUARTER]


def total(me, got, lse_rows):
    step = 4 * QUARTER
    return pl.pallas_call(
        total_kernel,
        out_shape=(
            jax.ShapeDtypeStruct((2 * QUARTER, D), jnp.float32),
            jax.ShapeDtypeStruct((1, 2 * QUARTER), jnp.float32),
        ),
        grid_spec=pltpu.PrefetchScalarGridSpec(
            num_scalar_prefetch=1,
            grid=(SUM_ROWS // step,),
            in_specs=[
                pl.BlockSpec((SHARDS, step, BLOCK), lambda i, *_: (0, i, 0)),
                pl.BlockSpec((SHARDS, 8, BLOCK), lambda i, *_: (0, SUM_ROWS // 8, 0)),
                full_spec(8, BLOCK),
            ],
            out_specs=(
                pl.BlockSpec((2 * QUARTER, step // QUARTER * BLOCK), lambda i, *_: (0, i)),
                full_spec(1, 2 * QUARTER),
            ),
            scratch_shapes=[pltpu.VMEM((8, BLOCK), jnp.float32)],
        ),
        name="total",
    )(me, got, got, lse_rows)


def ring(d, n=4):
    return [(i, (i + d) % n) for i in range(n)]


def send(value, axis, d, n=4):
    return lax.ppermute(value, axis, ring(d, n))


def together(*values):
    return lax.optimization_barrier(values)


def per_device(queries, passages, teacher, block_ids):
    mz, my, mx, mc = (lax.axis_index(a) for a in ("pb", "y", "x", "c"))
    me = my * 8 + mx * 2 + mc
    pos = jnp.stack([mz, my, mx, mc]).astype(jnp.int32)
    flat_ids = block_ids.reshape(-1)

    def exchange(value):
        return lax.all_to_all(value, PLANE, split_axis=0, concat_axis=0, tiled=True)

    sent0 = pack(0, flat_ids, teacher)
    recv0 = exchange(sent0)
    ids1, _ = together(flat_ids, sent0)
    sent1 = pack(1, ids1, teacher)
    s0, s1, lse, p0, p1 = score(queries, passages, teacher)
    sent1 = fill_lse(sent1, lse.reshape(LSE_ROWS, BLOCK))
    recv1 = exchange(sent1)
    ids2, _ = together(flat_ids, lse)
    sent2 = pack(2, ids2, teacher)
    sent2, _ = together(sent2, recv1[0, 0, 0])
    recv2 = exchange(sent2)
    meta = recv0[:, BLOCK, : 2 * CAP].astype(jnp.int32).reshape(-1)
    lists = tuple(make_lists(meta))
    every = recv1[:, BLOCK:, :]
    top = jnp.max(every, axis=0)
    lse = (top + jnp.log(jnp.sum(jnp.exp(every - top[None]), axis=0))).reshape(8, 2, 256)
    ds0, loss0 = rows0_call(lists, s0, lse, [recv0, recv1])
    z0 = columns_call(pos, ds0, queries, (2, 1, 3, 0))
    np0, nm0 = send(z0[2][0], "pb", 1), send(z0[2][1], "pb", -1)
    fp0, fm0 = send(z0[1][1], "pb", 1), send(z0[3][0], "pb", -1)
    q0 = query_call(ds0, p0)
    sp0 = send(z0[1][0] + np0, "pb", 1)
    sm0 = send(z0[3][1] + nm0, "pb", -1)

    ds1, own, other = rows1_call((pos,) + lists, s1, lse, recv2, q0, p1, loss0)
    swapped = send(other, "c", 1, 2)
    z1 = columns_call(pos, ds1, queries, (2, 1))
    both = own + swapped
    got = exchange(both)
    z1.update(columns_call(pos, ds1, queries, (3, 0)))
    np1, nm1 = send(z1[2][0], "pb", 1), send(z1[2][1], "pb", -1)
    fp1, fm1 = send(z1[1][1], "pb", 1), send(z1[3][0], "pb", -1)
    sp1 = send(z1[1][0] + np1, "pb", 1)
    sm1 = send(z1[3][1] + nm1, "pb", -1)

    h = D // 8
    parts = [
        z0[0][0][:h] + sp0 + fm0,
        z0[0][0][h:] + fp0 + sm0,
        z1[0][0][:h] + sp1 + fm1,
        z1[0][0][h:] + fp1 + sm1,
    ]
    gp0, gp1 = jnp.concatenate(parts[:2]), jnp.concatenate(parts[2:])
    grad_passages = jnp.stack(
        [gp0.reshape(4, BLOCK // 2, D), gp1.reshape(4, BLOCK // 2, D)], axis=1
    ).reshape(4 * BLOCK, D)
    lse_rows = lax.dynamic_slice_in_dim(
        lse[:, 0, :].reshape(ROWS), me * (ROWS // SHARDS), ROWS // SHARDS
    )
    lse_rows = jnp.broadcast_to(jnp.pad(lse_rows, (0, BLOCK - 2 * QUARTER)), (8, BLOCK))
    grad_queries, loss = total(me.astype(jnp.int32).reshape(1), got, lse_rows)
    return loss.reshape(2 * QUARTER), grad_queries, grad_passages


def solution(mesh):
    fine = Mesh(mesh.devices.reshape(4, 4, 4, 2), ("pb",) + PLANE)
    in_specs = (P("pb", None), P(PLANE, None), P("pb", PLANE), P("pb", PLANE))
    out_specs = (P(("pb",) + PLANE), P(("pb",) + PLANE, None), P(PLANE + ("pb",), None))
    return jax.shard_map(
        per_device, mesh=fine, in_specs=in_specs, out_specs=out_specs, check_vma=False
    )
```

```python
import functools

import jax
import jax.numpy as jnp
from jax import lax
from jax.experimental import pallas as pl
from jax.experimental.pallas import tpu as pltpu
from jax.sharding import Mesh
from jax.sharding import PartitionSpec as P


BLOCK = 128
D = 1024
ROWS = 2048
PBLOCKS_DEV = 16
SLOTS_DEV = 4
CAP = 4
SHARDS = 32
ENTRIES = 64
PACK_STEP = 8
QUARTER = 32
LSE_ROWS = 32
SUM_ROWS = 256
PLANE = ("y", "x", "c")
SCORE_SCALE = 0.0625
GRAD_SCALE = 64.0


def as_row(column):
    n = column.shape[0]
    return jnp.broadcast_to(column, (n, BLOCK)).T[0:1, :]


def as_lanes(row):
    n = row.shape[1]
    return jnp.broadcast_to(row, (BLOCK, n)).T


def pack_kernel(piece, ids_ref, whole_ref, out_ref, slot_ref, count_ref, teacher_ref, sem):
    step = pl.program_id(0)

    @pl.when(step == 0)
    def _():
        copy = pltpu.make_async_copy(whole_ref, teacher_ref, sem)
        copy.start()
        for i in range(SHARDS):
            count_ref[i] = 0
        for i in range(SHARDS * CAP):
            slot_ref[i] = -1

        def place(i, carry):
            owner = ids_ref[i] // PBLOCKS_DEV
            rank = count_ref[owner]
            count_ref[owner] = rank + 1
            slot_ref[owner * CAP + jnp.minimum(rank, CAP - 1)] = i
            return carry

        lax.fori_loop(0, ENTRIES, place, 0, unroll=8)
        copy.wait()

    quarter = lax.broadcasted_iota(jnp.int32, (BLOCK, BLOCK), 1) // QUARTER
    lane = lax.broadcasted_iota(jnp.int32, (8, BLOCK), 1)
    move = lambda t, lanes: t if lanes % BLOCK == 0 else pltpu.roll(t, lanes % BLOCK, 1)
    for j in range(PACK_STEP):
        meta = jnp.zeros((8, BLOCK), jnp.float32)
        tiles = []
        for k in range(CAP):
            slot = slot_ref[(step * PACK_STEP + j) * CAP + k]
            entry = jnp.maximum(slot, 0)
            row = pl.multiple_of((entry // SLOTS_DEV) * BLOCK, BLOCK)
            col = pl.multiple_of((entry % SLOTS_DEV) * BLOCK, BLOCK)
            tiles.append(teacher_ref[pl.ds(row, BLOCK), pl.ds(col, BLOCK)])
            if piece == 0:
                where = jnp.where(slot < 0, -1, entry // SLOTS_DEV).astype(jnp.float32)
                block = (ids_ref[entry] % PBLOCKS_DEV).astype(jnp.float32)
                meta = jnp.where(lane == k, where, meta)
                meta = jnp.where(lane == CAP + k, block, meta)
        if piece < 2:
            moved = [move(t, QUARTER * (k - piece)) for k, t in enumerate(tiles)]
            low = jnp.where(quarter == 0, moved[0], moved[1])
            high = jnp.where(quarter == 2, moved[2], moved[3])
            out_ref[j, :BLOCK, :] = jnp.where(quarter < 2, low, high)
        else:
            for pair in range(CAP // 2):
                first = pltpu.roll(tiles[2 * pair], BLOCK // 2, 1)
                rows = slice(pair * BLOCK, (pair + 1) * BLOCK)
                out_ref[j, rows, :] = jnp.where(quarter < 2, first, tiles[2 * pair + 1])
        if piece == 0:
            out_ref[j, BLOCK:, :] = meta


def pack(piece, ids, teacher):
    rows = (BLOCK + 8, BLOCK, 2 * BLOCK)[piece]
    total = rows + (LSE_ROWS if piece == 1 else 0)
    return pl.pallas_call(
        functools.partial(pack_kernel, piece),
        out_shape=jax.ShapeDtypeStruct((SHARDS, total, BLOCK), jnp.float32),
        grid_spec=pltpu.PrefetchScalarGridSpec(
            num_scalar_prefetch=1,
            grid=(SHARDS // PACK_STEP,),
            in_specs=[pl.BlockSpec(memory_space=pl.ANY)],
            out_specs=pl.BlockSpec((PACK_STEP, rows, BLOCK), lambda s, ids: (s, 0, 0)),
            scratch_shapes=[
                pltpu.SMEM((SHARDS * CAP,), jnp.int32),
                pltpu.SMEM((SHARDS,), jnp.int32),
                pltpu.VMEM((ROWS, SLOTS_DEV * BLOCK), jnp.float32),
                pltpu.SemaphoreType.DMA,
            ],
        ),
        name="pack",
    )(ids, teacher)


def fill_kernel(lse_ref, sent_ref, out_ref):
    out_ref[...] = jnp.broadcast_to(lse_ref[...][None], out_ref.shape)


def fill_lse(sent, lse):
    return pl.pallas_call(
        fill_kernel,
        out_shape=jax.ShapeDtypeStruct(sent.shape, sent.dtype),
        grid=(1,),
        in_specs=[
            pl.BlockSpec((LSE_ROWS, BLOCK), lambda i: (0, 0)),
            pl.BlockSpec(memory_space=pl.ANY),
        ],
        out_specs=pl.BlockSpec((SHARDS, LSE_ROWS, BLOCK), lambda i: (0, BLOCK // LSE_ROWS, 0)),
        input_output_aliases={1: 0},
        name="fill_lse",
    )(lse, sent)


def list_kernel(meta_ref, start_ref, row_ref, block_ref, next_ref):
    blocks = ROWS // BLOCK
    for r in range(blocks):
        next_ref[r] = 0

    def count(n, carry):
        r = meta_ref[(n // CAP) * (2 * CAP) + n % CAP]

        @pl.when(r >= 0)
        def _():
            next_ref[r] = next_ref[r] + 1

        row_ref[n] = 0
        block_ref[n] = 0
        return carry

    lax.fori_loop(0, SHARDS * CAP, count, 0, unroll=4)
    total = 0
    for r in range(blocks):
        start_ref[r] = total
        size = next_ref[r]
        next_ref[r] = total
        total = total + size
    start_ref[blocks] = total

    def place(n, carry):
        src, k = n // CAP, n % CAP
        r = meta_ref[src * (2 * CAP) + k]

        @pl.when(r >= 0)
        def _():
            at = next_ref[r]
            next_ref[r] = at + 1
            row_ref[at] = n
            block_ref[at] = meta_ref[src * (2 * CAP) + CAP + k]

        return carry

    lax.fori_loop(0, SHARDS * CAP, place, 0, unroll=4)


def make_lists(meta):
    smem = pl.BlockSpec(memory_space=pltpu.SMEM)
    ints = lambda n: jax.ShapeDtypeStruct((n,), jnp.int32)
    return pl.pallas_call(
        list_kernel,
        out_shape=(ints(ROWS // BLOCK + 1), ints(SHARDS * CAP), ints(SHARDS * CAP)),
        in_specs=[smem],
        out_specs=(smem, smem, smem),
        scratch_shapes=[pltpu.SMEM((ROWS // BLOCK,), jnp.int32)],
        name="make_lists",
    )(meta)


def score_kernel(q_ref, p_ref, t_ref, s0_ref, s1_ref, lse_ref, p0_ref, p1_ref):
    half = BLOCK // 2

    @pl.when(pl.program_id(0) == 0)
    def _():
        for block in range(PBLOCKS_DEV):
            here = slice(block * half, (block + 1) * half)
            p0_ref[here, :] = p_ref[block * BLOCK : block * BLOCK + half, :]
            p1_ref[here, :] = p_ref[block * BLOCK + half : (block + 1) * BLOCK, :]

    q = q_ref[...]
    nt = (((1,), (1,)), ((), ()))
    s0 = lax.dot_general(q, p0_ref[...], nt, preferred_element_type=jnp.float32) * SCORE_SCALE
    s1 = lax.dot_general(q, p1_ref[...], nt, preferred_element_type=jnp.float32) * SCORE_SCALE
    s0_ref[...] = s0
    s1_ref[...] = s1
    top = jnp.maximum(jnp.max(s0, axis=1, keepdims=True), jnp.max(s1, axis=1, keepdims=True))
    total = jnp.sum(jnp.exp(s0 - top), axis=1, keepdims=True) + jnp.sum(
        jnp.exp(s1 - top), axis=1, keepdims=True
    )
    lse_ref[0, 0:1, :] = as_row(top + jnp.log(total))
    t = t_ref[...]
    ttop = jnp.max(t, axis=1, keepdims=True)
    ttotal = jnp.sum(jnp.exp(t - ttop), axis=1, keepdims=True)
    lse_ref[0, 1:2, :] = as_row(ttop + jnp.log(ttotal))


def score(queries, passages, teacher):
    rb = 256
    block = pl.BlockSpec((rb, D), lambda i: (i, 0))
    whole = pl.BlockSpec((D, D), lambda i: (0, 0))
    scores = jax.ShapeDtypeStruct((ROWS, D), jnp.float32)
    part = jax.ShapeDtypeStruct((D, D), jnp.bfloat16)
    return pl.pallas_call(
        score_kernel,
        out_shape=(
            scores,
            scores,
            jax.ShapeDtypeStruct((ROWS // rb, 2, rb), jnp.float32),
            part,
            part,
        ),
        grid=(ROWS // rb,),
        in_specs=[
            block,
            pl.BlockSpec((ROWS, D), lambda i: (0, 0)),
            pl.BlockSpec((rb, SLOTS_DEV * BLOCK), lambda i: (i, 0)),
        ],
        out_specs=(block, block, pl.BlockSpec((1, 2, rb), lambda i: (i, 0, 0)), whole, whole),
        name="score",
    )(queries, passages, teacher)


def subtract_tiles(
    fetch, sub_rows, first, end, block_ref, s_cols, lt_ref, rows, w_ref, acc_ref
):
    lane = lax.broadcasted_iota(jnp.int32, (sub_rows, BLOCK), 1)
    side = lane // (BLOCK // 2)

    def body(n, carry):
        parts = []
        for at in (first + 2 * n, first + 2 * n + 1):
            here = jnp.minimum(at, end - 1)
            block = block_ref[here]
            x = fetch(here, block)
            keep = (side == block % 2) & (at < end)
            centred = x - lt_ref[rows, :]
            prob = jnp.where(keep, jnp.exp(centred), 0.0)
            cols = pl.ds(pl.multiple_of((block // 2) * BLOCK, BLOCK), BLOCK)
            term = jnp.where(keep, prob * (centred - s_cols(cols)), 0.0)
            parts.append((prob, cols, term))
        acc_ref[rows, :] = acc_ref[rows, :] + (parts[0][2] + parts[1][2])
        for prob, cols, _ in parts:
            w_ref[rows, cols] = w_ref[rows, cols] - prob
        return carry

    lax.fori_loop(0, (end - first + 1) // 2, body, 0)


def rows0_kernel(
    start_ref, row_ref, block_ref, s_ref, lse_ref, recv0_ref, recv1_ref,
    ds_ref, loss_ref, w_ref, lt_ref, acc_ref,
):
    step = pl.program_id(0)
    rb = 256
    half = BLOCK // 2
    ls = as_lanes(lse_ref[0, 0:1, :])
    lt_ref[...] = as_lanes(lse_ref[0, 1:2, :])
    for j in range(D // BLOCK):
        cols = slice(j * BLOCK, (j + 1) * BLOCK)
        w_ref[:, cols] = jnp.exp(s_ref[:, cols] - ls)
    acc_ref[...] = jnp.zeros_like(acc_ref)
    early = lax.broadcasted_iota(jnp.int32, (BLOCK, BLOCK), 1) % half < QUARTER

    def fetch(n, block):
        slot = row_ref[n]
        src, k = slot // CAP, slot % CAP
        shift = (block % 2) * half
        at = pl.multiple_of(src * (BLOCK + 8), 8)
        x = recv0_ref[pl.ds(at, BLOCK), :]
        x = pltpu.roll(x, (shift - k * QUARTER + BLOCK) % BLOCK, 1)
        at = pl.multiple_of(src * (BLOCK + LSE_ROWS), 8)
        y = recv1_ref[pl.ds(at, BLOCK), :]
        y = pltpu.roll(y, (shift + QUARTER - k * QUARTER + BLOCK) % BLOCK, 1)
        return jnp.where(early, x, y)

    for sub in range(rb // BLOCK):
        rows = slice(sub * BLOCK, (sub + 1) * BLOCK)
        r = step * (rb // BLOCK) + sub
        subtract_tiles(
            fetch, BLOCK, start_ref[r], start_ref[r + 1], block_ref,
            lambda cols: s_ref[rows, cols], lt_ref, rows, w_ref, acc_ref,
        )
    ds_ref[...] = (w_ref[...] * GRAD_SCALE).astype(jnp.bfloat16)
    loss_ref[0] = as_row(jnp.sum(acc_ref[...], axis=1, keepdims=True))


ROW_SCRATCH = [
    pltpu.VMEM((256, D), jnp.float32),
    pltpu.VMEM((256, BLOCK), jnp.float32),
    pltpu.VMEM((256, BLOCK), jnp.float32),
]


def full_spec(*shape):
    return pl.BlockSpec(shape, lambda i, *_: (0,) * len(shape))


def rows0_call(lists, scores, lse, recvs):
    rb = 256
    recvs = [r.reshape(-1, BLOCK) for r in recvs]
    block = pl.BlockSpec((rb, D), lambda i, *_: (i, 0))
    return pl.pallas_call(
        rows0_kernel,
        out_shape=(
            jax.ShapeDtypeStruct((ROWS, D), jnp.bfloat16),
            jax.ShapeDtypeStruct((ROWS // rb, 1, rb), jnp.float32),
        ),
        grid_spec=pltpu.PrefetchScalarGridSpec(
            num_scalar_prefetch=len(lists),
            grid=(ROWS // rb,),
            in_specs=[block, pl.BlockSpec((1, 2, rb), lambda i, *_: (i, 0, 0))]
            + [full_spec(*r.shape) for r in recvs],
            out_specs=(block, pl.BlockSpec((1, 1, rb), lambda i, *_: (i, 0, 0))),
            scratch_shapes=ROW_SCRATCH,
        ),
        compiler_params=pltpu.CompilerParams(vmem_limit_bytes=30 << 20),
        name="rows0",
    )(*lists, scores, lse, *recvs)


def rows1_kernel(
    pos_ref, start_ref, row_ref, block_ref, s_ref, lse_ref, recv_ref, add_ref, p_ref, loss0_ref,
    ds_ref, own_ref, other_ref, w_ref, lt_ref, acc_ref, past_ref, line_ref,
):
    step = pl.program_id(0)
    steps = pl.num_programs(0) - 1
    rb = 256
    half = BLOCK // 2
    part = add_ref[...] + jnp.dot(past_ref[...], p_ref[...], preferred_element_type=jnp.float32)
    ls = as_lanes(lse_ref[0, 0:1, :])
    lt_ref[...] = as_lanes(lse_ref[0, 1:2, :])
    for j in range(D // BLOCK):
        cols = slice(j * BLOCK, (j + 1) * BLOCK)
        w_ref[:, cols] = jnp.exp(s_ref[:, cols] - ls)
    acc_ref[...] = jnp.zeros_like(acc_ref)
    part = part.reshape(rb // (2 * QUARTER), 2, QUARTER, D)
    first = pos_ref[3] == 0
    for j in range(D // BLOCK):
        cols = slice(j * BLOCK, (j + 1) * BLOCK)
        rows = slice(j * QUARTER, (j + 1) * QUARTER)
        even, odd = part[:, 0, :, cols], part[:, 1, :, cols]
        own_ref[:, rows, :] = jnp.where(first, even, odd)
        other_ref[:, rows, :] = jnp.where(first, odd, even)
    lines = (own_ref.shape[0], 8, BLOCK)
    own_ref[:, SUM_ROWS:, :] = jnp.broadcast_to(line_ref[...][None], lines)
    other_ref[:, SUM_ROWS:, :] = jnp.zeros(lines, jnp.float32)

    def fetch(n, block):
        slot = row_ref[n]
        at = pl.multiple_of((slot // 2) * BLOCK, BLOCK)
        return pltpu.roll(recv_ref[pl.ds(at, BLOCK), :], ((block + slot) % 2) * half, 1)

    @pl.when(step < steps)
    def _():
        for sub in range(rb // BLOCK):
            rows = slice(sub * BLOCK, (sub + 1) * BLOCK)
            r = step * (rb // BLOCK) + sub
            subtract_tiles(
                fetch, BLOCK, start_ref[r], start_ref[r + 1], block_ref,
                lambda cols: s_ref[rows, cols], lt_ref, rows, w_ref, acc_ref,
            )
        ds = (w_ref[...] * GRAD_SCALE).astype(jnp.bfloat16)
        ds_ref[...] = ds
        past_ref[...] = ds
        loss = as_row(jnp.sum(acc_ref[...], axis=1, keepdims=True)) + loss0_ref[0]
        low = jnp.broadcast_to(loss[:, :BLOCK], (8, BLOCK))
        high = jnp.broadcast_to(loss[:, BLOCK:], (8, BLOCK))
        line_ref[...] = jnp.where(lax.broadcasted_iota(jnp.int32, (8, BLOCK), 0) == 0, low, high)


def rows1_call(scalars, scores, lse, recv, add, passages, loss0):
    rb = 256
    steps = ROWS // rb
    recv = recv.reshape(-1, BLOCK)
    now = lambda i, *_: (jnp.minimum(i, steps - 1), 0)
    now3 = lambda i, *_: (jnp.minimum(i, steps - 1), 0, 0)
    past = lambda i, *_: (jnp.maximum(i - 1, 0), 0)
    past3 = lambda i, *_: (jnp.maximum(i - 1, 0), 0, 0)
    out = pl.BlockSpec((rb // (2 * QUARTER), SUM_ROWS + 8, BLOCK), past3)
    out_type = jax.ShapeDtypeStruct((SHARDS, SUM_ROWS + 8, BLOCK), jnp.float32)
    return pl.pallas_call(
        rows1_kernel,
        out_shape=(
            jax.ShapeDtypeStruct((ROWS, D), jnp.bfloat16),
            out_type,
            out_type,
        ),
        grid_spec=pltpu.PrefetchScalarGridSpec(
            num_scalar_prefetch=len(scalars),
            grid=(steps + 1,),
            in_specs=[
                pl.BlockSpec((rb, D), now),
                pl.BlockSpec((1, 2, rb), now3),
                full_spec(*recv.shape),
                pl.BlockSpec((rb, D), past),
                full_spec(D, D),
                pl.BlockSpec((1, 1, rb), now3),
            ],
            out_specs=(pl.BlockSpec((rb, D), now), out, out),
            scratch_shapes=ROW_SCRATCH
            + [pltpu.VMEM((rb, D), jnp.bfloat16), pltpu.VMEM((8, BLOCK), jnp.float32)],
        ),
        compiler_params=pltpu.CompilerParams(vmem_limit_bytes=32 << 20),
        name="rows1",
    )(*scalars, scores, lse, recv, add, passages, loss0)


def query_kernel(ds_ref, p_ref, out_ref):
    out_ref[...] = jnp.dot(ds_ref[...], p_ref[...], preferred_element_type=jnp.float32)


def query_call(ds, passages):
    rb = 512
    return pl.pallas_call(
        query_kernel,
        out_shape=jax.ShapeDtypeStruct((ROWS, D), jnp.float32),
        grid=(ROWS // rb,),
        in_specs=[pl.BlockSpec((rb, D), lambda i: (i, 0)), full_spec(D, D)],
        out_specs=pl.BlockSpec((rb, D), lambda i: (i, 0)),
        compiler_params=pltpu.CompilerParams(vmem_limit_bytes=30 << 20),
        name="query",
    )(ds, passages)


def columns_kernel(groups, pos_ref, ds_ref, q_ref, *outs):
    step = pl.program_id(0)
    part = lax.dot_general(
        ds_ref[...], q_ref[...], (((0,), (0,)), ((), ())), preferred_element_type=jnp.float32
    )
    at = 0
    for i, d in enumerate(groups):
        count = 1 if d == 0 else 2
        mine = outs[at : at + count]
        at += count

        @pl.when(step == i)
        def _(mine=mine):
            size = D // 4 // len(mine)
            for n, out in enumerate(mine):
                out[...] = part[size * n : size * (n + 1)]


def columns_call(pos, ds, queries, groups):
    def column(i, pos_ref):
        d = functools.reduce(lambda v, n: jnp.where(i == n, groups[n], v), range(len(groups)), 0)
        return 0, (pos_ref[0] + d) % 4

    sizes = sum(([D // 4] if d == 0 else [D // 8] * 2 for d in groups), [])
    outs = pl.pallas_call(
        functools.partial(columns_kernel, groups),
        out_shape=tuple(jax.ShapeDtypeStruct((n, D), jnp.float32) for n in sizes),
        grid_spec=pltpu.PrefetchScalarGridSpec(
            num_scalar_prefetch=1,
            grid=(len(groups),),
            in_specs=[pl.BlockSpec((ROWS, D // 4), column), full_spec(ROWS, D)],
            out_specs=tuple(full_spec(n, D) for n in sizes),
        ),
        compiler_params=pltpu.CompilerParams(vmem_limit_bytes=30 << 20),
        name="columns",
    )(pos, ds, queries)
    outs = list(outs)
    return {d: [outs.pop(0) for _ in range(1 if d == 0 else 2)] for d in groups}


def total_kernel(me_ref, got_ref, lines_ref, lse_ref, grad_ref, loss_ref, sum_ref):
    chips = SHARDS // 2
    for core in range(2):
        for j in range(got_ref.shape[1] // QUARTER):
            rows = slice(j * QUARTER, (j + 1) * QUARTER)
            part = got_ref[core, rows, :]
            for chip in range(1, chips):
                part = part + got_ref[2 * chip + core, rows, :]
            to = slice(core * QUARTER, (core + 1) * QUARTER)
            grad_ref[to, j * BLOCK : (j + 1) * BLOCK] = part

    @pl.when(pl.program_id(0) == 0)
    def _():
        sum_ref[...] = jnp.sum(lines_ref[...], axis=0)
        mine = me_ref[0] % 4
        line = jnp.broadcast_to(sum_ref[pl.ds(mine // 2, 1), :], (8, BLOCK))
        line = pltpu.roll(line, (mine % 2) * (BLOCK // 2), 1) + lse_ref[...]
        loss_ref[...] = line[0:1, : 2 * QUARTER]


def total(me, got, lse_rows):
    step = 4 * QUARTER
    return pl.pallas_call(
        total_kernel,
        out_shape=(
            jax.ShapeDtypeStruct((2 * QUARTER, D), jnp.float32),
            jax.ShapeDtypeStruct((1, 2 * QUARTER), jnp.float32),
        ),
        grid_spec=pltpu.PrefetchScalarGridSpec(
            num_scalar_prefetch=1,
            grid=(SUM_ROWS // step,),
            in_specs=[
                pl.BlockSpec((SHARDS, step, BLOCK), lambda i, *_: (0, i, 0)),
                pl.BlockSpec((SHARDS, 8, BLOCK), lambda i, *_: (0, SUM_ROWS // 8, 0)),
                full_spec(8, BLOCK),
            ],
            out_specs=(
                pl.BlockSpec((2 * QUARTER, step // QUARTER * BLOCK), lambda i, *_: (0, i)),
                full_spec(1, 2 * QUARTER),
            ),
            scratch_shapes=[pltpu.VMEM((8, BLOCK), jnp.float32)],
        ),
        compiler_params=pltpu.CompilerParams(vmem_limit_bytes=16 << 20),
        name="total",
    )(me, got, got, lse_rows)


def ring(d, n=4):
    return [(i, (i + d) % n) for i in range(n)]


def send(value, axis, d, n=4):
    return lax.ppermute(value, axis, ring(d, n))


def together(*values):
    return lax.optimization_barrier(values)


def per_device(queries, passages, teacher, block_ids):
    mz, my, mx, mc = (lax.axis_index(a) for a in ("pb", "y", "x", "c"))
    me = my * 8 + mx * 2 + mc
    pos = jnp.stack([mz, my, mx, mc]).astype(jnp.int32)
    flat_ids = block_ids.reshape(-1)

    def exchange(value):
        return lax.all_to_all(value, PLANE, split_axis=0, concat_axis=0, tiled=True)

    sent0 = pack(0, flat_ids, teacher)
    recv0 = exchange(sent0)
    ids1, _ = together(flat_ids, sent0)
    sent1 = pack(1, ids1, teacher)
    s0, s1, lse, p0, p1 = score(queries, passages, teacher)
    sent1 = fill_lse(sent1, lse.reshape(LSE_ROWS, BLOCK))
    recv1 = exchange(sent1)
    ids2, _ = together(flat_ids, lse)
    sent2 = pack(2, ids2, teacher)
    sent2, _ = together(sent2, recv1[0, 0, 0])
    recv2 = exchange(sent2)
    meta = recv0[:, BLOCK, : 2 * CAP].astype(jnp.int32).reshape(-1)
    lists = tuple(make_lists(meta))
    every = recv1[:, BLOCK:, :]
    top = jnp.max(every, axis=0)
    lse = (top + jnp.log(jnp.sum(jnp.exp(every - top[None]), axis=0))).reshape(8, 2, 256)
    ds0, loss0 = rows0_call(lists, s0, lse, [recv0, recv1])
    z0 = columns_call(pos, ds0, queries, (2, 1, 3, 0))
    np0, nm0 = send(z0[2][0], "pb", 1), send(z0[2][1], "pb", -1)
    fp0, fm0 = send(z0[1][1], "pb", 1), send(z0[3][0], "pb", -1)
    q0 = query_call(ds0, p0)
    sp0 = send(z0[1][0] + np0, "pb", 1)
    sm0 = send(z0[3][1] + nm0, "pb", -1)

    ds1, own, other = rows1_call((pos,) + lists, s1, lse, recv2, q0, p1, loss0)
    swapped = send(other, "c", 1, 2)
    z1 = columns_call(pos, ds1, queries, (2, 1))
    both = own + swapped
    got = exchange(both)
    z1.update(columns_call(pos, ds1, queries, (3, 0)))
    np1, nm1 = send(z1[2][0], "pb", 1), send(z1[2][1], "pb", -1)
    fp1, fm1 = send(z1[1][1], "pb", 1), send(z1[3][0], "pb", -1)
    sp1 = send(z1[1][0] + np1, "pb", 1)
    sm1 = send(z1[3][1] + nm1, "pb", -1)

    h = D // 8
    parts = [
        z0[0][0][:h] + sp0 + fm0,
        z0[0][0][h:] + fp0 + sm0,
        z1[0][0][:h] + sp1 + fm1,
        z1[0][0][h:] + fp1 + sm1,
    ]
    gp0, gp1 = jnp.concatenate(parts[:2]), jnp.concatenate(parts[2:])
    grad_passages = jnp.stack(
        [gp0.reshape(4, BLOCK // 2, D), gp1.reshape(4, BLOCK // 2, D)], axis=1
    ).reshape(4 * BLOCK, D)
    lse_rows = lax.dynamic_slice_in_dim(
        lse[:, 0, :].reshape(ROWS), me * (ROWS // SHARDS), ROWS // SHARDS
    )
    lse_rows = jnp.broadcast_to(jnp.pad(lse_rows, (0, BLOCK - 2 * QUARTER)), (8, BLOCK))
    grad_queries, loss = total(me.astype(jnp.int32).reshape(1), got, lse_rows)
    return loss.reshape(2 * QUARTER), grad_queries, grad_passages


def solution(mesh):
    fine = Mesh(mesh.devices.reshape(4, 4, 4, 2), ("pb",) + PLANE)
    in_specs = (P("pb", None), P(PLANE, None), P("pb", PLANE), P("pb", PLANE))
    out_specs = (P(("pb",) + PLANE), P(("pb",) + PLANE, None), P(PLANE + ("pb",), None))
    return jax.shard_map(
        per_device, mesh=fine, in_specs=in_specs, out_specs=out_specs, check_vma=False
    )
```

```python
import functools

import jax
import jax.numpy as jnp
from jax import lax
from jax.experimental import pallas as pl
from jax.experimental.pallas import tpu as pltpu
from jax.sharding import Mesh
from jax.sharding import PartitionSpec as P


BLOCK = 128
D = 1024
ROWS = 2048
PBLOCKS_DEV = 16
SLOTS_DEV = 4
CAP = 4
SHARDS = 32
ENTRIES = 64
PACK_STEP = 8
QUARTER = 32
LSE_ROWS = 16
SUM_ROWS = 256
PLANE = ("y", "x", "c")
SCORE_SCALE = 0.0625
GRAD_SCALE = 64.0


def as_row(column):
    n = column.shape[0]
    return jnp.broadcast_to(column, (n, BLOCK)).T[0:1, :]


def as_lanes(row):
    n = row.shape[1]
    return jnp.broadcast_to(row, (BLOCK, n)).T


def pack_kernel(piece, ids_ref, whole_ref, out_ref, slot_ref, count_ref, teacher_ref, sem):
    step = pl.program_id(0)

    @pl.when(step == 0)
    def _():
        copy = pltpu.make_async_copy(whole_ref, teacher_ref, sem)
        copy.start()
        for i in range(SHARDS):
            count_ref[i] = 0
        for i in range(SHARDS * CAP):
            slot_ref[i] = -1

        def place(i, carry):
            owner = ids_ref[i] // PBLOCKS_DEV
            rank = count_ref[owner]
            count_ref[owner] = rank + 1
            slot_ref[owner * CAP + jnp.minimum(rank, CAP - 1)] = i
            return carry

        lax.fori_loop(0, ENTRIES, place, 0, unroll=8)
        copy.wait()

    quarter = lax.broadcasted_iota(jnp.int32, (BLOCK, BLOCK), 1) // QUARTER
    lane = lax.broadcasted_iota(jnp.int32, (8, BLOCK), 1)
    move = lambda t, lanes: t if lanes % BLOCK == 0 else pltpu.roll(t, lanes % BLOCK, 1)
    for j in range(PACK_STEP):
        meta = jnp.zeros((8, BLOCK), jnp.float32)
        tiles = []
        for k in range(CAP):
            slot = slot_ref[(step * PACK_STEP + j) * CAP + k]
            entry = jnp.maximum(slot, 0)
            row = pl.multiple_of((entry // SLOTS_DEV) * BLOCK, BLOCK)
            col = pl.multiple_of((entry % SLOTS_DEV) * BLOCK, BLOCK)
            tiles.append(teacher_ref[pl.ds(row, BLOCK), pl.ds(col, BLOCK)])
            if piece == 0:
                where = jnp.where(slot < 0, -1, entry // SLOTS_DEV).astype(jnp.float32)
                block = (ids_ref[entry] % PBLOCKS_DEV).astype(jnp.float32)
                meta = jnp.where(lane == k, where, meta)
                meta = jnp.where(lane == CAP + k, block, meta)
        if piece < 2:
            moved = [move(t, QUARTER * (k - piece)) for k, t in enumerate(tiles)]
            low = jnp.where(quarter == 0, moved[0], moved[1])
            high = jnp.where(quarter == 2, moved[2], moved[3])
            out_ref[j, :BLOCK, :] = jnp.where(quarter < 2, low, high)
        else:
            for pair in range(CAP // 2):
                first = pltpu.roll(tiles[2 * pair], BLOCK // 2, 1)
                rows = slice(pair * BLOCK, (pair + 1) * BLOCK)
                out_ref[j, rows, :] = jnp.where(quarter < 2, first, tiles[2 * pair + 1])
        if piece == 0:
            out_ref[j, BLOCK:, :] = meta


def pack(piece, ids, teacher):
    rows = (BLOCK + 8, BLOCK, 2 * BLOCK)[piece]
    total = rows + (LSE_ROWS if piece == 1 else 0)
    return pl.pallas_call(
        functools.partial(pack_kernel, piece),
        out_shape=jax.ShapeDtypeStruct((SHARDS, total, BLOCK), jnp.float32),
        grid_spec=pltpu.PrefetchScalarGridSpec(
            num_scalar_prefetch=1,
            grid=(SHARDS // PACK_STEP,),
            in_specs=[pl.BlockSpec(memory_space=pl.ANY)],
            out_specs=pl.BlockSpec((PACK_STEP, rows, BLOCK), lambda s, ids: (s, 0, 0)),
            scratch_shapes=[
                pltpu.SMEM((SHARDS * CAP,), jnp.int32),
                pltpu.SMEM((SHARDS,), jnp.int32),
                pltpu.VMEM((ROWS, SLOTS_DEV * BLOCK), jnp.float32),
                pltpu.SemaphoreType.DMA,
            ],
        ),
        name="pack",
    )(ids, teacher)


def fill_kernel(lse_ref, sent_ref, out_ref):
    halves = lse_ref[...].reshape(1, 2, LSE_ROWS, BLOCK)
    pairs = jnp.broadcast_to(halves, (SHARDS // 2, 2, LSE_ROWS, BLOCK))
    out_ref[...] = pairs.reshape(out_ref.shape)


def fill_lse(sent, lse):
    return pl.pallas_call(
        fill_kernel,
        out_shape=jax.ShapeDtypeStruct(sent.shape, sent.dtype),
        grid=(1,),
        in_specs=[
            pl.BlockSpec((2 * LSE_ROWS, BLOCK), lambda i: (0, 0)),
            pl.BlockSpec(memory_space=pl.ANY),
        ],
        out_specs=pl.BlockSpec((SHARDS, LSE_ROWS, BLOCK), lambda i: (0, BLOCK // LSE_ROWS, 0)),
        input_output_aliases={1: 0},
        name="fill_lse",
    )(lse, sent)


def list_kernel(meta_ref, start_ref, row_ref, block_ref, next_ref):
    blocks = ROWS // BLOCK
    for r in range(blocks):
        next_ref[r] = 0

    def count(n, carry):
        r = meta_ref[(n // CAP) * (2 * CAP) + n % CAP]

        @pl.when(r >= 0)
        def _():
            next_ref[r] = next_ref[r] + 1

        row_ref[n] = 0
        block_ref[n] = 0
        return carry

    lax.fori_loop(0, SHARDS * CAP, count, 0, unroll=4)
    total = 0
    for r in range(blocks):
        start_ref[r] = total
        size = next_ref[r]
        next_ref[r] = total
        total = total + size
    start_ref[blocks] = total

    def place(n, carry):
        src, k = n // CAP, n % CAP
        r = meta_ref[src * (2 * CAP) + k]

        @pl.when(r >= 0)
        def _():
            at = next_ref[r]
            next_ref[r] = at + 1
            row_ref[at] = n
            block_ref[at] = meta_ref[src * (2 * CAP) + CAP + k]

        return carry

    lax.fori_loop(0, SHARDS * CAP, place, 0, unroll=4)


def make_lists(meta):
    smem = pl.BlockSpec(memory_space=pltpu.SMEM)
    ints = lambda n: jax.ShapeDtypeStruct((n,), jnp.int32)
    return pl.pallas_call(
        list_kernel,
        out_shape=(ints(ROWS // BLOCK + 1), ints(SHARDS * CAP), ints(SHARDS * CAP)),
        in_specs=[smem],
        out_specs=(smem, smem, smem),
        scratch_shapes=[pltpu.SMEM((ROWS // BLOCK,), jnp.int32)],
        name="make_lists",
    )(meta)


def score_kernel(q_ref, p_ref, t_ref, s0_ref, s1_ref, lse_ref, p0_ref, p1_ref):
    half = BLOCK // 2

    @pl.when(pl.program_id(0) == 0)
    def _():
        for block in range(PBLOCKS_DEV):
            here = slice(block * half, (block + 1) * half)
            p0_ref[here, :] = p_ref[block * BLOCK : block * BLOCK + half, :]
            p1_ref[here, :] = p_ref[block * BLOCK + half : (block + 1) * BLOCK, :]

    q = q_ref[...]
    nt = (((1,), (1,)), ((), ()))
    s0 = lax.dot_general(q, p0_ref[...], nt, preferred_element_type=jnp.float32) * SCORE_SCALE
    s1 = lax.dot_general(q, p1_ref[...], nt, preferred_element_type=jnp.float32) * SCORE_SCALE
    s0_ref[...] = s0
    s1_ref[...] = s1
    top = jnp.maximum(jnp.max(s0, axis=1, keepdims=True), jnp.max(s1, axis=1, keepdims=True))
    total = jnp.sum(jnp.exp(s0 - top), axis=1, keepdims=True) + jnp.sum(
        jnp.exp(s1 - top), axis=1, keepdims=True
    )
    lse_ref[0, 0:1, :] = as_row(top + jnp.log(total))
    t = t_ref[...]
    ttop = jnp.max(t, axis=1, keepdims=True)
    ttotal = jnp.sum(jnp.exp(t - ttop), axis=1, keepdims=True)
    lse_ref[0, 1:2, :] = as_row(ttop + jnp.log(ttotal))


def score(queries, passages, teacher):
    rb = 256
    block = pl.BlockSpec((rb, D), lambda i: (i, 0))
    whole = pl.BlockSpec((D, D), lambda i: (0, 0))
    scores = jax.ShapeDtypeStruct((ROWS, D), jnp.float32)
    part = jax.ShapeDtypeStruct((D, D), jnp.bfloat16)
    return pl.pallas_call(
        score_kernel,
        out_shape=(
            scores,
            scores,
            jax.ShapeDtypeStruct((ROWS // rb, 2, rb), jnp.float32),
            part,
            part,
        ),
        grid=(ROWS // rb,),
        in_specs=[
            block,
            pl.BlockSpec((ROWS, D), lambda i: (0, 0)),
            pl.BlockSpec((rb, SLOTS_DEV * BLOCK), lambda i: (i, 0)),
        ],
        out_specs=(block, block, pl.BlockSpec((1, 2, rb), lambda i: (i, 0, 0)), whole, whole),
        name="score",
    )(queries, passages, teacher)


def subtract_tiles(
    fetch, sub_rows, first, end, block_ref, s_cols, lt_ref, rows, w_ref, acc_ref
):
    lane = lax.broadcasted_iota(jnp.int32, (sub_rows, BLOCK), 1)
    side = lane // (BLOCK // 2)

    def body(n, carry):
        parts = []
        for at in (first + 2 * n, first + 2 * n + 1):
            here = jnp.minimum(at, end - 1)
            block = block_ref[here]
            x = fetch(here, block)
            keep = (side == block % 2) & (at < end)
            centred = x - lt_ref[rows, :]
            prob = jnp.where(keep, jnp.exp(centred), 0.0)
            cols = pl.ds(pl.multiple_of((block // 2) * BLOCK, BLOCK), BLOCK)
            term = jnp.where(keep, prob * (centred - s_cols(cols)), 0.0)
            parts.append((prob, cols, term))
        acc_ref[rows, :] = acc_ref[rows, :] + (parts[0][2] + parts[1][2])
        for prob, cols, _ in parts:
            w_ref[rows, cols] = w_ref[rows, cols] - prob
        return carry

    lax.fori_loop(0, (end - first + 1) // 2, body, 0)


def rows0_kernel(
    start_ref, row_ref, block_ref, s_ref, lse_ref, recv0_ref, recv1_ref,
    ds_ref, loss_ref, w_ref, lt_ref, acc_ref,
):
    step = pl.program_id(0)
    rb = 256
    half = BLOCK // 2
    ls = as_lanes(lse_ref[0, 0:1, :])
    lt_ref[...] = as_lanes(lse_ref[0, 1:2, :])
    for j in range(D // BLOCK):
        cols = slice(j * BLOCK, (j + 1) * BLOCK)
        w_ref[:, cols] = jnp.exp(s_ref[:, cols] - ls)
    acc_ref[...] = jnp.zeros_like(acc_ref)
    early = lax.broadcasted_iota(jnp.int32, (BLOCK, BLOCK), 1) % half < QUARTER

    def fetch(n, block):
        slot = row_ref[n]
        src, k = slot // CAP, slot % CAP
        shift = (block % 2) * half
        at = pl.multiple_of(src * (BLOCK + 8), 8)
        x = recv0_ref[pl.ds(at, BLOCK), :]
        x = pltpu.roll(x, (shift - k * QUARTER + BLOCK) % BLOCK, 1)
        at = pl.multiple_of(src * (BLOCK + LSE_ROWS), 8)
        y = recv1_ref[pl.ds(at, BLOCK), :]
        y = pltpu.roll(y, (shift + QUARTER - k * QUARTER + BLOCK) % BLOCK, 1)
        return jnp.where(early, x, y)

    for sub in range(rb // BLOCK):
        rows = slice(sub * BLOCK, (sub + 1) * BLOCK)
        r = step * (rb // BLOCK) + sub
        subtract_tiles(
            fetch, BLOCK, start_ref[r], start_ref[r + 1], block_ref,
            lambda cols: s_ref[rows, cols], lt_ref, rows, w_ref, acc_ref,
        )
    ds_ref[...] = (w_ref[...] * GRAD_SCALE).astype(jnp.bfloat16)
    loss_ref[0] = as_row(jnp.sum(acc_ref[...], axis=1, keepdims=True))


ROW_SCRATCH = [
    pltpu.VMEM((256, D), jnp.float32),
    pltpu.VMEM((256, BLOCK), jnp.float32),
    pltpu.VMEM((256, BLOCK), jnp.float32),
]


def full_spec(*shape):
    return pl.BlockSpec(shape, lambda i, *_: (0,) * len(shape))


def rows0_call(lists, scores, lse, recvs):
    rb = 256
    recvs = [r.reshape(-1, BLOCK) for r in recvs]
    block = pl.BlockSpec((rb, D), lambda i, *_: (i, 0))
    return pl.pallas_call(
        rows0_kernel,
        out_shape=(
            jax.ShapeDtypeStruct((ROWS, D), jnp.bfloat16),
            jax.ShapeDtypeStruct((ROWS // rb, 1, rb), jnp.float32),
        ),
        grid_spec=pltpu.PrefetchScalarGridSpec(
            num_scalar_prefetch=len(lists),
            grid=(ROWS // rb,),
            in_specs=[block, pl.BlockSpec((1, 2, rb), lambda i, *_: (i, 0, 0))]
            + [full_spec(*r.shape) for r in recvs],
            out_specs=(block, pl.BlockSpec((1, 1, rb), lambda i, *_: (i, 0, 0))),
            scratch_shapes=ROW_SCRATCH,
        ),
        compiler_params=pltpu.CompilerParams(vmem_limit_bytes=30 << 20),
        name="rows0",
    )(*lists, scores, lse, *recvs)


def rows1_kernel(
    pos_ref, start_ref, row_ref, block_ref, s_ref, lse_ref, recv_ref, add_ref, p_ref, loss0_ref,
    ds_ref, own_ref, other_ref, w_ref, lt_ref, acc_ref, past_ref, line_ref,
):
    step = pl.program_id(0)
    steps = pl.num_programs(0) - 1
    rb = 256
    half = BLOCK // 2
    part = add_ref[...] + jnp.dot(past_ref[...], p_ref[...], preferred_element_type=jnp.float32)
    ls = as_lanes(lse_ref[0, 0:1, :])
    lt_ref[...] = as_lanes(lse_ref[0, 1:2, :])
    for j in range(D // BLOCK):
        cols = slice(j * BLOCK, (j + 1) * BLOCK)
        w_ref[:, cols] = jnp.exp(s_ref[:, cols] - ls)
    acc_ref[...] = jnp.zeros_like(acc_ref)
    part = part.reshape(rb // (2 * QUARTER), 2, QUARTER, D)
    first = pos_ref[3] == 0
    for j in range(D // BLOCK):
        cols = slice(j * BLOCK, (j + 1) * BLOCK)
        rows = slice(j * QUARTER, (j + 1) * QUARTER)
        even, odd = part[:, 0, :, cols], part[:, 1, :, cols]
        own_ref[:, rows, :] = jnp.where(first, even, odd)
        other_ref[:, rows, :] = jnp.where(first, odd, even)
    lines = (own_ref.shape[0], 8, BLOCK)
    own_ref[:, SUM_ROWS:, :] = jnp.broadcast_to(line_ref[...][None], lines)
    other_ref[:, SUM_ROWS:, :] = jnp.zeros(lines, jnp.float32)

    def fetch(n, block):
        slot = row_ref[n]
        at = pl.multiple_of((slot // 2) * BLOCK, BLOCK)
        return pltpu.roll(recv_ref[pl.ds(at, BLOCK), :], ((block + slot) % 2) * half, 1)

    @pl.when(step < steps)
    def _():
        for sub in range(rb // BLOCK):
            rows = slice(sub * BLOCK, (sub + 1) * BLOCK)
            r = step * (rb // BLOCK) + sub
            subtract_tiles(
                fetch, BLOCK, start_ref[r], start_ref[r + 1], block_ref,
                lambda cols: s_ref[rows, cols], lt_ref, rows, w_ref, acc_ref,
            )
        ds = (w_ref[...] * GRAD_SCALE).astype(jnp.bfloat16)
        ds_ref[...] = ds
        past_ref[...] = ds
        loss = as_row(jnp.sum(acc_ref[...], axis=1, keepdims=True)) + loss0_ref[0]
        low = jnp.broadcast_to(loss[:, :BLOCK], (8, BLOCK))
        high = jnp.broadcast_to(loss[:, BLOCK:], (8, BLOCK))
        line_ref[...] = jnp.where(lax.broadcasted_iota(jnp.int32, (8, BLOCK), 0) == 0, low, high)


def rows1_call(scalars, scores, lse, recv, add, passages, loss0):
    rb = 256
    steps = ROWS // rb
    recv = recv.reshape(-1, BLOCK)
    now = lambda i, *_: (jnp.minimum(i, steps - 1), 0)
    now3 = lambda i, *_: (jnp.minimum(i, steps - 1), 0, 0)
    past = lambda i, *_: (jnp.maximum(i - 1, 0), 0)
    past3 = lambda i, *_: (jnp.maximum(i - 1, 0), 0, 0)
    out = pl.BlockSpec((rb // (2 * QUARTER), SUM_ROWS + 8, BLOCK), past3)
    out_type = jax.ShapeDtypeStruct((SHARDS, SUM_ROWS + 8, BLOCK), jnp.float32)
    return pl.pallas_call(
        rows1_kernel,
        out_shape=(
            jax.ShapeDtypeStruct((ROWS, D), jnp.bfloat16),
            out_type,
            out_type,
        ),
        grid_spec=pltpu.PrefetchScalarGridSpec(
            num_scalar_prefetch=len(scalars),
            grid=(steps + 1,),
            in_specs=[
                pl.BlockSpec((rb, D), now),
                pl.BlockSpec((1, 2, rb), now3),
                full_spec(*recv.shape),
                pl.BlockSpec((rb, D), past),
                full_spec(D, D),
                pl.BlockSpec((1, 1, rb), now3),
            ],
            out_specs=(pl.BlockSpec((rb, D), now), out, out),
            scratch_shapes=ROW_SCRATCH
            + [pltpu.VMEM((rb, D), jnp.bfloat16), pltpu.VMEM((8, BLOCK), jnp.float32)],
        ),
        compiler_params=pltpu.CompilerParams(vmem_limit_bytes=32 << 20),
        name="rows1",
    )(*scalars, scores, lse, recv, add, passages, loss0)


def query_kernel(ds_ref, p_ref, out_ref):
    out_ref[...] = jnp.dot(ds_ref[...], p_ref[...], preferred_element_type=jnp.float32)


def query_call(ds, passages):
    rb = 512
    return pl.pallas_call(
        query_kernel,
        out_shape=jax.ShapeDtypeStruct((ROWS, D), jnp.float32),
        grid=(ROWS // rb,),
        in_specs=[pl.BlockSpec((rb, D), lambda i: (i, 0)), full_spec(D, D)],
        out_specs=pl.BlockSpec((rb, D), lambda i: (i, 0)),
        compiler_params=pltpu.CompilerParams(vmem_limit_bytes=30 << 20),
        name="query",
    )(ds, passages)


def columns_kernel(groups, pos_ref, ds_ref, q_ref, *outs):
    step = pl.program_id(0)
    part = lax.dot_general(
        ds_ref[...], q_ref[...], (((0,), (0,)), ((), ())), preferred_element_type=jnp.float32
    )
    at = 0
    for i, d in enumerate(groups):
        count = 1 if d == 0 else 2
        mine = outs[at : at + count]
        at += count

        @pl.when(step == i)
        def _(mine=mine):
            size = D // 4 // len(mine)
            for n, out in enumerate(mine):
                out[...] = part[size * n : size * (n + 1)]


def columns_call(pos, ds, queries, groups):
    def column(i, pos_ref):
        d = functools.reduce(lambda v, n: jnp.where(i == n, groups[n], v), range(len(groups)), 0)
        return 0, (pos_ref[0] + d) % 4

    sizes = sum(([D // 4] if d == 0 else [D // 8] * 2 for d in groups), [])
    outs = pl.pallas_call(
        functools.partial(columns_kernel, groups),
        out_shape=tuple(jax.ShapeDtypeStruct((n, D), jnp.float32) for n in sizes),
        grid_spec=pltpu.PrefetchScalarGridSpec(
            num_scalar_prefetch=1,
            grid=(len(groups),),
            in_specs=[pl.BlockSpec((ROWS, D // 4), column), full_spec(ROWS, D)],
            out_specs=tuple(full_spec(n, D) for n in sizes),
        ),
        compiler_params=pltpu.CompilerParams(vmem_limit_bytes=30 << 20),
        name="columns",
    )(pos, ds, queries)
    outs = list(outs)
    return {d: [outs.pop(0) for _ in range(1 if d == 0 else 2)] for d in groups}


def total_kernel(me_ref, got_ref, lines_ref, lse_ref, grad_ref, loss_ref, sum_ref):
    chips = SHARDS // 2
    for core in range(2):
        for j in range(got_ref.shape[1] // QUARTER):
            rows = slice(j * QUARTER, (j + 1) * QUARTER)
            part = got_ref[core, rows, :]
            for chip in range(1, chips):
                part = part + got_ref[2 * chip + core, rows, :]
            to = slice(core * QUARTER, (core + 1) * QUARTER)
            grad_ref[to, j * BLOCK : (j + 1) * BLOCK] = part

    @pl.when(pl.program_id(0) == 0)
    def _():
        sum_ref[...] = jnp.sum(lines_ref[...], axis=0)
        mine = me_ref[0] % 4
        line = jnp.broadcast_to(sum_ref[pl.ds(mine // 2, 1), :], (8, BLOCK))
        line = pltpu.roll(line, (mine % 2) * (BLOCK // 2), 1) + lse_ref[...]
        loss_ref[...] = line[0:1, : 2 * QUARTER]


def total(me, got, lse_rows):
    step = 4 * QUARTER
    return pl.pallas_call(
        total_kernel,
        out_shape=(
            jax.ShapeDtypeStruct((2 * QUARTER, D), jnp.float32),
            jax.ShapeDtypeStruct((1, 2 * QUARTER), jnp.float32),
        ),
        grid_spec=pltpu.PrefetchScalarGridSpec(
            num_scalar_prefetch=1,
            grid=(SUM_ROWS // step,),
            in_specs=[
                pl.BlockSpec((SHARDS, step, BLOCK), lambda i, *_: (0, i, 0)),
                pl.BlockSpec((SHARDS, 8, BLOCK), lambda i, *_: (0, SUM_ROWS // 8, 0)),
                full_spec(8, BLOCK),
            ],
            out_specs=(
                pl.BlockSpec((2 * QUARTER, step // QUARTER * BLOCK), lambda i, *_: (0, i)),
                full_spec(1, 2 * QUARTER),
            ),
            scratch_shapes=[pltpu.VMEM((8, BLOCK), jnp.float32)],
        ),
        compiler_params=pltpu.CompilerParams(vmem_limit_bytes=16 << 20),
        name="total",
    )(me, got, got, lse_rows)


def ring(d, n=4):
    return [(i, (i + d) % n) for i in range(n)]


def send(value, axis, d, n=4):
    return lax.ppermute(value, axis, ring(d, n))


def together(*values):
    return lax.optimization_barrier(values)


def per_device(queries, passages, teacher, block_ids):
    mz, my, mx, mc = (lax.axis_index(a) for a in ("pb", "y", "x", "c"))
    me = my * 8 + mx * 2 + mc
    pos = jnp.stack([mz, my, mx, mc]).astype(jnp.int32)
    flat_ids = block_ids.reshape(-1)

    def exchange(value):
        return lax.all_to_all(value, PLANE, split_axis=0, concat_axis=0, tiled=True)

    sent0 = pack(0, flat_ids, teacher)
    recv0 = exchange(sent0)
    ids1, _ = together(flat_ids, sent0)
    sent1 = pack(1, ids1, teacher)
    s0, s1, lse, p0, p1 = score(queries, passages, teacher)
    sent1 = fill_lse(sent1, lse.reshape(2 * LSE_ROWS, BLOCK))
    recv1 = exchange(sent1)
    ids2, _ = together(flat_ids, lse)
    sent2 = pack(2, ids2, teacher)
    sent2, _ = together(sent2, recv1[0, 0, 0])
    recv2 = exchange(sent2)
    meta = recv0[:, BLOCK, : 2 * CAP].astype(jnp.int32).reshape(-1)
    lists = tuple(make_lists(meta))
    every = recv1[:, BLOCK:, :]
    top = jnp.max(every, axis=0)
    mine = top + jnp.log(jnp.sum(jnp.exp(every - top[None]), axis=0))
    theirs = send(mine, "c", 1, 2)
    even, odd = jnp.where(mc == 0, mine, theirs), jnp.where(mc == 0, theirs, mine)
    lse = jnp.concatenate([even, odd], axis=0).reshape(8, 2, 256)
    ds0, loss0 = rows0_call(lists, s0, lse, [recv0, recv1])
    z0 = columns_call(pos, ds0, queries, (2, 1, 3, 0))
    np0, nm0 = send(z0[2][0], "pb", 1), send(z0[2][1], "pb", -1)
    fp0, fm0 = send(z0[1][1], "pb", 1), send(z0[3][0], "pb", -1)
    q0 = query_call(ds0, p0)
    sp0 = send(z0[1][0] + np0, "pb", 1)
    sm0 = send(z0[3][1] + nm0, "pb", -1)

    ds1, own, other = rows1_call((pos,) + lists, s1, lse, recv2, q0, p1, loss0)
    swapped = send(other, "c", 1, 2)
    z1 = columns_call(pos, ds1, queries, (2, 1))
    both = own + swapped
    got = exchange(both)
    z1.update(columns_call(pos, ds1, queries, (3, 0)))
    np1, nm1 = send(z1[2][0], "pb", 1), send(z1[2][1], "pb", -1)
    fp1, fm1 = send(z1[1][1], "pb", 1), send(z1[3][0], "pb", -1)
    sp1 = send(z1[1][0] + np1, "pb", 1)
    sm1 = send(z1[3][1] + nm1, "pb", -1)

    h = D // 8
    parts = [
        z0[0][0][:h] + sp0 + fm0,
        z0[0][0][h:] + fp0 + sm0,
        z1[0][0][:h] + sp1 + fm1,
        z1[0][0][h:] + fp1 + sm1,
    ]
    gp0, gp1 = jnp.concatenate(parts[:2]), jnp.concatenate(parts[2:])
    grad_passages = jnp.stack(
        [gp0.reshape(4, BLOCK // 2, D), gp1.reshape(4, BLOCK // 2, D)], axis=1
    ).reshape(4 * BLOCK, D)
    lse_rows = lax.dynamic_slice_in_dim(
        lse[:, 0, :].reshape(ROWS), me * (ROWS // SHARDS), ROWS // SHARDS
    )
    lse_rows = jnp.broadcast_to(jnp.pad(lse_rows, (0, BLOCK - 2 * QUARTER)), (8, BLOCK))
    grad_queries, loss = total(me.astype(jnp.int32).reshape(1), got, lse_rows)
    return loss.reshape(2 * QUARTER), grad_queries, grad_passages


def solution(mesh):
    fine = Mesh(mesh.devices.reshape(4, 4, 4, 2), ("pb",) + PLANE)
    in_specs = (P("pb", None), P(PLANE, None), P("pb", PLANE), P("pb", PLANE))
    out_specs = (P(("pb",) + PLANE), P(("pb",) + PLANE, None), P(PLANE + ("pb",), None))
    return jax.shard_map(
        per_device, mesh=fine, in_specs=in_specs, out_specs=out_specs, check_vma=False
    )
```
